512 devices in a mesh: rep: 4 (over y_hi, core), sp: 128 (over y_lo, z, x).
Axes of the slice: x: 4, y: 8 (y_hi: 2, y_lo: 4; y = y_hi * 4 + y_lo), z: 8, core: 2. Of those that a mesh axis runs over, the one named last changes fastest.
Arguments:
- film_start: float32 [4, 2048, 2048], P('rep', 'sp'), may hold values from 0.2 to 2
- evaporation: float32 [4, 2048, 2048], P('rep', 'sp'), may hold values from 0.05 to 0.5
- contact_mask: int32 [4, 2048, 2048], P('rep', 'sp'), may hold values 0 or 1
- first_classes: int32 [4, 2048, 16], P('rep'), may hold values from 0 to 3
- second_classes: int32 [4, 2048, 16], P('rep', 'sp'), may hold values from 0 to 3
- span_inverses: float32 [4, 128, 128], replicated, may hold values from -0.4 to 1
- conv_weight: bfloat16 [3, 3, 4, 64], replicated, may hold values from -0.5 to 0.5
- mixing_weight: bfloat16 [64, 64], replicated, may hold values from -0.75 to 0.75
- flux_weight: bfloat16 [64], replicated, may hold values from -0.75 to 0.75
- film_cotangent: float32 [4, 2048, 2048], P('rep', 'sp'), may hold values from -6 to 6
Outputs:
- final_film: float32 [4, 2048, 2048], P('rep', 'sp')
- film_grad: float32 [4, 2048, 2048], P('rep', 'sp')
- conv_grad: float32 [3, 3, 4, 64], replicated
- mixing_grad: float32 [64, 64], replicated
- flux_grad: float32 [64], replicated
The draws below stay inside these ranges and needn't reach their ends.
All inputs are finite; a program needn't handle non-finite values. No bound on the sum of `contact_mask` on one device may be relied on, other than what follows from the above.
Results may differ from the reference program's by a relative error of at most 0.019.
Values may be sent and summed in bfloat16 or wider, within the bound.
A program may use at most 128 MiB of HBM per device.

```python
import math
import jax
import jax.numpy as jnp
from jax import lax

HID = 64
C_IN = 4
SPAN = 128
NCLS = 4
STEPS = 1
SIDE = 2048
REPS = 4
NSPAN = 16


def draw_span_inverses(key, part):
    shape = (NCLS, SPAN, SPAN)
    noise = jnp.clip(jax.random.normal(key, shape, jnp.float32), -4.0, 4.0)
    return 0.6 * jnp.eye(SPAN, dtype=jnp.float32)[None] + noise * (0.4 / math.sqrt(SPAN))


def plant(values, stream_key, smallest, high):
    index_at = [jax.random.randint(jax.random.fold_in(stream_key, axis), (), 0, length) for axis, length in enumerate(values.shape)]
    widest = values.shape.index(max(values.shape))
    next_to = index_at[:widest] + [(index_at[widest] + 1) % values.shape[widest]] + index_at[widest + 1:]
    return values.at[tuple(index_at)].set(smallest).at[tuple(next_to)].set(high)


def levels(stream_key, shape, cuts, smallest, top_value):
    level, own = 1.0, jax.random.fold_in(stream_key, 6)
    for dim, shards_of in cuts:
        heights = jnp.exp(jax.random.uniform(jax.random.fold_in(own, dim), (shards_of,), jnp.float32, smallest / len(cuts), top_value / len(cuts)))
        level = level * jnp.repeat(heights, shape[dim] // shards_of).reshape([-1 if axis == dim else 1 for axis in range(len(shape))])
    return level


def centred(rng, extent, width, most, cuts=(), kind=jnp.bfloat16):
    gain = levels(rng, extent, cuts, -0.22, 0.18) if cuts else 1.0
    values = jax.random.normal(rng, extent, jnp.float32) * width * gain
    return jnp.minimum(jnp.maximum(values, -most), most).astype(kind)


def setup_inputs(seed: int = 0) -> dict:
    arg_keys = jax.random.split(jax.random.key(seed), 11)
    return {
        "film_start": jnp.clip(0.2 + 1.8 * jax.random.uniform(arg_keys[0], (REPS, SIDE, SIDE), jnp.float32) ** levels(arg_keys[0], (REPS, SIDE, SIDE), ((0, 4), (1, 128)), -0.2, 0.2), 0.2, 2.0),
        "evaporation": jnp.clip(jnp.exp(math.log(0.5) - 2.3025851 * jax.random.uniform(arg_keys[1], (REPS, SIDE, SIDE), jnp.float32) ** levels(arg_keys[1], (REPS, SIDE, SIDE), ((0, 4), (1, 128)), -0.2, 0.2)), 0.05, 0.5),
        "contact_mask": plant((jax.random.randint(arg_keys[2], (REPS, SIDE, SIDE), 0, 4) < 1).astype(jnp.int32), jax.random.fold_in(arg_keys[2], 1), 0, 1),
        "first_classes": plant(jax.random.randint(arg_keys[3], (REPS, SIDE, NSPAN), 0, NCLS), jax.random.fold_in(arg_keys[3], 1), 0, NCLS - 1).astype(jnp.int32),
        "second_classes": plant(jax.random.randint(arg_keys[4], (REPS, SIDE, NSPAN), 0, NCLS), jax.random.fold_in(arg_keys[4], 1), 0, NCLS - 1).astype(jnp.int32),
        "span_inverses": draw_span_inverses(jax.random.fold_in(arg_keys[10], 71), 0),
        "conv_weight": centred(arg_keys[6], (3, 3, C_IN, HID), (36 * C_IN) ** -0.5, 0.5),
        "mixing_weight": centred(arg_keys[7], (HID, HID), HID ** -0.5, 0.75),
        "flux_weight": centred(arg_keys[8], (HID,), HID ** -0.5, 0.75),
        "film_cotangent": centred(arg_keys[9], (REPS, SIDE, SIDE), 1.0, 6.0, ((0, 4), (1, 128)), jnp.float32),
    }


time_step = 0.5

def apply_spans(lines, classes, inverses, transpose):
    shape = lines.shape
    count = classes.shape[-1]
    parts = lines.reshape(shape[:-1] + (count, shape[-1] // count))
    form = 'ji,...kj->...ki' if transpose else 'ij,...kj->...ki'
    result = jnp.zeros_like(parts)
    for group in range(inverses.shape[0]):
        product = jnp.einsum(form, inverses[group], parts, precision=lax.Precision.HIGHEST)
        result = jnp.where((classes == group)[..., None], product, result)
    return result.reshape(shape)

def closure_rows(padded, conv_w, mixing_w, flux_w):
    total = padded.shape[1] - 2
    cols = padded.shape[2] - 2
    rows = min(64, total)

    def row_block(start):
        piece = lax.dynamic_slice_in_dim(padded, start, rows + 2, 1)
        pre_first = None
        for row_tap in range(3):
            for col_tap in range(3):
                term = jnp.einsum('co,cxy->oxy', conv_w[row_tap, col_tap], piece[:, row_tap:row_tap + rows, col_tap:col_tap + cols])
                pre_first = term if pre_first is None else pre_first + term
        first_act = lax.optimization_barrier(jnp.tanh(pre_first).astype(jnp.bfloat16)).astype(jnp.float32)
        pre_second = jnp.einsum('op,oxy->pxy', mixing_w, first_act)
        second_act = lax.optimization_barrier(jnp.tanh(pre_second).astype(jnp.bfloat16)).astype(jnp.float32)
        return jnp.einsum('p,pxy->xy', flux_w, second_act)
    starts = jnp.arange(total // rows, dtype=jnp.int32) * rows
    return lax.map(jax.checkpoint(row_block), starts).reshape(total, cols)

def advance(film, evaporation, maskf, first_cls, second_cls, inverses, conv_w, mixing_w, flux_w):
    height = film
    for step in range(STEPS):
        features = jnp.stack([height, height * height, maskf, evaporation]).astype(jnp.bfloat16)
        padded = jnp.pad(features, ((0, 0), (1, 1), (1, 1))).astype(jnp.float32)
        flux = closure_rows(padded, conv_w, mixing_w, flux_w)
        source_side = height + time_step * (flux - maskf * evaporation)
        across = apply_spans(source_side.T, first_cls, inverses, False).T
        height = apply_spans(across, second_cls, inverses, False)
    return height

def reference(film_start, evaporation, contact_mask, first_classes, second_classes, span_inverses, conv_weight, mixing_weight, flux_weight, film_cotangent):
    conv_w = conv_weight.astype(jnp.float32)
    mixing_w = mixing_weight.astype(jnp.float32)
    flux_w = flux_weight.astype(jnp.float32)

    def one_replica(items):
        film, evap, mask, first_cls, second_cls, cotangent = items
        maskf = mask.astype(jnp.float32)

        def forward(start, conv_v, mixing_v, flux_v):
            return advance(start, evap, maskf, first_cls, second_cls, span_inverses, conv_v, mixing_v, flux_v)
        final, pullback = jax.vjp(forward, film, conv_w, mixing_w, flux_w)
        grads = pullback(cotangent)
        return (final, grads[0], grads[1], grads[2], grads[3])
    final, film_grad, conv_g, mixing_g, flux_g = lax.map(one_replica, (film_start, evaporation, contact_mask, first_classes, second_classes, film_cotangent))
    scale = 1.0 / math.sqrt(REPS * SIDE * SIDE)
    return (final, film_grad, lax.optimization_barrier(jnp.sum(conv_g, axis=0)) * scale, lax.optimization_barrier(jnp.sum(mixing_g, axis=0)) * scale, lax.optimization_barrier(jnp.sum(flux_g, axis=0)) * scale)
```

```python
import math

import jax
import jax.numpy as jnp
from jax import lax
from jax.experimental import pallas as pl
from jax.experimental.pallas import tpu as pltpu
from jax.sharding import PartitionSpec as P

BF = jnp.bfloat16
F32 = jnp.float32
MESH = pl.DeviceIdType.MESH
SPAN = 128
ROWS = 16
HALF = 8
HID = 64
CIN = 4
PIECES = 12
WIDTH = 256
NCLS = 4
GROUP = SPAN // ROWS
DX, DZ, DYLO, DYHI, DCORE = 4, 8, 4, 2, 2
TIME_STEP = 0.5


def nt(a, b):
    return lax.dot_general(a, b, (((1,), (1,)), ((), ())), preferred_element_type=F32)


def nn(a, b):
    return lax.dot_general(a, b, (((1,), (0,)), ((), ())), preferred_element_type=F32)


def split2(v):
    hi = v.astype(BF)
    return hi, (v - hi.astype(F32)).astype(BF)


def split3(v):
    hi = v.astype(BF)
    rest = v - hi.astype(F32)
    mid = rest.astype(BF)
    return hi, mid, (rest - mid.astype(F32)).astype(BF)


def iota(shape, dim):
    return lax.broadcasted_iota(jnp.int32, shape, dim)


def onehot(cond):
    return jnp.where(cond, 1.0, 0.0).astype(BF)


def span_select(products, cls_ref, store):
    for k in range(products.shape[0] // ROWS):
        column = cls_ref[0, :, k : k + 1]
        result = products[k * ROWS : (k + 1) * ROWS, 0:SPAN]
        for group in range(1, NCLS):
            part = products[k * ROWS : (k + 1) * ROWS, group * SPAN : (group + 1) * SPAN]
            result = jnp.where(column == group, part, result)
        store(k, result)


def kernel(
    film_ref,
    evap_ref,
    mask_ref,
    fcls_ref,
    scls_ref,
    inv_ref,
    convw_ref,
    mixw_ref,
    fluxw_ref,
    cot_ref,
    final_ref,
    grad_ref,
    convg_ref,
    mixg_ref,
    fluxg_ref,
    invhi_ref,
    invlo_ref,
    invt_ref,
    gath_b,
    gath_f,
    halo_s,
    halo_r,
    padf_ref,
    x_ref,
    wb_ref,
    wct_ref,
    bdf_ref,
    bdb_ref,
    fwb_ref,
    fwc_ref,
    clsrow_ref,
    a1_ref,
    d1_ref,
    sa_ref,
    d2_ref,
    src_ref,
    back_ref,
    sg_ref,
    cacc_ref,
    macc_ref,
    facc_ref,
    tt_ref,
    tot_ref,
    rim_s,
    rim_r,
    w36_ref,
    g_ref,
    p1_ref,
    q1_ref,
    p2_ref,
    q2_ref,
    p3_ref,
    q3_ref,
    p4_ref,
    ag_ssem,
    ag_rsem,
    nb_ssem,
    nb_rsem,
    ar_ssem,
    ar_rsem,
):
    side = film_ref.shape[2]
    nblocks = side // WIDTH
    sp = lax.axis_index("sp")
    rep = lax.axis_index("rep")
    nsp = DYLO * DZ * DX
    x_at = sp % DX
    z_at = (sp // DX) % DZ
    ylo_at = sp // (DX * DZ)
    yhi_at = rep // DCORE
    core_at = rep % DCORE
    y_at = yhi_at * DYLO + ylo_at
    member = sp % GROUP
    first = sp - member

    def at(r, s):
        return {"rep": r, "sp": s}

    up = (sp + nsp - 1) % nsp
    down = (sp + 1) % nsp

    def group_peer(s):
        return at(rep, first + (member + s) % GROUP)

    j_at = core_at * DX + x_at

    def corner_peer(s):
        other = (j_at + s) % (DCORE * DX)
        return at(yhi_at * DCORE + other // DX, sp - x_at + other % DX)

    def z_peer(s):
        other = (z_at + s) % DZ
        return at(rep, (ylo_at * DZ + other) * DX + x_at)

    def y_peer(s):
        other = (y_at + s) % (DYHI * DYLO)
        return at(
            (other // DYLO) * DCORE + core_at,
            ((other % DYLO) * DZ + z_at) * DX + x_at,
        )

    barrier = pltpu.get_barrier_semaphore()
    peers = [at(rep, up), at(rep, down)]
    for s in range(1, 8):
        peers += [group_peer(s), corner_peer(s), z_peer(s), y_peer(s)]
    for peer in peers:
        pl.semaphore_signal(barrier, inc=1, device_id=peer, device_id_type=MESH)

    def remote(src, dst, ssem, rsem, peer):
        return pltpu.make_async_remote_copy(
            src_ref=src,
            dst_ref=dst,
            send_sem=ssem,
            recv_sem=rsem,
            device_id=peer,
            device_id_type=MESH,
        )

    inv = inv_ref[...].reshape(NCLS * SPAN, SPAN)
    inv_hi, inv_lo = split2(inv)
    invhi_ref[...] = inv_hi
    invlo_ref[...] = inv_lo
    for c in range(NCLS):
        t_hi, t_lo = split2(inv_ref[c].T)
        invt_ref[0, c] = t_hi
        invt_ref[1, c] = t_lo

    nspan = side // SPAN
    lines = jnp.concatenate(
        [cot_ref[0, :, k * SPAN : (k + 1) * SPAN] for k in range(nspan)], axis=0
    )
    l_hi, l_lo = split2(lines)
    right_hi = jnp.concatenate([inv_hi[c * SPAN : (c + 1) * SPAN] for c in range(NCLS)], axis=1)
    right_lo = jnp.concatenate([inv_lo[c * SPAN : (c + 1) * SPAN] for c in range(NCLS)], axis=1)
    products = nn(l_hi, right_hi) + nn(l_lo, right_hi) + nn(l_hi, right_lo)

    def store_back(k, value):
        back_ref[:, k * SPAN : (k + 1) * SPAN] = value.astype(BF)

    span_select(products, scls_ref, store_back)
    own_rows = pl.ds(pl.multiple_of(member * ROWS, ROWS), ROWS)
    gath_b[own_rows, :] = back_ref[...]

    film = film_ref[0]
    evap = evap_ref[0]
    maskf = mask_ref[0].astype(F32)
    for c, feature in enumerate((film, film * film, maskf, evap)):
        feature = feature.astype(BF).astype(F32)
        padf_ref[c, 1 : ROWS + 1, :] = feature
        padf_ref[c, ROWS + 2 :, :] = jnp.zeros((6, side), F32)
        halo_s[0, c : c + 1, :] = feature[0:1]
        halo_s[1, c : c + 1, :] = feature[ROWS - 1 :]

    pl.semaphore_wait(barrier, len(peers))

    halo_up = remote(halo_s.at[0], halo_r.at[1], nb_ssem.at[0], nb_rsem.at[0], at(rep, up))
    halo_down = remote(halo_s.at[1], halo_r.at[0], nb_ssem.at[1], nb_rsem.at[1], at(rep, down))
    halo_up.start()
    halo_down.start()

    def gather_copies(which, slab, gath):
        return [
            remote(
                slab,
                gath.at[own_rows],
                ag_ssem.at[which, s - 1],
                ag_rsem.at[which, s - 1],
                group_peer(s),
            )
            for s in range(1, GROUP)
        ]

    back_copies = gather_copies(0, back_ref, gath_b)
    for copy in back_copies:
        copy.start()

    w36_ref[...] = jnp.zeros_like(w36_ref)
    for a in range(3):
        for b in range(3):
            k = (a * 3 + b) * CIN
            w36_ref[k : k + CIN, 0:HID] = convw_ref[a, b].astype(F32)
    w_t = w36_ref[...].T[:HID].astype(BF)
    k_at = iota((SPAN, WIDTH), 0)
    col = iota((SPAN, WIDTH), 1)
    piece = col // 16
    tap_row = col % 16
    wanted = (tap_row * 3 + piece % 3) * CIN + piece // 3
    pick = (k_at == wanted) & (tap_row < 3) & (piece < PIECES)
    band0 = nn(w_t, onehot(pick))
    band = jnp.concatenate(
        [band0] + [pltpu.roll(band0, r, axis=1) for r in range(1, HALF)], axis=0
    )
    wb_ref[...] = band.astype(BF)
    wct_ref[...] = band[:, :SPAN].T[:96].astype(BF)
    mix = mixw_ref[...]
    tile4 = onehot(iota((HID, WIDTH), 1) % HID == iota((HID, WIDTH), 0))
    wide = nn(mix, tile4)
    tall = jnp.concatenate([wide] * 4, axis=0)
    same = iota((WIDTH, WIDTH), 0) // HID == iota((WIDTH, WIDTH), 1) // HID
    diag = jnp.where(same, tall, 0.0)
    bdb_ref[...] = diag.astype(BF)
    bdf_ref[...] = diag.T.astype(BF)
    fw = fluxw_ref[...]
    tile8 = onehot(iota((HID, HALF * HID), 1) % HID == iota((HID, HALF * HID), 0))
    fw_wide = nn(jnp.broadcast_to(fw, (16, HID)), tile8)
    own = iota((16, HALF * HID), 1) // HID == iota((16, HALF * HID), 0)
    fwb_ref[...] = jnp.where(own, fw_wide, 0.0).astype(BF)
    eye = iota((HID, HID), 0) == iota((HID, HID), 1)
    fw_col = jnp.sum(
        jnp.where(eye, jnp.broadcast_to(fw.astype(F32), (HID, HID)), 0.0), axis=1, keepdims=True
    )
    fwc_ref[...] = jnp.broadcast_to(fw_col, (HID, WIDTH))

    fcls = fcls_ref[0].astype(F32).astype(BF)
    pick_span = onehot(iota((16, nspan), 1) == sp // GROUP)
    clsrow_ref[...] = nt(pick_span, fcls)

    halo_up.wait()
    halo_down.wait()
    for c in range(CIN):
        padf_ref[c, 0:1, :] = jnp.where(sp > 0, halo_r[0, c : c + 1, :], 0.0)
        padf_ref[c, ROWS + 1 : ROWS + 2, :] = jnp.where(
            sp < nsp - 1, halo_r[1, c : c + 1, :], 0.0
        )
    lane = iota((24, side), 1)
    for c in range(CIN):
        middle = padf_ref[c]
        left = jnp.where(lane == 0, 0.0, pltpu.roll(middle, 1, axis=1))
        right = jnp.where(lane == side - 1, 0.0, pltpu.roll(middle, side - 1, axis=1))
        for b, values in enumerate((left, middle, right)):
            s = (c * 3 + b) * 16
            for h in range(2):
                x_ref[h, s : s + 16, :] = values[HALF * h : HALF * h + 16].astype(BF)

    def forward(i, carry):
        cols = pl.ds(pl.multiple_of(i * WIDTH, WIDTH), WIDTH)
        sources = []
        for h in range(2):
            t1 = jnp.tanh(nn(wb_ref[:, : PIECES * 16], x_ref[h, :, cols]))
            a1 = t1.astype(BF)
            a1_ref[h, :, cols] = a1
            d1_ref[h, :, cols] = 1.0 - t1 * t1
            t2 = jnp.tanh(
                jnp.concatenate([nn(bdf_ref[...], a1[:WIDTH]), nn(bdf_ref[...], a1[WIDTH:])], axis=0)
            )
            sa = t2.astype(BF)
            sa_ref[h, :, cols] = sa
            d2_ref[h, :, cols] = 1.0 - t2 * t2
            flux = nn(fwb_ref[...], sa)[:HALF]
            rows = slice(HALF * h, HALF * h + HALF)
            drain = mask_ref[0, rows, cols].astype(F32) * evap_ref[0, rows, cols]
            sources.append(film_ref[0, rows, cols] + TIME_STEP * (flux - drain))
        src_ref[:, cols] = jnp.concatenate(sources, axis=0).astype(BF)
        return carry

    lax.fori_loop(0, nblocks, forward, 0)
    gath_f[own_rows, :] = src_ref[...]
    source_copies = gather_copies(1, src_ref, gath_f)
    for copy in source_copies:
        copy.start()

    def along_first(left, gathered, cols):
        both = nn(left, gathered[:, cols])
        total = both[: NCLS * ROWS] + both[NCLS * ROWS :]
        classes = clsrow_ref[:, cols]
        result = total[:ROWS]
        for c in range(1, NCLS):
            result = jnp.where(classes == c, total[c * ROWS : (c + 1) * ROWS], result)
        return result

    for s in range(1, GROUP):
        remote(
            back_ref,
            gath_b.at[pl.ds(pl.multiple_of(((member + GROUP - s) % GROUP) * ROWS, ROWS), ROWS)],
            ag_ssem.at[0, s - 1],
            ag_rsem.at[0, s - 1],
            group_peer(s),
        ).wait()
    left_t = jnp.concatenate(
        [invt_ref[n, c, own_rows, :] for n in range(2) for c in range(NCLS)], axis=0
    )
    wide_cols = min(512, side)

    def adjoint(i, carry):
        cols = pl.ds(pl.multiple_of(i * wide_cols, wide_cols), wide_cols)
        sg_ref[:, cols] = along_first(left_t, gath_b, cols)
        return carry

    lax.fori_loop(0, side // wide_cols, adjoint, 0)

    cacc_ref[...] = jnp.zeros_like(cacc_ref)
    macc_ref[...] = jnp.zeros_like(macc_ref)
    facc_ref[...] = jnp.zeros_like(facc_ref)

    def backward(i, carry):
        cols = pl.ds(pl.multiple_of(i * WIDTH, WIDTH), WIDTH)
        flux_sum = facc_ref[...]
        mixing = macc_ref[...]
        for h in range(2):
            flux_cot = TIME_STEP * sg_ref[HALF * h : HALF * h + HALF, cols]
            cots = []
            for r in range(HALF):
                of = slice(r * HID, (r + 1) * HID)
                row = jnp.broadcast_to(flux_cot[r : r + 1], (HID, WIDTH))
                flux_sum = flux_sum + sa_ref[h, of, cols].astype(F32) * row
                second_cot = (fwc_ref[...] * row).astype(BF).astype(F32)
                pre = (second_cot * d2_ref[h, of, cols]).astype(BF)
                mixing = mixing + nt(a1_ref[h, of, cols], pre)
                cots.append(pre)
            firsts = []
            for q in range(2):
                first_cot = nn(bdb_ref[...], jnp.concatenate(cots[4 * q : 4 * q + 4], axis=0))
                first_cot = first_cot.astype(BF).astype(F32)
                firsts.append((first_cot * d1_ref[h, WIDTH * q : WIDTH * q + WIDTH, cols]).astype(BF))
            pre_first = jnp.concatenate(firsts, axis=0)
            a1_ref[h, :, cols] = pre_first
            cacc_ref[...] += nt(pre_first, x_ref[h, :, cols])
        facc_ref[...] = flux_sum
        macc_ref[...] = mixing
        return carry

    lax.fori_loop(0, nblocks, backward, 0)

    whole = jnp.concatenate(
        [cacc_ref[...], jnp.zeros((HALF * HID, WIDTH - PIECES * 16), F32)], axis=1
    )
    taps = whole[:HID]
    for r in range(1, HALF):
        taps = taps + pltpu.roll(whole[r * HID : (r + 1) * HID], WIDTH - r, axis=1)
    k_at = iota((HID, WIDTH), 0)
    col = iota((HID, WIDTH), 1)
    piece = col // 16
    tap_row = col % 16
    wanted = (tap_row * 3 + piece % 3) * CIN + piece // 3
    pick = onehot((k_at == wanted) & (tap_row < 3) & (piece < PIECES))
    ones_row = onehot(k_at == 9 * CIN)
    low = jnp.zeros((HID, WIDTH), BF)
    right = jnp.zeros((HID, 2 * HID), F32)
    for t, f in zip(split3(taps), split3(facc_ref[...])):
        right = right + nt(pick, jnp.concatenate([low, t], axis=0))
        right = right + nt(ones_row, jnp.concatenate([low, f], axis=0))
    g_ref[...] = right
    g_ref[:, 0:HID] = macc_ref[...]

    own_block = pl.ds(pl.multiple_of(j_at * 8, 8), 8)
    p1_ref[j_at] = g_ref[own_block, :]
    stage1 = []
    for s in range(1, 8):
        other = (j_at + s) % 8
        stage1.append(
            remote(
                g_ref.at[pl.ds(pl.multiple_of(other * 8, 8), 8)],
                p1_ref.at[j_at],
                ar_ssem.at[0, s - 1],
                ar_rsem.at[0, s - 1],
                corner_peer(s),
            )
        )
    for copy in stage1:
        copy.start()

    def features_back(i, carry):
        cols = pl.ds(pl.multiple_of(i * WIDTH, WIDTH), WIDTH)
        for h in range(2):
            tt_ref[h, :, cols] = nn(wct_ref[...], a1_ref[h, :, cols])
        return carry

    lax.fori_loop(0, nblocks, features_back, 0)

    def finish(stage, slots, at_index, source, send_peer):
        for s in range(1, 8):
            remote(
                source,
                slots.at[(at_index + 8 - s) % 8],
                ar_ssem.at[stage, s - 1],
                ar_rsem.at[stage, s - 1],
                send_peer(s),
            ).wait()

    def begin(stage, slots, at_index, source, send_peer):
        for s in range(1, 8):
            remote(
                source,
                slots.at[at_index],
                ar_ssem.at[stage, s - 1],
                ar_rsem.at[stage, s - 1],
                send_peer(s),
            ).start()

    def summed(slots):
        total = slots[0]
        for n in range(1, 8):
            total = total + slots[n]
        return total

    finish(0, p1_ref, j_at, g_ref.at[own_block], corner_peer)
    q1_ref[...] = summed(p1_ref)
    p2_ref[z_at] = q1_ref[...]
    begin(1, p2_ref, z_at, q1_ref, z_peer)

    lane = iota((16, side), 1)
    for c in range(2):
        parts = []
        for h in range(2):
            s = c * 48
            left = jnp.where(lane == side - 1, 0.0, pltpu.roll(tt_ref[h, s : s + 16, :], side - 1, axis=1))
            right = jnp.where(lane == 0, 0.0, pltpu.roll(tt_ref[h, s + 32 : s + 48, :], 1, axis=1))
            parts.append(left + tt_ref[h, s + 16 : s + 32, :] + right)
        tot_ref[c, 0:8, :] = parts[0][0:8]
        tot_ref[c, 8:16, :] = parts[0][8:16] + parts[1][0:8]
        tot_ref[c, 16:24, :] = parts[1][8:16]
        rim_s[0, c : c + 1, :] = parts[0][0:1]
        rim_s[1, c : c + 1, :] = parts[1][9:10]
    rim_up = remote(rim_s.at[0], rim_r.at[1], nb_ssem.at[2], nb_rsem.at[2], at(rep, up))
    rim_down = remote(rim_s.at[1], rim_r.at[0], nb_ssem.at[3], nb_rsem.at[3], at(rep, down))
    rim_up.start()
    rim_down.start()

    for s in range(1, GROUP):
        remote(
            src_ref,
            gath_f.at[pl.ds(pl.multiple_of(((member + GROUP - s) % GROUP) * ROWS, ROWS), ROWS)],
            ag_ssem.at[1, s - 1],
            ag_rsem.at[1, s - 1],
            group_peer(s),
        ).wait()
    left_f = jnp.concatenate(
        [
            half[pl.ds(pl.multiple_of(c * SPAN + member * ROWS, ROWS), ROWS), :]
            for half in (invhi_ref, invlo_ref)
            for c in range(NCLS)
        ],
        axis=0,
    )
    pieces = []
    for i in range(side // wide_cols):
        across = along_first(left_f, gath_f, slice(i * wide_cols, (i + 1) * wide_cols))
        for k in range(wide_cols // SPAN):
            pieces.append(across[:, k * SPAN : (k + 1) * SPAN])
    l_hi, l_lo = split2(jnp.concatenate(pieces, axis=0))
    f_hi = invhi_ref[...]
    products = nt(l_hi, f_hi) + nt(l_lo, f_hi) + nt(l_hi, invlo_ref[...])

    def store_final(k, value):
        final_ref[0, :, k * SPAN : (k + 1) * SPAN] = value

    span_select(products, scls_ref, store_final)

    finish(1, p2_ref, z_at, q1_ref, z_peer)
    q2_ref[...] = summed(p2_ref)
    p3_ref[y_at] = q2_ref[...]
    begin(2, p3_ref, y_at, q2_ref, y_peer)

    rim_up.wait()
    rim_down.wait()
    for c in range(2):
        tot_ref[c, 1:2, :] += jnp.where(sp > 0, rim_r[0, c : c + 1, :], 0.0)
        tot_ref[c, ROWS : ROWS + 1, :] += jnp.where(sp < nsp - 1, rim_r[1, c : c + 1, :], 0.0)
    cot0 = tot_ref[0, 1 : ROWS + 1, :].astype(BF).astype(F32)
    cot1 = tot_ref[1, 1 : ROWS + 1, :].astype(BF).astype(F32)
    grad_ref[0] = sg_ref[...] + cot0 + 2.0 * film_ref[0] * cot1

    finish(2, p3_ref, y_at, q2_ref, y_peer)
    q3_ref[...] = summed(p3_ref)
    p4_ref[j_at] = q3_ref[...]
    begin(3, p4_ref, j_at, q3_ref, corner_peer)
    finish(3, p4_ref, j_at, q3_ref, corner_peer)
    scale = 1.0 / math.sqrt(DYHI * DCORE * side * side)
    result = p4_ref[...].reshape(HID, 2 * HID) * scale
    mixg_ref[...] = result[:, :HID]
    other = pltpu.roll(result, HID, axis=1)[:, :HID]
    for a in range(3):
        for b in range(3):
            k = (a * 3 + b) * CIN
            convg_ref[a, b] = other[k : k + CIN]
    fluxg_ref[...] = other[9 * CIN : 9 * CIN + 1]


def on_device(film, evap, mask, fcls, scls, inv, convw, mixw, fluxw, cot):
    side = film.shape[2]
    rows = film.shape[1]
    vmem = pl.BlockSpec(memory_space=pltpu.VMEM)
    outs = pl.pallas_call(
        kernel,
        out_shape=(
            jax.ShapeDtypeStruct(film.shape, F32),
            jax.ShapeDtypeStruct(film.shape, F32),
            jax.ShapeDtypeStruct(convw.shape, F32),
            jax.ShapeDtypeStruct(mixw.shape, F32),
            jax.ShapeDtypeStruct((1, HID), F32),
        ),
        in_specs=[vmem] * 10,
        out_specs=(vmem,) * 5,
        scratch_shapes=[
            pltpu.VMEM((NCLS * SPAN, SPAN), BF),
            pltpu.VMEM((NCLS * SPAN, SPAN), BF),
            pltpu.VMEM((2, NCLS, SPAN, SPAN), BF),
            pltpu.VMEM((SPAN, side), BF),
            pltpu.VMEM((SPAN, side), BF),
            pltpu.VMEM((2, CIN, side), F32),
            pltpu.VMEM((2, CIN, side), F32),
            pltpu.VMEM((CIN, 24, side), F32),
            pltpu.VMEM((2, PIECES * 16, side), BF),
            pltpu.VMEM((HALF * HID, WIDTH), BF),
            pltpu.VMEM((96, HALF * HID), BF),
            pltpu.VMEM((WIDTH, WIDTH), BF),
            pltpu.VMEM((WIDTH, WIDTH), BF),
            pltpu.VMEM((16, HALF * HID), BF),
            pltpu.VMEM((HID, WIDTH), F32),
            pltpu.VMEM((16, side), F32),
            pltpu.VMEM((2, HALF * HID, side), BF),
            pltpu.VMEM((2, HALF * HID, side), F32),
            pltpu.VMEM((2, HALF * HID, side), BF),
            pltpu.VMEM((2, HALF * HID, side), F32),
            pltpu.VMEM((rows, side), BF),
            pltpu.VMEM((rows, side), BF),
            pltpu.VMEM((rows, side), F32),
            pltpu.VMEM((HALF * HID, PIECES * 16), F32),
            pltpu.VMEM((HID, HID), F32),
            pltpu.VMEM((HID, WIDTH), F32),
            pltpu.VMEM((2, 96, side), F32),
            pltpu.VMEM((2, 24, side), F32),
            pltpu.VMEM((2, 2, side), F32),
            pltpu.VMEM((2, 2, side), F32),
            pltpu.VMEM((SPAN, SPAN), F32),
            pltpu.VMEM((HID, 2 * HID), F32),
            pltpu.VMEM((8, 8, 2 * HID), F32),
            pltpu.VMEM((8, 2 * HID), F32),
            pltpu.VMEM((8, 8, 2 * HID), F32),
            pltpu.VMEM((8, 2 * HID), F32),
            pltpu.VMEM((8, 8, 2 * HID), F32),
            pltpu.VMEM((8, 2 * HID), F32),
            pltpu.VMEM((8, 8, 2 * HID), F32),
            pltpu.SemaphoreType.DMA((2, 7)),
            pltpu.SemaphoreType.DMA((2, 7)),
            pltpu.SemaphoreType.DMA((4,)),
            pltpu.SemaphoreType.DMA((4,)),
            pltpu.SemaphoreType.DMA((4, 7)),
            pltpu.SemaphoreType.DMA((4, 7)),
        ],
        compiler_params=pltpu.CompilerParams(
            collective_id=0, has_side_effects=True, vmem_limit_bytes=60 * 1024 * 1024
        ),
    )(film, evap, mask, fcls, scls, inv, convw, mixw, fluxw.reshape(1, HID), cot)
    return outs[0], outs[1], outs[2], outs[3], outs[4].reshape(HID)


def solution(mesh):
    sizes = dict(mesh.shape)
    assert sizes == {"rep": DYHI * DCORE, "sp": DYLO * DZ * DX}
    return jax.shard_map(
        on_device,
        mesh=mesh,
        in_specs=(
            P("rep", "sp", None),
            P("rep", "sp", None),
            P("rep", "sp", None),
            P("rep", None, None),
            P("rep", "sp", None),
            P(),
            P(),
            P(),
            P(),
            P("rep", "sp", None),
        ),
        out_specs=(P("rep", "sp", None), P("rep", "sp", None), P(), P(), P()),
        check_vma=False,
    )
```

```python
import math

import jax
import jax.numpy as jnp
from jax import lax
from jax.experimental import pallas as pl
from jax.experimental.pallas import tpu as pltpu
from jax.sharding import PartitionSpec as P

BF = jnp.bfloat16
F32 = jnp.float32
MESH = pl.DeviceIdType.MESH
SPAN = 128
ROWS = 16
HALF = 8
HID = 64
CIN = 4
PIECES = 12
WIDTH = 256
NCLS = 4
GROUP = SPAN // ROWS
DX, DZ, DYLO, DYHI, DCORE = 4, 8, 4, 2, 2
TIME_STEP = 0.5


def nt(a, b):
    return lax.dot_general(a, b, (((1,), (1,)), ((), ())), preferred_element_type=F32)


def nn(a, b):
    return lax.dot_general(a, b, (((1,), (0,)), ((), ())), preferred_element_type=F32)


def split2(v):
    hi = v.astype(BF)
    return hi, (v - hi.astype(F32)).astype(BF)


def split3(v):
    hi = v.astype(BF)
    rest = v - hi.astype(F32)
    mid = rest.astype(BF)
    return hi, mid, (rest - mid.astype(F32)).astype(BF)


def iota(shape, dim):
    return lax.broadcasted_iota(jnp.int32, shape, dim)


def onehot(cond):
    return jnp.where(cond, 1.0, 0.0).astype(BF)


def span_select(products, cls_ref, store):
    for k in range(products.shape[0] // ROWS):
        column = cls_ref[0, :, k : k + 1]
        result = products[k * ROWS : (k + 1) * ROWS, 0:SPAN]
        for group in range(1, NCLS):
            part = products[k * ROWS : (k + 1) * ROWS, group * SPAN : (group + 1) * SPAN]
            result = jnp.where(column == group, part, result)
        store(k, result)


def kernel(
    film_hbm,
    evap_hbm,
    mask_hbm,
    fcls_hbm,
    scls_hbm,
    inv_hbm,
    convw_hbm,
    mixw_hbm,
    fluxw_hbm,
    cot_hbm,
    final_hbm,
    grad_hbm,
    gsum_hbm,
    film_ref,
    evap_ref,
    mask_ref,
    fcls_ref,
    scls_ref,
    inv_ref,
    convw_ref,
    mixw_ref,
    fluxw_ref,
    cot_ref,
    final_ref,
    grad_ref,
    gsum_ref,
    invs_ref,
    recv_ref,
    mid_ref,
    halo_s,
    halo_r,
    padf_ref,
    x_ref,
    wb_ref,
    wct_ref,
    bdf_ref,
    bdb_ref,
    fwb_ref,
    fwc_ref,
    a1_ref,
    d1_ref,
    sa_ref,
    u_ref,
    v_ref,
    src_ref,
    back_ref,
    sg_ref,
    across_ref,
    cacc_ref,
    macc_ref,
    facc_ref,
    tt_ref,
    tot_ref,
    rim_s,
    rim_r,
    w36_ref,
    g_ref,
    p1_ref,
    q1_ref,
    p2_ref,
    q2_ref,
    p3_ref,
    q3_ref,
    p4_ref,
    in_sem,
    out_sem,
    ag_ssem,
    ag_rsem,
    nb_ssem,
    nb_rsem,
    ar_ssem,
    ar_rsem,
):
    inputs = [
        pltpu.make_async_copy(hbm, ref, in_sem.at[n])
        for n, (hbm, ref) in enumerate(
            (
                (cot_hbm, cot_ref),
                (inv_hbm, inv_ref),
                (scls_hbm, scls_ref),
                (film_hbm, film_ref),
                (evap_hbm, evap_ref),
                (mask_hbm, mask_ref),
                (fcls_hbm, fcls_ref),
                (convw_hbm, convw_ref),
                (mixw_hbm, mixw_ref),
                (fluxw_hbm, fluxw_ref),
            )
        )
    ]
    for copy in inputs:
        copy.start()
    side = film_ref.shape[2]
    nblocks = side // WIDTH
    sp = lax.axis_index("sp")
    rep = lax.axis_index("rep")
    nsp = DYLO * DZ * DX
    x_at = sp % DX
    z_at = (sp // DX) % DZ
    ylo_at = sp // (DX * DZ)
    yhi_at = rep // DCORE
    core_at = rep % DCORE
    y_at = yhi_at * DYLO + ylo_at
    member = sp % GROUP
    first = sp - member

    def at(r, s):
        return {"rep": r, "sp": s}

    up = (sp + nsp - 1) % nsp
    down = (sp + 1) % nsp

    def group_peer(s):
        return at(rep, first + (member + s) % GROUP)

    j_at = core_at * DX + x_at

    def corner_peer(s):
        other = (j_at + s) % (DCORE * DX)
        return at(yhi_at * DCORE + other // DX, sp - x_at + other % DX)

    def z_peer(s):
        other = (z_at + s) % DZ
        return at(rep, (ylo_at * DZ + other) * DX + x_at)

    def y_peer(s):
        other = (y_at + s) % (DYHI * DYLO)
        return at(
            (other // DYLO) * DCORE + core_at,
            ((other % DYLO) * DZ + z_at) * DX + x_at,
        )

    barrier = pltpu.get_barrier_semaphore()
    peers = [at(rep, up), at(rep, down)]
    for s in range(1, 8):
        peers += [group_peer(s), corner_peer(s), z_peer(s), y_peer(s)]
    for peer in peers:
        pl.semaphore_signal(barrier, inc=1, device_id=peer, device_id_type=MESH)

    def remote(src, dst, ssem, rsem, peer):
        return pltpu.make_async_remote_copy(
            src_ref=src,
            dst_ref=dst,
            send_sem=ssem,
            recv_sem=rsem,
            device_id=peer,
            device_id_type=MESH,
        )

    for copy in inputs[:3]:
        copy.wait()
    inv_hi, inv_lo = split2(inv_ref[...].reshape(NCLS * SPAN, SPAN))
    for c in range(NCLS):
        of = slice(c * SPAN, (c + 1) * SPAN)
        t_hi, t_lo = split2(inv_ref[c].T)
        invs_ref[0, 0, c] = t_hi
        invs_ref[0, 1, c] = t_lo
        invs_ref[1, 0, c] = inv_hi[of]
        invs_ref[1, 1, c] = inv_lo[of]

    nspan = side // SPAN
    lines = jnp.concatenate(
        [cot_ref[0, :, k * SPAN : (k + 1) * SPAN] for k in range(nspan)], axis=0
    )
    l_hi, l_lo = split2(lines)
    right_hi = jnp.concatenate([inv_hi[c * SPAN : (c + 1) * SPAN] for c in range(NCLS)], axis=1)
    right_lo = jnp.concatenate([inv_lo[c * SPAN : (c + 1) * SPAN] for c in range(NCLS)], axis=1)
    products = nn(l_hi, right_hi) + nn(l_lo, right_hi) + nn(l_hi, right_lo)

    def store_back(k, value):
        back_ref[:, k * SPAN : (k + 1) * SPAN] = value.astype(BF)

    span_select(products, scls_ref, store_back)
    own_rows = pl.ds(pl.multiple_of(member * ROWS, ROWS), ROWS)
    chunk = side // GROUP

    def columns_of(n):
        return pl.ds(pl.multiple_of(n * chunk, chunk), chunk)

    def rows_of(n):
        return pl.ds(pl.multiple_of(n * ROWS, ROWS), ROWS)

    def from_peer(s):
        return (member + GROUP - s) % GROUP

    def span_out(which, field):
        recv_ref[which, own_rows, :] = field[:, columns_of(member)]
        for s in range(1, GROUP):
            remote(
                field.at[:, columns_of((member + s) % GROUP)],
                recv_ref.at[which, own_rows],
                ag_ssem.at[2 * which, s - 1],
                ag_rsem.at[2 * which, s - 1],
                group_peer(s),
            ).start()

    def span_solve(which, field, result):
        for s in range(1, GROUP):
            remote(
                field.at[:, columns_of((member + s) % GROUP)],
                recv_ref.at[which, rows_of(from_peer(s))],
                ag_ssem.at[2 * which, s - 1],
                ag_rsem.at[2 * which, s - 1],
                group_peer(s),
            ).wait()
        values = recv_ref[which]
        line_cls = fcls_ref[0, :, columns_of(member)]
        own_span = iota(line_cls.shape, 0) == sp // GROUP
        classes = jnp.sum(jnp.where(own_span, line_cls, 0), axis=0, keepdims=True)
        solved = None
        for c in range(NCLS):
            product = nn(invs_ref[which, 0, c], values) + nn(invs_ref[which, 1, c], values)
            solved = product if c == 0 else jnp.where(classes == c, product, solved)
        mid_ref[which] = solved.astype(BF)
        result[:, columns_of(member)] = mid_ref[which, own_rows, :]
        for s in range(1, GROUP):
            remote(
                mid_ref.at[which, rows_of((member + s) % GROUP)],
                result.at[:, columns_of(member)],
                ag_ssem.at[2 * which + 1, s - 1],
                ag_rsem.at[2 * which + 1, s - 1],
                group_peer(s),
            ).start()

    def span_in(which, result):
        for s in range(1, GROUP):
            remote(
                mid_ref.at[which, rows_of((member + s) % GROUP)],
                result.at[:, columns_of(from_peer(s))],
                ag_ssem.at[2 * which + 1, s - 1],
                ag_rsem.at[2 * which + 1, s - 1],
                group_peer(s),
            ).wait()

    for copy in inputs[3:]:
        copy.wait()

    film = film_ref[0]
    evap = evap_ref[0]
    maskf = mask_ref[0].astype(F32)
    for c, feature in enumerate((film, film * film, maskf, evap)):
        feature = feature.astype(BF).astype(F32)
        padf_ref[c, 1 : ROWS + 1, :] = feature
        padf_ref[c, ROWS + 2 :, :] = jnp.zeros((6, side), F32)
        halo_s[0, c : c + 1, :] = feature[0:1]
        halo_s[1, c : c + 1, :] = feature[ROWS - 1 :]

    pl.semaphore_wait(barrier, len(peers))

    halo_up = remote(halo_s.at[0], halo_r.at[1], nb_ssem.at[0], nb_rsem.at[0], at(rep, up))
    halo_down = remote(halo_s.at[1], halo_r.at[0], nb_ssem.at[1], nb_rsem.at[1], at(rep, down))
    halo_up.start()
    halo_down.start()

    span_out(0, back_ref)

    w36_ref[...] = jnp.zeros_like(w36_ref)
    for a in range(3):
        for b in range(3):
            k = (a * 3 + b) * CIN
            w36_ref[k : k + CIN, 0:HID] = convw_ref[a, b].astype(F32)
    w_t = w36_ref[...].T[:HID].astype(BF)
    k_at = iota((SPAN, WIDTH), 0)
    col = iota((SPAN, WIDTH), 1)
    piece = col // 16
    tap_row = col % 16
    wanted = (tap_row * 3 + piece % 3) * CIN + piece // 3
    pick = (k_at == wanted) & (tap_row < 3) & (piece < PIECES)
    band0 = nn(w_t, onehot(pick))
    band = jnp.concatenate(
        [band0] + [pltpu.roll(band0, r, axis=1) for r in range(1, HALF)], axis=0
    )
    wb_ref[...] = band.astype(BF)
    wct_ref[...] = band[:, :SPAN].T[:96].astype(BF)
    mix = mixw_ref[...]
    tile4 = onehot(iota((HID, WIDTH), 1) % HID == iota((HID, WIDTH), 0))
    wide = nn(mix, tile4)
    tall = jnp.concatenate([wide] * 4, axis=0)
    same = iota((WIDTH, WIDTH), 0) // HID == iota((WIDTH, WIDTH), 1) // HID
    diag = jnp.where(same, tall, 0.0)
    bdb_ref[...] = diag.astype(BF)
    bdf_ref[...] = diag.T.astype(BF)
    fw = fluxw_ref[...]
    tile8 = onehot(iota((HID, HALF * HID), 1) % HID == iota((HID, HALF * HID), 0))
    fw_wide = nn(jnp.broadcast_to(fw, (16, HID)), tile8)
    own = iota((16, HALF * HID), 1) // HID == iota((16, HALF * HID), 0)
    fwb_ref[...] = jnp.where(own, fw_wide, 0.0).astype(BF)
    eye = iota((HID, HID), 0) == iota((HID, HID), 1)
    fw_col = jnp.sum(
        jnp.where(eye, jnp.broadcast_to(fw.astype(F32), (HID, HID)), 0.0), axis=1, keepdims=True
    )
    fwc_ref[...] = jnp.concatenate([jnp.broadcast_to(fw_col, (HID, WIDTH))] * 4, axis=0)

    halo_up.wait()
    halo_down.wait()
    for c in range(CIN):
        padf_ref[c, 0:1, :] = jnp.where(sp > 0, halo_r[0, c : c + 1, :], 0.0)
        padf_ref[c, ROWS + 1 : ROWS + 2, :] = jnp.where(
            sp < nsp - 1, halo_r[1, c : c + 1, :], 0.0
        )
    lane = iota((24, side), 1)
    for c in range(CIN):
        middle = padf_ref[c]
        left = jnp.where(lane == 0, 0.0, pltpu.roll(middle, 1, axis=1))
        right = jnp.where(lane == side - 1, 0.0, pltpu.roll(middle, side - 1, axis=1))
        for b, values in enumerate((left, middle, right)):
            s = (c * 3 + b) * 16
            for h in range(2):
                x_ref[h, s : s + 16, :] = values[HALF * h : HALF * h + 16].astype(BF)

    def forward(i, carry):
        cols = pl.ds(pl.multiple_of(i * WIDTH, WIDTH), WIDTH)
        sources = []
        for h in range(2):
            t1 = jnp.tanh(nn(wb_ref[:, : PIECES * 16], x_ref[h, :, cols]))
            a1 = t1.astype(BF)
            a1_ref[h, :, cols] = a1
            d1_ref[h] = 1.0 - t1 * t1
            actives = []
            for q in range(2):
                of = slice(q * WIDTH, (q + 1) * WIDTH)
                t2 = jnp.tanh(nn(bdf_ref[...], a1[of]))
                actives.append(t2.astype(BF))
                u = (fwc_ref[...] * (1.0 - t2 * t2)).astype(BF)
                u_ref[h, of, cols] = u
                v_ref[h, of, cols] = (d1_ref[h, of, :] * nn(bdb_ref[...], u)).astype(BF)
            sa = jnp.concatenate(actives, axis=0)
            sa_ref[h, :, cols] = sa
            flux = nn(fwb_ref[...], sa)[:HALF]
            rows = slice(HALF * h, HALF * h + HALF)
            drain = mask_ref[0, rows, cols].astype(F32) * evap_ref[0, rows, cols]
            sources.append(film_ref[0, rows, cols] + TIME_STEP * (flux - drain))
        src_ref[:, cols] = jnp.concatenate(sources, axis=0).astype(BF)
        return carry

    lax.fori_loop(0, nblocks // 2, forward, 0)
    span_solve(0, back_ref, sg_ref)
    lax.fori_loop(nblocks // 2, nblocks, forward, 0)
    span_out(1, src_ref)
    span_in(0, sg_ref)

    cacc_ref[...] = jnp.zeros_like(cacc_ref)
    macc_ref[...] = jnp.zeros_like(macc_ref)
    facc_ref[...] = jnp.zeros_like(facc_ref)

    def backward(i, carry):
        cols = pl.ds(pl.multiple_of(i * WIDTH, WIDTH), WIDTH)
        flux_sum = facc_ref[...]
        mixing = macc_ref[...]
        flux_cots = TIME_STEP * sg_ref[:, cols].astype(F32)
        for h in range(2):
            firsts = []
            for r in range(HALF):
                of = slice(r * HID, (r + 1) * HID)
                at_row = HALF * h + r
                row = jnp.broadcast_to(flux_cots[at_row : at_row + 1], (HID, WIDTH))
                flux_sum = flux_sum + sa_ref[h, of, cols].astype(F32) * row
                pre = (u_ref[h, of, cols].astype(F32) * row).astype(BF)
                mixing = mixing + nt(a1_ref[h, of, cols], pre)
                firsts.append((v_ref[h, of, cols].astype(F32) * row).astype(BF))
            pre_first = jnp.concatenate(firsts, axis=0)
            v_ref[h, :, cols] = pre_first
            cacc_ref[...] += nt(pre_first, x_ref[h, :, cols])
        facc_ref[...] = flux_sum
        macc_ref[...] = mixing
        return carry

    lax.fori_loop(0, nblocks, backward, 0)

    whole = jnp.concatenate(
        [cacc_ref[...], jnp.zeros((HALF * HID, WIDTH - PIECES * 16), F32)], axis=1
    )
    taps = whole[:HID]
    for r in range(1, HALF):
        taps = taps + pltpu.roll(whole[r * HID : (r + 1) * HID], WIDTH - r, axis=1)
    k_at = iota((HID, WIDTH), 0)
    col = iota((HID, WIDTH), 1)
    piece = col // 16
    tap_row = col % 16
    wanted = (tap_row * 3 + piece % 3) * CIN + piece // 3
    pick = onehot((k_at == wanted) & (tap_row < 3) & (piece < PIECES))
    ones_row = onehot(k_at == 9 * CIN)
    low = jnp.zeros((HID, WIDTH), BF)
    right = jnp.zeros((HID, 2 * HID), F32)
    for t, f in zip(split3(taps), split3(facc_ref[...])):
        right = right + nt(pick, jnp.concatenate([low, t], axis=0))
        right = right + nt(ones_row, jnp.concatenate([low, f], axis=0))
    g_ref[...] = right
    g_ref[:, 0:HID] = macc_ref[...]

    own_block = pl.ds(pl.multiple_of(j_at * 8, 8), 8)
    p1_ref[j_at] = g_ref[own_block, :]
    stage1 = []
    for s in range(1, 8):
        other = (j_at + s) % 8
        stage1.append(
            remote(
                g_ref.at[pl.ds(pl.multiple_of(other * 8, 8), 8)],
                p1_ref.at[j_at],
                ar_ssem.at[0, s - 1],
                ar_rsem.at[0, s - 1],
                corner_peer(s),
            )
        )
    for copy in stage1:
        copy.start()

    span_solve(1, src_ref, across_ref)

    def features_back(i, carry):
        cols = pl.ds(pl.multiple_of(i * WIDTH, WIDTH), WIDTH)
        for h in range(2):
            tt_ref[h, :, cols] = nn(wct_ref[...], v_ref[h, :, cols])
        return carry

    lax.fori_loop(0, nblocks, features_back, 0)

    def finish(stage, slots, at_index, source, send_peer):
        for s in range(1, 8):
            remote(
                source,
                slots.at[(at_index + 8 - s) % 8],
                ar_ssem.at[stage, s - 1],
                ar_rsem.at[stage, s - 1],
                send_peer(s),
            ).wait()

    def begin(stage, slots, at_index, source, send_peer):
        for s in range(1, 8):
            remote(
                source,
                slots.at[at_index],
                ar_ssem.at[stage, s - 1],
                ar_rsem.at[stage, s - 1],
                send_peer(s),
            ).start()

    def summed(slots):
        total = slots[0]
        for n in range(1, 8):
            total = total + slots[n]
        return total

    finish(0, p1_ref, j_at, g_ref.at[own_block], corner_peer)
    q1_ref[...] = summed(p1_ref)
    p2_ref[z_at] = q1_ref[...]
    begin(1, p2_ref, z_at, q1_ref, z_peer)

    lane = iota((16, side), 1)
    for c in range(2):
        parts = []
        for h in range(2):
            s = c * 48
            left = jnp.where(lane == side - 1, 0.0, pltpu.roll(tt_ref[h, s : s + 16, :], side - 1, axis=1))
            right = jnp.where(lane == 0, 0.0, pltpu.roll(tt_ref[h, s + 32 : s + 48, :], 1, axis=1))
            parts.append(left + tt_ref[h, s + 16 : s + 32, :] + right)
        tot_ref[c, 0:8, :] = parts[0][0:8]
        tot_ref[c, 8:16, :] = parts[0][8:16] + parts[1][0:8]
        tot_ref[c, 16:24, :] = parts[1][8:16]
        rim_s[0, c : c + 1, :] = parts[0][0:1]
        rim_s[1, c : c + 1, :] = parts[1][9:10]
    rim_up = remote(rim_s.at[0], rim_r.at[1], nb_ssem.at[2], nb_rsem.at[2], at(rep, up))
    rim_down = remote(rim_s.at[1], rim_r.at[0], nb_ssem.at[3], nb_rsem.at[3], at(rep, down))
    rim_up.start()
    rim_down.start()

    span_in(1, across_ref)
    pieces = [across_ref[:, k * SPAN : (k + 1) * SPAN] for k in range(nspan)]
    lines = jnp.concatenate(pieces, axis=0)
    f_hi = invs_ref[1, 0].reshape(NCLS * SPAN, SPAN)
    f_lo = invs_ref[1, 1].reshape(NCLS * SPAN, SPAN)
    products = nt(lines, f_hi) + nt(lines, f_lo)

    def store_final(k, value):
        final_ref[0, :, k * SPAN : (k + 1) * SPAN] = value

    span_select(products, scls_ref, store_final)
    final_out = pltpu.make_async_copy(final_ref, final_hbm, out_sem.at[0])
    final_out.start()

    finish(1, p2_ref, z_at, q1_ref, z_peer)
    q2_ref[...] = summed(p2_ref)
    p3_ref[y_at] = q2_ref[...]
    begin(2, p3_ref, y_at, q2_ref, y_peer)

    rim_up.wait()
    rim_down.wait()
    for c in range(2):
        tot_ref[c, 1:2, :] += jnp.where(sp > 0, rim_r[0, c : c + 1, :], 0.0)
        tot_ref[c, ROWS : ROWS + 1, :] += jnp.where(sp < nsp - 1, rim_r[1, c : c + 1, :], 0.0)
    cot0 = tot_ref[0, 1 : ROWS + 1, :].astype(BF).astype(F32)
    cot1 = tot_ref[1, 1 : ROWS + 1, :].astype(BF).astype(F32)
    grad_ref[0] = sg_ref[...].astype(F32) + cot0 + 2.0 * film_ref[0] * cot1
    grad_out = pltpu.make_async_copy(grad_ref, grad_hbm, out_sem.at[1])
    grad_out.start()

    finish(2, p3_ref, y_at, q2_ref, y_peer)
    q3_ref[...] = summed(p3_ref)
    p4_ref[j_at] = q3_ref[...]
    begin(3, p4_ref, j_at, q3_ref, corner_peer)
    finish(3, p4_ref, j_at, q3_ref, corner_peer)
    scale = 1.0 / math.sqrt(DYHI * DCORE * side * side)
    gsum_ref[...] = p4_ref[...].reshape(HID, 2 * HID) * scale
    gsum_out = pltpu.make_async_copy(gsum_ref, gsum_hbm, out_sem.at[2])
    gsum_out.start()
    final_out.wait()
    grad_out.wait()
    gsum_out.wait()


def hand_out(final_in, grad_in, gsum_in, final_ref, grad_ref, convg_ref, mixg_ref, fluxg_ref):
    final_ref[...] = final_in[...]
    grad_ref[...] = grad_in[...]
    result = gsum_in[...]
    mixg_ref[...] = result[:, :HID]
    other = pltpu.roll(result, HID, axis=1)[:, :HID]
    for a in range(3):
        for b in range(3):
            k = (a * 3 + b) * CIN
            convg_ref[a, b] = other[k : k + CIN]
    fluxg_ref[...] = other[9 * CIN : 9 * CIN + 1]


def on_device(film, evap, mask, fcls, scls, inv, convw, mixw, fluxw, cot):
    side = film.shape[2]
    rows = film.shape[1]
    vmem = pl.BlockSpec(memory_space=pltpu.VMEM)
    hbm = pl.BlockSpec(memory_space=pl.ANY)
    args = (
        film,
        evap,
        mask,
        jnp.swapaxes(fcls, 1, 2),
        scls,
        inv,
        convw,
        mixw,
        fluxw.reshape(1, HID),
        cot,
    )
    chunk = side // GROUP
    tall = HALF * HID
    slab = jax.ShapeDtypeStruct(film.shape, F32)
    block = jax.ShapeDtypeStruct((HID, 2 * HID), F32)
    final, grad, gsum = pl.pallas_call(
        kernel,
        out_shape=(slab, slab, block),
        in_specs=[hbm] * 10,
        out_specs=(hbm,) * 3,
        scratch_shapes=[pltpu.VMEM(a.shape, a.dtype) for a in args]
        + [
            pltpu.VMEM(film.shape, F32),
            pltpu.VMEM(film.shape, F32),
            pltpu.VMEM((HID, 2 * HID), F32),
            pltpu.VMEM((2, 2, NCLS, SPAN, SPAN), BF),
            pltpu.VMEM((2, SPAN, chunk), BF),
            pltpu.VMEM((2, SPAN, chunk), BF),
            pltpu.VMEM((2, CIN, side), F32),
            pltpu.VMEM((2, CIN, side), F32),
            pltpu.VMEM((CIN, 24, side), F32),
            pltpu.VMEM((2, PIECES * 16, side), BF),
            pltpu.VMEM((tall, WIDTH), BF),
            pltpu.VMEM((96, tall), BF),
            pltpu.VMEM((WIDTH, WIDTH), BF),
            pltpu.VMEM((WIDTH, WIDTH), BF),
            pltpu.VMEM((16, tall), BF),
            pltpu.VMEM((WIDTH, WIDTH), F32),
            pltpu.VMEM((2, tall, side), BF),
            pltpu.VMEM((2, tall, WIDTH), F32),
            pltpu.VMEM((2, tall, side), BF),
            pltpu.VMEM((2, tall, side), BF),
            pltpu.VMEM((2, tall, side), BF),
            pltpu.VMEM((rows, side), BF),
            pltpu.VMEM((rows, side), BF),
            pltpu.VMEM((rows, side), BF),
            pltpu.VMEM((rows, side), BF),
            pltpu.VMEM((tall, PIECES * 16), F32),
            pltpu.VMEM((HID, HID), F32),
            pltpu.VMEM((HID, WIDTH), F32),
            pltpu.VMEM((2, 96, side), F32),
            pltpu.VMEM((2, 24, side), F32),
            pltpu.VMEM((2, 2, side), F32),
            pltpu.VMEM((2, 2, side), F32),
            pltpu.VMEM((SPAN, SPAN), F32),
            pltpu.VMEM((HID, 2 * HID), F32),
            pltpu.VMEM((8, 8, 2 * HID), F32),
            pltpu.VMEM((8, 2 * HID), F32),
            pltpu.VMEM((8, 8, 2 * HID), F32),
            pltpu.VMEM((8, 2 * HID), F32),
            pltpu.VMEM((8, 8, 2 * HID), F32),
            pltpu.VMEM((8, 2 * HID), F32),
            pltpu.VMEM((8, 8, 2 * HID), F32),
            pltpu.SemaphoreType.DMA((10,)),
            pltpu.SemaphoreType.DMA((3,)),
            pltpu.SemaphoreType.DMA((4, 7)),
            pltpu.SemaphoreType.DMA((4, 7)),
            pltpu.SemaphoreType.DMA((4,)),
            pltpu.SemaphoreType.DMA((4,)),
            pltpu.SemaphoreType.DMA((4, 7)),
            pltpu.SemaphoreType.DMA((4, 7)),
        ],
        compiler_params=pltpu.CompilerParams(
            collective_id=0, has_side_effects=True, vmem_limit_bytes=60 * 1024 * 1024
        ),
    )(*args)
    outs = pl.pallas_call(
        hand_out,
        out_shape=(
            slab,
            slab,
            jax.ShapeDtypeStruct(convw.shape, F32),
            jax.ShapeDtypeStruct(mixw.shape, F32),
            jax.ShapeDtypeStruct((1, HID), F32),
        ),
        in_specs=[vmem] * 3,
        out_specs=(vmem,) * 5,
    )(final, grad, gsum)
    return outs[0], outs[1], outs[2], outs[3], outs[4].reshape(HID)


def solution(mesh):
    sizes = dict(mesh.shape)
    assert sizes == {"rep": DYHI * DCORE, "sp": DYLO * DZ * DX}
    return jax.shard_map(
        on_device,
        mesh=mesh,
        in_specs=(
            P("rep", "sp", None),
            P("rep", "sp", None),
            P("rep", "sp", None),
            P("rep", None, None),
            P("rep", "sp", None),
            P(),
            P(),
            P(),
            P(),
            P("rep", "sp", None),
        ),
        out_specs=(P("rep", "sp", None), P("rep", "sp", None), P(), P(), P()),
        check_vma=False,
    )
```

```python
import math

import jax
import jax.numpy as jnp
from jax import lax
from jax.experimental import pallas as pl
from jax.experimental.pallas import tpu as pltpu
from jax.sharding import PartitionSpec as P

BF = jnp.bfloat16
F32 = jnp.float32
MESH = pl.DeviceIdType.MESH
SPAN = 128
ROWS = 16
HALF = 8
HID = 64
CIN = 4
PIECES = 12
WIDTH = 256
NCLS = 4
GROUP = SPAN // ROWS
DX, DZ, DYLO, DYHI, DCORE = 4, 8, 4, 2, 2
TIME_STEP = 0.5


def nt(a, b):
    return lax.dot_general(a, b, (((1,), (1,)), ((), ())), preferred_element_type=F32)


def nn(a, b):
    return lax.dot_general(a, b, (((1,), (0,)), ((), ())), preferred_element_type=F32)


def split2(v):
    hi = v.astype(BF)
    return hi, (v - hi.astype(F32)).astype(BF)


def split3(v):
    hi = v.astype(BF)
    rest = v - hi.astype(F32)
    mid = rest.astype(BF)
    return hi, mid, (rest - mid.astype(F32)).astype(BF)


def mod(a, n):
    return lax.rem(a, jnp.int32(n))


def div(a, n):
    return lax.div(a, jnp.int32(n))


def shift_of(group, r):
    return r if group == 0 or r < HALF // 2 else r + HALF // 2


def row_of(group, r):
    if group == 0:
        return r + HALF // 2
    return r if r < HALF // 2 else r + HALF


def group_rows(values, group):
    quarter = HALF // 2
    if group == 0:
        return values[quarter : quarter + HALF]
    return jnp.concatenate([values[:quarter], values[quarter + HALF :]], axis=0)


def iota(shape, dim):
    return lax.broadcasted_iota(jnp.int32, shape, dim)


def onehot(cond):
    return jnp.where(cond, 1.0, 0.0).astype(BF)


def span_select(products, cls_ref, store):
    for k in range(products.shape[0] // ROWS):
        column = cls_ref[0, :, k : k + 1]
        result = products[k * ROWS : (k + 1) * ROWS, 0:SPAN]
        for group in range(1, NCLS):
            part = products[k * ROWS : (k + 1) * ROWS, group * SPAN : (group + 1) * SPAN]
            result = jnp.where(column == group, part, result)
        store(k, result)


def kernel(
    film_hbm,
    evap_hbm,
    mask_hbm,
    fcls_hbm,
    scls_hbm,
    inv_hbm,
    convw_hbm,
    mixw_hbm,
    fluxw_hbm,
    cot_hbm,
    final_hbm,
    grad_hbm,
    gsum_hbm,
    film_ref,
    evap_ref,
    mask_ref,
    fcls_ref,
    scls_ref,
    inv_ref,
    convw_ref,
    mixw_ref,
    fluxw_ref,
    cot_ref,
    final_ref,
    grad_ref,
    gsum_ref,
    invs_ref,
    recv_ref,
    mid_ref,
    halo_s,
    halo_r,
    padf_ref,
    x_ref,
    wb_ref,
    wct_ref,
    bdf_ref,
    bdb_ref,
    fwb_ref,
    fwc_ref,
    a1_ref,
    d1_ref,
    sa_ref,
    u_ref,
    v_ref,
    la_ref,
    srcf_ref,
    src_ref,
    back_ref,
    sg_ref,
    across_ref,
    cacc_ref,
    macc_ref,
    facc_ref,
    tt_ref,
    tot_ref,
    rim_s,
    rim_r,
    w36_ref,
    g_ref,
    p1_ref,
    q1_ref,
    p2_ref,
    q2_ref,
    p3_ref,
    q3_ref,
    p4_ref,
    in_sem,
    out_sem,
    ag_ssem,
    ag_rsem,
    nb_ssem,
    nb_rsem,
    ar_ssem,
    ar_rsem,
):
    inputs = [
        pltpu.make_async_copy(hbm, ref, in_sem.at[n])
        for n, (hbm, ref) in enumerate(
            (
                (cot_hbm, cot_ref),
                (inv_hbm, inv_ref),
                (scls_hbm, scls_ref),
                (film_hbm, film_ref),
                (evap_hbm, evap_ref),
                (mask_hbm, mask_ref),
                (fcls_hbm, fcls_ref),
                (convw_hbm, convw_ref),
                (mixw_hbm, mixw_ref),
                (fluxw_hbm, fluxw_ref),
            )
        )
    ]
    for copy in inputs[:3]:
        copy.start()
    side = film_ref.shape[2]
    nblocks = side // WIDTH
    sp = lax.axis_index("sp")
    rep = lax.axis_index("rep")
    nsp = DYLO * DZ * DX
    x_at = mod(sp, DX)
    z_at = mod(div(sp, DX), DZ)
    ylo_at = div(sp, DX * DZ)
    yhi_at = div(rep, DCORE)
    core_at = mod(rep, DCORE)
    y_at = yhi_at * DYLO + ylo_at
    member = mod(sp, GROUP)
    first = sp - member

    def at(r, s):
        return {"rep": r, "sp": s}

    up = mod(sp + nsp - 1, nsp)
    down = mod(sp + 1, nsp)

    def group_peer(s):
        return at(rep, first + mod(member + s, GROUP))

    j_at = core_at * DX + x_at

    def corner_peer(s):
        other = mod(j_at + s, DCORE * DX)
        return at(yhi_at * DCORE + div(other, DX), sp - x_at + mod(other, DX))

    def z_peer(s):
        return at(rep, sp + (mod(z_at + s, DZ) - z_at) * DX)

    def y_peer(s):
        other = mod(y_at + s, DYHI * DYLO)
        return at(
            div(other, DYLO) * DCORE + core_at,
            sp + (mod(other, DYLO) - ylo_at) * DX * DZ,
        )

    barrier = pltpu.get_barrier_semaphore()
    peers = [at(rep, up), at(rep, down)]
    for s in range(1, 8):
        peers += [group_peer(s), corner_peer(s), z_peer(s), y_peer(s)]
    for peer in peers:
        pl.semaphore_signal(barrier, inc=1, device_id=peer, device_id_type=MESH)
    for copy in inputs[3:]:
        copy.start()

    def remote(src, dst, ssem, rsem, peer):
        return pltpu.make_async_remote_copy(
            src_ref=src,
            dst_ref=dst,
            send_sem=ssem,
            recv_sem=rsem,
            device_id=peer,
            device_id_type=MESH,
        )

    for copy in inputs[:3]:
        copy.wait()
    inv_hi, inv_lo = split2(inv_ref[...].reshape(NCLS * SPAN, SPAN))
    for c in range(NCLS):
        of = slice(c * SPAN, (c + 1) * SPAN)
        t_hi, t_lo = split2(inv_ref[c].T)
        invs_ref[0, 0, c] = t_hi
        invs_ref[0, 1, c] = t_lo
        invs_ref[1, 0, c] = inv_hi[of]
        invs_ref[1, 1, c] = inv_lo[of]

    nspan = side // SPAN
    lines = jnp.concatenate(
        [cot_ref[0, :, k * SPAN : (k + 1) * SPAN] for k in range(nspan)], axis=0
    )
    l_hi, l_lo = split2(lines)
    right_hi = jnp.concatenate([inv_hi[c * SPAN : (c + 1) * SPAN] for c in range(NCLS)], axis=1)
    right_lo = jnp.concatenate([inv_lo[c * SPAN : (c + 1) * SPAN] for c in range(NCLS)], axis=1)
    products = nn(l_hi, right_hi) + nn(l_lo, right_hi) + nn(l_hi, right_lo)

    def store_back(k, value):
        back_ref[:, k * SPAN : (k + 1) * SPAN] = value.astype(BF)

    span_select(products, scls_ref, store_back)
    own_rows = pl.ds(pl.multiple_of(member * ROWS, ROWS), ROWS)
    chunk = side // GROUP

    def columns_of(n):
        return pl.ds(pl.multiple_of(n * chunk, chunk), chunk)

    def rows_of(n):
        return pl.ds(pl.multiple_of(n * ROWS, ROWS), ROWS)

    def span_out(which, field):
        recv_ref[which, own_rows, :] = field[:, columns_of(member)]
        for s in range(1, GROUP):
            remote(
                field.at[:, columns_of(mod(member + s, GROUP))],
                recv_ref.at[which, own_rows],
                ag_ssem.at[2 * which],
                ag_rsem.at[2 * which],
                group_peer(s),
            ).start()

    def span_solve(which, field, result):
        others = GROUP - 1
        remote(
            field.at[:, pl.ds(0, others * chunk)],
            recv_ref.at[which, pl.ds(0, others * ROWS)],
            ag_ssem.at[2 * which],
            ag_rsem.at[2 * which],
            group_peer(1),
        ).wait()
        values = recv_ref[which]
        line_cls = fcls_ref[0, :, columns_of(member)]
        own_span = iota(line_cls.shape, 0) == div(sp, GROUP)
        classes = jnp.sum(jnp.where(own_span, line_cls, 0), axis=0, keepdims=True)
        solved = None
        for c in range(NCLS):
            product = nn(invs_ref[which, 0, c], values) + nn(invs_ref[which, 1, c], values)
            solved = product if c == 0 else jnp.where(classes == c, product, solved)
        mid_ref[which] = solved.astype(BF)
        result[:, columns_of(member)] = mid_ref[which, own_rows, :]
        for s in range(1, GROUP):
            remote(
                mid_ref.at[which, rows_of(mod(member + s, GROUP))],
                result.at[:, columns_of(member)],
                ag_ssem.at[2 * which + 1],
                ag_rsem.at[2 * which + 1],
                group_peer(s),
            ).start()

    def span_in(which, result):
        others = GROUP - 1
        remote(
            mid_ref.at[which, pl.ds(0, others * ROWS)],
            result.at[:, pl.ds(0, others * chunk)],
            ag_ssem.at[2 * which + 1],
            ag_rsem.at[2 * which + 1],
            group_peer(1),
        ).wait()

    for copy in inputs[3:]:
        copy.wait()

    film = film_ref[0]
    evap = evap_ref[0]
    maskf = mask_ref[0].astype(F32)
    for c, feature in enumerate((film, film * film, maskf, evap)):
        feature = feature.astype(BF).astype(F32)
        padf_ref[c, 1 : ROWS + 1, :] = feature
        padf_ref[c, ROWS + 2 :, :] = jnp.zeros((6, side), F32)
        halo_s[0, c : c + 1, :] = feature[0:1]
        halo_s[1, c : c + 1, :] = feature[ROWS - 1 :]

    w36_ref[...] = jnp.zeros_like(w36_ref)
    for a in range(3):
        for b in range(3):
            k = (a * 3 + b) * CIN
            w36_ref[k : k + CIN, 0:HID] = convw_ref[a, b].astype(F32)
    w_t = w36_ref[...].T[:HID].astype(BF)
    k_at = iota((SPAN, WIDTH), 0)
    col = iota((SPAN, WIDTH), 1)
    piece = col // 16
    tap_row = col % 16
    wanted = (tap_row * 3 + piece % 3) * CIN + piece // 3
    pick = (k_at == wanted) & (tap_row < 3) & (piece < PIECES)
    band0 = nn(w_t, onehot(pick))
    for g in range(2):
        shifts = [shift_of(g, r) for r in range(HALF)]
        band = jnp.concatenate(
            [band0 if n == 0 else pltpu.roll(band0, n, axis=1) for n in shifts], axis=0
        )
        wb_ref[g] = band.astype(BF)
        wct_ref[g] = band[:, :SPAN].T[:96].astype(BF)
    mix = mixw_ref[...]
    tile4 = onehot(iota((HID, WIDTH), 1) % HID == iota((HID, WIDTH), 0))
    wide = nn(mix, tile4)
    tall = jnp.concatenate([wide] * 4, axis=0)
    same = iota((WIDTH, WIDTH), 0) // HID == iota((WIDTH, WIDTH), 1) // HID
    diag = jnp.where(same, tall, 0.0)
    bdb_ref[...] = diag.astype(BF)
    bdf_ref[...] = diag.T.astype(BF)
    fw = fluxw_ref[...]
    tile8 = onehot(iota((HID, HALF * HID), 1) % HID == iota((HID, HALF * HID), 0))
    fw_wide = nn(jnp.broadcast_to(fw, (16, HID)), tile8)
    own = iota((16, HALF * HID), 1) // HID == iota((16, HALF * HID), 0)
    fwb_ref[...] = jnp.where(own, fw_wide, 0.0).astype(BF)
    eye = iota((HID, HID), 0) == iota((HID, HID), 1)
    fw_col = jnp.sum(
        jnp.where(eye, jnp.broadcast_to(fw.astype(F32), (HID, HID)), 0.0), axis=1, keepdims=True
    )
    fwc_ref[...] = jnp.concatenate([jnp.broadcast_to(fw_col, (HID, WIDTH))] * 4, axis=0)

    lane = iota((24, side), 1)

    def build_pieces(g):
        for c in range(CIN):
            middle = padf_ref[c]
            left = jnp.where(lane == 0, 0.0, pltpu.roll(middle, 1, axis=1))
            right = jnp.where(lane == side - 1, 0.0, pltpu.roll(middle, side - 1, axis=1))
            for b, values in enumerate((left, middle, right)):
                s = (c * 3 + b) * 16
                if g == 0:
                    piece = values[4:20]
                else:
                    piece = jnp.concatenate([values[0:8], values[12:20]], axis=0)
                x_ref[g, s : s + 16, :] = piece.astype(BF)

    def forward(g):
        def body(i, carry):
            def cols_at(n):
                start = pl.multiple_of(i * (2 * WIDTH) + n * WIDTH, WIDTH)
                return pl.ds(start, WIDTH)

            def first_layer(n):
                cols = cols_at(n)
                t1 = jnp.tanh(nn(wb_ref[g, :, : PIECES * 16], x_ref[g, :, cols]))
                a1 = t1.astype(BF)
                a1_ref[g, :, cols] = a1
                la_ref[n] = a1
                d1_ref[n] = 1.0 - t1 * t1

            factors = {}

            def second_layer(n, q):
                of = slice(q * WIDTH, (q + 1) * WIDTH)
                cols = cols_at(n)
                t2 = jnp.tanh(nn(bdf_ref[...], la_ref[n, of, :]))
                sa_ref[g, of, cols] = t2.astype(BF)
                u = (fwc_ref[...] * (1.0 - t2 * t2)).astype(BF)
                u_ref[g, of, cols] = u
                factors[n, q] = (u, t2.astype(BF))

            def combine(n, q):
                of = slice(q * WIDTH, (q + 1) * WIDTH)
                v = d1_ref[n, of, :] * nn(bdb_ref[...], factors[n, q][0])
                v_ref[g, of, cols_at(n)] = v.astype(BF)

            def sources(n):
                cols = cols_at(n)
                sa = jnp.concatenate([factors[n, 0][1], factors[n, 1][1]], axis=0)
                flux = nn(fwb_ref[...], sa)[:HALF]
                drain = mask_ref[0, :, cols].astype(F32) * evap_ref[0, :, cols]
                rest = film_ref[0, :, cols] - TIME_STEP * drain
                source = group_rows(rest, g) + TIME_STEP * flux
                quarter = HALF // 2
                if g == 0:
                    srcf_ref[quarter : quarter + HALF, cols] = source
                else:
                    srcf_ref[0:quarter, cols] = source[:quarter]
                    srcf_ref[quarter + HALF :, cols] = source[quarter:]

            first_layer(0)
            second_layer(0, 0)
            first_layer(1)
            second_layer(0, 1)
            combine(0, 0)
            second_layer(1, 0)
            combine(0, 1)
            sources(0)
            second_layer(1, 1)
            combine(1, 0)
            combine(1, 1)
            sources(1)
            return carry

        return body

    pairs = nblocks // 2
    build_pieces(0)
    lax.fori_loop(0, 1, forward(0), 0)

    pl.semaphore_wait(barrier, len(peers))
    remote(halo_s.at[0], halo_r.at[1], nb_ssem.at[0], nb_rsem.at[0], at(rep, up)).start()
    remote(halo_s.at[1], halo_r.at[0], nb_ssem.at[0], nb_rsem.at[0], at(rep, down)).start()
    span_out(0, back_ref)

    lax.fori_loop(1, pairs, forward(0), 0)

    remote(halo_s, halo_r, nb_ssem.at[0], nb_rsem.at[0], at(rep, up)).wait()
    for c in range(CIN):
        padf_ref[c, 0:1, :] = jnp.where(sp > 0, halo_r[0, c : c + 1, :], 0.0)
        padf_ref[c, ROWS + 1 : ROWS + 2, :] = jnp.where(
            sp < nsp - 1, halo_r[1, c : c + 1, :], 0.0
        )
    build_pieces(1)
    span_solve(0, back_ref, sg_ref)
    lax.fori_loop(0, pairs, forward(1), 0)
    src_ref[...] = srcf_ref[...].astype(BF)
    span_out(1, src_ref)
    span_in(0, sg_ref)

    cacc_ref[...] = jnp.zeros_like(cacc_ref)
    macc_ref[...] = jnp.zeros_like(macc_ref)
    facc_ref[...] = jnp.zeros_like(facc_ref)

    def backward(i, carry):
        cols = pl.ds(pl.multiple_of(i * WIDTH, WIDTH), WIDTH)
        mixing = macc_ref[...]
        flux_cots = TIME_STEP * sg_ref[:, cols].astype(F32)
        for g in range(2):
            firsts = []
            for r in range(HALF):
                of = slice(r * HID, (r + 1) * HID)
                at_row = row_of(g, r)
                row = jnp.broadcast_to(flux_cots[at_row : at_row + 1], (HID, WIDTH)).astype(BF)
                mixing = mixing + nt(a1_ref[g, of, cols], u_ref[g, of, cols] * row)
                firsts.append(v_ref[g, of, cols] * row)
            pre_first = jnp.concatenate(firsts, axis=0)
            v_ref[g, :, cols] = pre_first
            cots = group_rows(flux_cots, g).astype(BF)
            facc_ref[...] += nt(cots, sa_ref[g, :, cols])
            cacc_ref[g] += nt(pre_first, x_ref[g, :, cols])
        macc_ref[...] = mixing
        return carry

    lax.fori_loop(0, nblocks, backward, 0)

    rolled = {}
    for g in range(2):
        for r in range(HALF):
            n = shift_of(g, r)
            term = cacc_ref[g, r * HID : (r + 1) * HID]
            rolled[n] = term if n not in rolled else rolled[n] + term
    taps = jnp.zeros((HID, WIDTH), F32)
    spare = jnp.zeros((HID, WIDTH - PIECES * 16), F32)
    for n, term in rolled.items():
        whole = jnp.concatenate([term, spare], axis=1)
        taps = taps + (whole if n == 0 else pltpu.roll(whole, WIDTH - n, axis=1))
    k_at = iota((HID, WIDTH), 0)
    col = iota((HID, WIDTH), 1)
    piece = col // 16
    tap_row = col % 16
    wanted = (tap_row * 3 + piece % 3) * CIN + piece // 3
    pick = onehot((k_at == wanted) & (tap_row < 3) & (piece < PIECES))
    low = jnp.zeros((HID, WIDTH), BF)
    right = jnp.zeros((HID, 2 * HID), F32)
    for t in split3(taps):
        right = right + nt(pick, jnp.concatenate([low, t], axis=0))
    tall = HALF * HID
    fold = onehot(mod(iota((tall, 2 * HID), 0), HID) + HID == iota((tall, 2 * HID), 1))
    mine = div(iota((HALF, tall), 1), HID) == iota((HALF, tall), 0)
    flux_rows = jnp.zeros((HALF, 2 * HID), F32)
    for f in split3(jnp.where(mine, facc_ref[...], 0.0)):
        flux_rows = flux_rows + nn(f, fold)
    flux_row = jnp.sum(flux_rows, axis=0, keepdims=True)
    right = right + jnp.where(iota((HID, 2 * HID), 0) == 9 * CIN, flux_row, 0.0)
    g_ref[...] = right
    g_ref[:, 0:HID] = macc_ref[...]

    own_block = pl.ds(pl.multiple_of(j_at * 8, 8), 8)
    p1_ref[j_at] = g_ref[own_block, :]
    stage1 = []
    for s in range(1, 8):
        other = mod(j_at + s, 8)
        stage1.append(
            remote(
                g_ref.at[pl.ds(pl.multiple_of(other * 8, 8), 8)],
                p1_ref.at[j_at],
                ar_ssem.at[0],
                ar_rsem.at[0],
                corner_peer(s),
            )
        )
    for copy in stage1:
        copy.start()

    span_solve(1, src_ref, across_ref)

    def features_back(i, carry):
        cols = pl.ds(pl.multiple_of(i * WIDTH, WIDTH), WIDTH)
        for h in range(2):
            tt_ref[h, :, cols] = nn(wct_ref[h], v_ref[h, :, cols])
        return carry

    lax.fori_loop(0, nblocks, features_back, 0)

    def finish(stage, slots, send_peer):
        remote(
            slots.at[pl.ds(0, 7)],
            slots.at[pl.ds(0, 7)],
            ar_ssem.at[stage],
            ar_rsem.at[stage],
            send_peer(1),
        ).wait()

    def begin(stage, slots, at_index, source, send_peer):
        for s in range(1, 8):
            remote(
                source,
                slots.at[at_index],
                ar_ssem.at[stage],
                ar_rsem.at[stage],
                send_peer(s),
            ).start()

    def summed(slots):
        total = slots[0]
        for n in range(1, 8):
            total = total + slots[n]
        return total

    finish(0, p1_ref, corner_peer)
    q1_ref[...] = summed(p1_ref)
    p2_ref[z_at] = q1_ref[...]
    begin(1, p2_ref, z_at, q1_ref, z_peer)

    lane = iota((16, side), 1)
    for c in range(2):
        parts = []
        for h in range(2):
            s = c * 48
            left = jnp.where(lane == side - 1, 0.0, pltpu.roll(tt_ref[h, s : s + 16, :], side - 1, axis=1))
            right = jnp.where(lane == 0, 0.0, pltpu.roll(tt_ref[h, s + 32 : s + 48, :], 1, axis=1))
            parts.append(left + tt_ref[h, s + 16 : s + 32, :] + right)
        tot_ref[c, 0:8, :] = parts[1][0:8]
        tot_ref[c, 8:12, :] = jnp.zeros((4, side), F32)
        tot_ref[c, 12:20, :] = parts[1][8:16]
        tot_ref[c, 4:20, :] += parts[0]
        rim_s[0, c : c + 1, :] = parts[1][0:1]
        rim_s[1, c : c + 1, :] = parts[1][13:14]
    remote(rim_s.at[0], rim_r.at[1], nb_ssem.at[1], nb_rsem.at[1], at(rep, up)).start()
    remote(rim_s.at[1], rim_r.at[0], nb_ssem.at[1], nb_rsem.at[1], at(rep, down)).start()

    span_in(1, across_ref)
    pieces = [across_ref[:, k * SPAN : (k + 1) * SPAN] for k in range(nspan)]
    lines = jnp.concatenate(pieces, axis=0)
    f_hi = invs_ref[1, 0].reshape(NCLS * SPAN, SPAN)
    f_lo = invs_ref[1, 1].reshape(NCLS * SPAN, SPAN)
    products = nt(lines, f_hi) + nt(lines, f_lo)

    def store_final(k, value):
        final_ref[0, :, k * SPAN : (k + 1) * SPAN] = value

    span_select(products, scls_ref, store_final)
    final_out = pltpu.make_async_copy(final_ref, final_hbm, out_sem.at[0])
    final_out.start()

    finish(1, p2_ref, z_peer)
    q2_ref[...] = summed(p2_ref)
    p3_ref[y_at] = q2_ref[...]
    begin(2, p3_ref, y_at, q2_ref, y_peer)

    remote(rim_s, rim_r, nb_ssem.at[1], nb_rsem.at[1], at(rep, up)).wait()
    for c in range(2):
        tot_ref[c, 1:2, :] += jnp.where(sp > 0, rim_r[0, c : c + 1, :], 0.0)
        tot_ref[c, ROWS : ROWS + 1, :] += jnp.where(sp < nsp - 1, rim_r[1, c : c + 1, :], 0.0)
    cot0 = tot_ref[0, 1 : ROWS + 1, :].astype(BF).astype(F32)
    cot1 = tot_ref[1, 1 : ROWS + 1, :].astype(BF).astype(F32)
    grad_ref[0] = sg_ref[...].astype(F32) + cot0 + 2.0 * film_ref[0] * cot1
    grad_out = pltpu.make_async_copy(grad_ref, grad_hbm, out_sem.at[1])
    grad_out.start()

    finish(2, p3_ref, y_peer)
    q3_ref[...] = summed(p3_ref)
    p4_ref[j_at] = q3_ref[...]
    begin(3, p4_ref, j_at, q3_ref, corner_peer)
    finish(3, p4_ref, corner_peer)
    scale = 1.0 / math.sqrt(DYHI * DCORE * side * side)
    gsum_ref[...] = p4_ref[...].reshape(HID, 2 * HID) * scale
    gsum_out = pltpu.make_async_copy(gsum_ref, gsum_hbm, out_sem.at[2])
    gsum_out.start()
    final_out.wait()
    grad_out.wait()
    gsum_out.wait()


def hand_out(final_in, grad_in, gsum_in, final_ref, grad_ref, convg_ref, mixg_ref, fluxg_ref):
    final_ref[...] = final_in[...]
    grad_ref[...] = grad_in[...]
    result = gsum_in[...]
    mixg_ref[...] = result[:, :HID]
    other = pltpu.roll(result, HID, axis=1)[:, :HID]
    for a in range(3):
        for b in range(3):
            k = (a * 3 + b) * CIN
            convg_ref[a, b] = other[k : k + CIN]
    fluxg_ref[...] = other[9 * CIN : 9 * CIN + 1]


def on_device(film, evap, mask, fcls, scls, inv, convw, mixw, fluxw, cot):
    side = film.shape[2]
    rows = film.shape[1]
    vmem = pl.BlockSpec(memory_space=pltpu.VMEM)
    hbm = pl.BlockSpec(memory_space=pltpu.HBM)
    free = pl.BlockSpec(memory_space=pl.ANY)
    args = (
        film,
        evap,
        mask,
        jnp.swapaxes(fcls, 1, 2),
        scls,
        inv,
        convw,
        mixw,
        fluxw.reshape(1, HID),
        cot,
    )
    args = tuple(pltpu.with_memory_space_constraint(a, pltpu.HBM) for a in args)
    chunk = side // GROUP
    tall = HALF * HID
    slab = jax.ShapeDtypeStruct(film.shape, F32)
    block = jax.ShapeDtypeStruct((HID, 2 * HID), F32)
    final, grad, gsum = pl.pallas_call(
        kernel,
        out_shape=(slab, slab, block),
        in_specs=[hbm] * 10,
        out_specs=(free,) * 3,
        scratch_shapes=[pltpu.VMEM(a.shape, a.dtype) for a in args]
        + [
            pltpu.VMEM(film.shape, F32),
            pltpu.VMEM(film.shape, F32),
            pltpu.VMEM((HID, 2 * HID), F32),
            pltpu.VMEM((2, 2, NCLS, SPAN, SPAN), BF),
            pltpu.VMEM((2, SPAN, chunk), BF),
            pltpu.VMEM((2, SPAN, chunk), BF),
            pltpu.VMEM((2, CIN, side), F32),
            pltpu.VMEM((2, CIN, side), F32),
            pltpu.VMEM((CIN, 24, side), F32),
            pltpu.VMEM((2, PIECES * 16, side), BF),
            pltpu.VMEM((2, tall, WIDTH), BF),
            pltpu.VMEM((2, 96, tall), BF),
            pltpu.VMEM((WIDTH, WIDTH), BF),
            pltpu.VMEM((WIDTH, WIDTH), BF),
            pltpu.VMEM((16, tall), BF),
            pltpu.VMEM((WIDTH, WIDTH), F32),
            pltpu.VMEM((2, tall, side), BF),
            pltpu.VMEM((2, tall, WIDTH), F32),
            pltpu.VMEM((2, tall, side), BF),
            pltpu.VMEM((2, tall, side), BF),
            pltpu.VMEM((2, tall, side), BF),
            pltpu.VMEM((2, tall, WIDTH), BF),
            pltpu.VMEM((rows, side), F32),
            pltpu.VMEM((rows, side), BF),
            pltpu.VMEM((rows, side), BF),
            pltpu.VMEM((rows, side), BF),
            pltpu.VMEM((rows, side), BF),
            pltpu.VMEM((2, tall, PIECES * 16), F32),
            pltpu.VMEM((HID, HID), F32),
            pltpu.VMEM((HALF, tall), F32),
            pltpu.VMEM((2, 96, side), F32),
            pltpu.VMEM((2, 24, side), F32),
            pltpu.VMEM((2, 2, side), F32),
            pltpu.VMEM((2, 2, side), F32),
            pltpu.VMEM((SPAN, SPAN), F32),
            pltpu.VMEM((HID, 2 * HID), F32),
            pltpu.VMEM((8, 8, 2 * HID), F32),
            pltpu.VMEM((8, 2 * HID), F32),
            pltpu.VMEM((8, 8, 2 * HID), F32),
            pltpu.VMEM((8, 2 * HID), F32),
            pltpu.VMEM((8, 8, 2 * HID), F32),
            pltpu.VMEM((8, 2 * HID), F32),
            pltpu.VMEM((8, 8, 2 * HID), F32),
            pltpu.SemaphoreType.DMA((10,)),
            pltpu.SemaphoreType.DMA((3,)),
            pltpu.SemaphoreType.DMA((4,)),
            pltpu.SemaphoreType.DMA((4,)),
            pltpu.SemaphoreType.DMA((2,)),
            pltpu.SemaphoreType.DMA((2,)),
            pltpu.SemaphoreType.DMA((4,)),
            pltpu.SemaphoreType.DMA((4,)),
        ],
        compiler_params=pltpu.CompilerParams(
            collective_id=0, has_side_effects=True, vmem_limit_bytes=48 * 1024 * 1024
        ),
    )(*args)
    outs = pl.pallas_call(
        hand_out,
        out_shape=(
            slab,
            slab,
            jax.ShapeDtypeStruct(convw.shape, F32),
            jax.ShapeDtypeStruct(mixw.shape, F32),
            jax.ShapeDtypeStruct((1, HID), F32),
        ),
        in_specs=[vmem] * 3,
        out_specs=(vmem,) * 5,
        compiler_params=pltpu.CompilerParams(vmem_limit_bytes=4 * 1024 * 1024),
    )(final, grad, gsum)
    return outs[0], outs[1], outs[2], outs[3], outs[4].reshape(HID)


def solution(mesh):
    sizes = dict(mesh.shape)
    assert sizes == {"rep": DYHI * DCORE, "sp": DYLO * DZ * DX}
    return jax.shard_map(
        on_device,
        mesh=mesh,
        in_specs=(
            P("rep", "sp", None),
            P("rep", "sp", None),
            P("rep", "sp", None),
            P("rep", None, None),
            P("rep", "sp", None),
            P(),
            P(),
            P(),
            P(),
            P("rep", "sp", None),
        ),
        out_specs=(P("rep", "sp", None), P("rep", "sp", None), P(), P(), P()),
        check_vma=False,
    )
```

```python
import math

import jax
import jax.numpy as jnp
from jax import lax
from jax.experimental import pallas as pl
from jax.experimental.pallas import tpu as pltpu
from jax.sharding import PartitionSpec as P

BF = jnp.bfloat16
F32 = jnp.float32
MESH = pl.DeviceIdType.MESH
SPAN = 128
ROWS = 16
HALF = 8
HID = 64
CIN = 4
PIECES = 12
WIDTH = 256
NCLS = 4
GROUP = SPAN // ROWS
DX, DZ, DYLO, DYHI, DCORE = 4, 8, 4, 2, 2
TIME_STEP = 0.5


def nt(a, b):
    return lax.dot_general(a, b, (((1,), (1,)), ((), ())), preferred_element_type=F32)


def nn(a, b):
    return lax.dot_general(a, b, (((1,), (0,)), ((), ())), preferred_element_type=F32)


def split2(v):
    hi = v.astype(BF)
    return hi, (v - hi.astype(F32)).astype(BF)


def split3(v):
    hi = v.astype(BF)
    rest = v - hi.astype(F32)
    mid = rest.astype(BF)
    return hi, mid, (rest - mid.astype(F32)).astype(BF)


def mod(a, n):
    return lax.rem(a, jnp.int32(n))


def div(a, n):
    return lax.div(a, jnp.int32(n))


def shift_of(group, r):
    return r if group == 0 or r < HALF // 2 else r + HALF // 2


def row_of(group, r):
    if group == 0:
        return r + HALF // 2
    return r if r < HALF // 2 else r + HALF


def group_rows(values, group):
    quarter = HALF // 2
    if group == 0:
        return values[quarter : quarter + HALF]
    return jnp.concatenate([values[:quarter], values[quarter + HALF :]], axis=0)


def iota(shape, dim):
    return lax.broadcasted_iota(jnp.int32, shape, dim)


def onehot(cond):
    return jnp.where(cond, 1.0, 0.0).astype(BF)


def span_select(products, cls_ref, store):
    for k in range(products.shape[0] // ROWS):
        column = cls_ref[0, :, k : k + 1]
        result = products[k * ROWS : (k + 1) * ROWS, 0:SPAN]
        for group in range(1, NCLS):
            part = products[k * ROWS : (k + 1) * ROWS, group * SPAN : (group + 1) * SPAN]
            result = jnp.where(column == group, part, result)
        store(k, result)


def kernel(
    film_hbm,
    evap_hbm,
    mask_hbm,
    fcls_hbm,
    scls_hbm,
    inv_hbm,
    convw_hbm,
    mixw_hbm,
    fluxw_hbm,
    cot_hbm,
    final_hbm,
    grad_hbm,
    gsum_hbm,
    film_ref,
    evap_ref,
    mask_ref,
    fcls_ref,
    scls_ref,
    inv_ref,
    convw_ref,
    mixw_ref,
    fluxw_ref,
    cot_ref,
    final_ref,
    grad_ref,
    gsum_ref,
    invs_ref,
    recv_ref,
    mid_ref,
    halo_s,
    halo_r,
    padf_ref,
    x_ref,
    wb_ref,
    wct_ref,
    bdf_ref,
    bdb_ref,
    fwb_ref,
    fwc_ref,
    a1_ref,
    d1_ref,
    sa_ref,
    u_ref,
    v_ref,
    srcf_ref,
    src_ref,
    back_ref,
    sg_ref,
    across_ref,
    cacc_ref,
    macc_ref,
    facc_ref,
    tt_ref,
    tot_ref,
    rim_s,
    rim_r,
    w36_ref,
    g_ref,
    p1_ref,
    q1_ref,
    p2_ref,
    q2_ref,
    p3_ref,
    q3_ref,
    p4_ref,
    in_sem,
    out_sem,
    ag_ssem,
    ag_rsem,
    nb_ssem,
    nb_rsem,
    ar_ssem,
    ar_rsem,
):
    inputs = [
        pltpu.make_async_copy(hbm, ref, in_sem.at[n])
        for n, (hbm, ref) in enumerate(
            (
                (convw_hbm, convw_ref),
                (mixw_hbm, mixw_ref),
                (fluxw_hbm, fluxw_ref),
                (cot_hbm, cot_ref),
                (inv_hbm, inv_ref),
                (scls_hbm, scls_ref),
                (film_hbm, film_ref),
                (evap_hbm, evap_ref),
                (mask_hbm, mask_ref),
                (fcls_hbm, fcls_ref),
            )
        )
    ]
    for copy in inputs[:6]:
        copy.start()
    side = film_ref.shape[2]
    sp = lax.axis_index("sp")
    rep = lax.axis_index("rep")
    nsp = DYLO * DZ * DX
    x_at = mod(sp, DX)
    z_at = mod(div(sp, DX), DZ)
    ylo_at = div(sp, DX * DZ)
    yhi_at = div(rep, DCORE)
    core_at = mod(rep, DCORE)
    y_at = yhi_at * DYLO + ylo_at
    member = mod(sp, GROUP)
    first = sp - member

    def at(r, s):
        return {"rep": r, "sp": s}

    def group_peer(s):
        return at(rep, first + mod(member + s, GROUP))

    j_at = core_at * DX + x_at

    def corner_peer(s):
        other = mod(j_at + s, DCORE * DX)
        return at(yhi_at * DCORE + div(other, DX), sp - x_at + mod(other, DX))

    def z_peer(s):
        return at(rep, sp + (mod(z_at + s, DZ) - z_at) * DX)

    def y_peer(s):
        other = mod(y_at + s, DYHI * DYLO)
        return at(
            div(other, DYLO) * DCORE + core_at,
            sp + (mod(other, DYLO) - ylo_at) * DX * DZ,
        )

    barrier = pltpu.get_barrier_semaphore()
    def signal(peer):
        pl.semaphore_signal(barrier, inc=1, device_id=peer, device_id_type=MESH)

    peers = [group_peer(s) for s in range(1, GROUP)]
    peers += [corner_peer(s) for s in range(1, 8)]
    peers += [z_peer(s) for s in range(1, 8)]
    peers += [y_peer(s) for s in range(1, 8)]
    has_up = sp > 0
    has_down = sp < nsp - 1
    for peer in peers:
        signal(peer)

    @pl.when(has_up)
    def _():
        signal(at(rep, sp - 1))

    @pl.when(has_down)
    def _():
        signal(at(rep, sp + 1))

    for copy in inputs[6:]:
        copy.start()

    def remote(src, dst, ssem, rsem, peer):
        return pltpu.make_async_remote_copy(
            src_ref=src,
            dst_ref=dst,
            send_sem=ssem,
            recv_sem=rsem,
            device_id=peer,
            device_id_type=MESH,
        )

    for copy in inputs[:3]:
        copy.wait()

    w36_ref[...] = jnp.zeros_like(w36_ref)
    for a in range(3):
        for b in range(3):
            k = (a * 3 + b) * CIN
            w36_ref[k : k + CIN, 0:HID] = convw_ref[a, b].astype(F32)
    w_t = w36_ref[...].T[:HID].astype(BF)
    k_at = iota((SPAN, WIDTH), 0)
    col = iota((SPAN, WIDTH), 1)
    piece = col // 16
    tap_row = col % 16
    wanted = (tap_row * 3 + piece % 3) * CIN + piece // 3
    pick = (k_at == wanted) & (tap_row < 3) & (piece < PIECES)
    band0 = nn(w_t, onehot(pick))
    for g in range(2):
        shifts = [shift_of(g, r) for r in range(HALF)]
        band = jnp.concatenate(
            [band0 if n == 0 else pltpu.roll(band0, n, axis=1) for n in shifts], axis=0
        )
        wb_ref[g] = band.astype(BF)
        wct_ref[g] = band[:, :SPAN].T[:96].astype(BF)
    mix = mixw_ref[...]
    tile4 = onehot(iota((HID, WIDTH), 1) % HID == iota((HID, WIDTH), 0))
    wide = nn(mix, tile4)
    tall = jnp.concatenate([wide] * 4, axis=0)
    same = iota((WIDTH, WIDTH), 0) // HID == iota((WIDTH, WIDTH), 1) // HID
    diag = jnp.where(same, tall, 0.0)
    bdb_ref[...] = diag.astype(BF)
    bdf_ref[...] = diag.T.astype(BF)
    fw = fluxw_ref[...]
    tile8 = onehot(iota((HID, HALF * HID), 1) % HID == iota((HID, HALF * HID), 0))
    fw_wide = nn(jnp.broadcast_to(fw, (16, HID)), tile8)
    own = iota((16, HALF * HID), 1) // HID == iota((16, HALF * HID), 0)
    fwb_ref[...] = jnp.where(own, fw_wide, 0.0).astype(BF)
    eye = iota((HID, HID), 0) == iota((HID, HID), 1)
    fw_col = jnp.sum(
        jnp.where(eye, jnp.broadcast_to(fw.astype(F32), (HID, HID)), 0.0), axis=1, keepdims=True
    )
    fwc_ref[...] = jnp.concatenate([jnp.broadcast_to(fw_col, (HID, 2 * WIDTH))] * 4, axis=0)

    for copy in inputs[3:6]:
        copy.wait()
    inv_hi, inv_lo = split2(inv_ref[...].reshape(NCLS * SPAN, SPAN))
    for c in range(NCLS):
        of = slice(c * SPAN, (c + 1) * SPAN)
        t_hi, t_lo = split2(inv_ref[c].T)
        invs_ref[0, 0, c] = t_hi
        invs_ref[0, 1, c] = t_lo
        invs_ref[1, 0, c] = inv_hi[of]
        invs_ref[1, 1, c] = inv_lo[of]

    nspan = side // SPAN
    lines = jnp.concatenate(
        [cot_ref[0, :, k * SPAN : (k + 1) * SPAN] for k in range(nspan)], axis=0
    )
    l_hi, l_lo = split2(lines)
    right_hi = jnp.concatenate([inv_hi[c * SPAN : (c + 1) * SPAN] for c in range(NCLS)], axis=1)
    right_lo = jnp.concatenate([inv_lo[c * SPAN : (c + 1) * SPAN] for c in range(NCLS)], axis=1)
    products = nn(l_hi, right_hi) + nn(l_lo, right_hi) + nn(l_hi, right_lo)

    def store_back(k, value):
        back_ref[:, k * SPAN : (k + 1) * SPAN] = value.astype(BF)

    span_select(products, scls_ref, store_back)
    own_rows = pl.ds(pl.multiple_of(member * ROWS, ROWS), ROWS)
    chunk = side // GROUP

    def columns_of(n):
        return pl.ds(pl.multiple_of(n * chunk, chunk), chunk)

    def rows_of(n):
        return pl.ds(pl.multiple_of(n * ROWS, ROWS), ROWS)

    def span_out(which, field):
        recv_ref[which, own_rows, :] = field[:, columns_of(member)]
        for s in range(1, GROUP):
            remote(
                field.at[:, columns_of(mod(member + s, GROUP))],
                recv_ref.at[which, own_rows],
                ag_ssem.at[2 * which],
                ag_rsem.at[2 * which],
                group_peer(s),
            ).start()

    def span_solve(which, field, result):
        others = GROUP - 1
        remote(
            field.at[:, pl.ds(0, others * chunk)],
            recv_ref.at[which, pl.ds(0, others * ROWS)],
            ag_ssem.at[2 * which],
            ag_rsem.at[2 * which],
            group_peer(1),
        ).wait()
        values = recv_ref[which]
        line_cls = fcls_ref[0, :, columns_of(member)]
        own_span = iota(line_cls.shape, 0) == div(sp, GROUP)
        classes = jnp.sum(jnp.where(own_span, line_cls, 0), axis=0, keepdims=True)
        solved = None
        for c in range(NCLS):
            product = nn(invs_ref[which, 0, c], values) + nn(invs_ref[which, 1, c], values)
            solved = product if c == 0 else jnp.where(classes == c, product, solved)
        mid_ref[which] = solved.astype(BF)
        result[:, columns_of(member)] = mid_ref[which, own_rows, :]
        for s in range(1, GROUP):
            remote(
                mid_ref.at[which, rows_of(mod(member + s, GROUP))],
                result.at[:, columns_of(member)],
                ag_ssem.at[2 * which + 1],
                ag_rsem.at[2 * which + 1],
                group_peer(s),
            ).start()

    def span_in(which, result):
        others = GROUP - 1
        remote(
            mid_ref.at[which, pl.ds(0, others * ROWS)],
            result.at[:, pl.ds(0, others * chunk)],
            ag_ssem.at[2 * which + 1],
            ag_rsem.at[2 * which + 1],
            group_peer(1),
        ).wait()

    for copy in inputs[6:]:
        copy.wait()

    film = film_ref[0]
    evap = evap_ref[0]
    maskf = mask_ref[0].astype(F32)
    features = [f.astype(BF).astype(F32) for f in (film, film * film, maskf, evap)]
    for c, feature in enumerate(features):
        padf_ref[c, 0:1, :] = jnp.zeros((1, side), F32)
        padf_ref[c, 1 : ROWS + 1, :] = feature
        padf_ref[c, ROWS + 1 :, :] = jnp.zeros((7, side), F32)
    halo_s[0] = jnp.concatenate([f[0:1] for f in features], axis=0).astype(BF)
    halo_s[1] = jnp.concatenate([f[ROWS - 1 :] for f in features], axis=0).astype(BF)

    def to_neighbours(n, sent, landed):
        upward = remote(
            sent.at[0], landed.at[1], nb_ssem.at[n, 0], nb_rsem.at[n, 0], at(rep, sp - 1)
        )
        downward = remote(
            sent.at[1], landed.at[0], nb_ssem.at[n, 1], nb_rsem.at[n, 1], at(rep, sp + 1)
        )
        return upward, downward

    def exchange_start(n, sent, landed):
        upward, downward = to_neighbours(n, sent, landed)

        @pl.when(has_up)
        def _():
            upward.start()

        @pl.when(has_down)
        def _():
            downward.start()

    def exchange_wait(n, sent, landed, use):
        upward, downward = to_neighbours(n, sent, landed)

        @pl.when(has_up)
        def _():
            upward.wait_send()
            downward.wait_recv()
            use(landed[0].astype(F32), 0)

        @pl.when(has_down)
        def _():
            downward.wait_send()
            upward.wait_recv()
            use(landed[1].astype(F32), ROWS + 1)

    wide = 2 * WIDTH
    lane = iota((24, side), 1)

    def build_pieces(g):
        for c in range(CIN):
            middle = padf_ref[c]
            left = jnp.where(lane == 0, 0.0, pltpu.roll(middle, 1, axis=1))
            right = jnp.where(lane == side - 1, 0.0, pltpu.roll(middle, side - 1, axis=1))
            for b, values in enumerate((left, middle, right)):
                s = (c * 3 + b) * 16
                if g == 0:
                    piece = values[4:20]
                else:
                    piece = jnp.concatenate([values[0:8], values[12:20]], axis=0)
                x_ref[g, s : s + 16, :] = piece.astype(BF)

    def forward(g):
        def body(i, carry):
            cols = pl.ds(pl.multiple_of(i * wide, wide), wide)
            factors = {}

            def rows_at(q):
                return slice(q * WIDTH, (q + 1) * WIDTH)

            def conv(q):
                return nn(wb_ref[g, rows_at(q), : PIECES * 16], x_ref[g, :, cols])

            def first_act(q, total):
                of = rows_at(q)
                t1 = jnp.tanh(total)
                a1 = t1.astype(BF)
                a1_ref[g, of, cols] = a1
                d1_ref[of, :] = 1.0 - t1 * t1
                return nn(bdf_ref[...], a1)

            def second_act(q, total):
                of = rows_at(q)
                t2 = jnp.tanh(total)
                active = t2.astype(BF)
                sa_ref[g, of, cols] = active
                u = (fwc_ref[...] * (1.0 - t2 * t2)).astype(BF)
                u_ref[g, of, cols] = u
                factors[q] = (u, active)
                return nn(bdb_ref[...], u)

            def combine(q, total):
                of = rows_at(q)
                v_ref[g, of, cols] = (d1_ref[of, :] * total).astype(BF)

            def sources():
                sa = jnp.concatenate([factors[0][1], factors[1][1]], axis=0)
                flux = nn(fwb_ref[...], sa)[:HALF]
                drain = mask_ref[0, :, cols].astype(F32) * evap_ref[0, :, cols]
                rest = film_ref[0, :, cols] - TIME_STEP * drain
                source = group_rows(rest, g) + TIME_STEP * flux
                quarter = HALF // 2
                if g == 0:
                    srcf_ref[quarter : quarter + HALF, cols] = source
                else:
                    srcf_ref[0:quarter, cols] = source[:quarter]
                    srcf_ref[quarter + HALF :, cols] = source[quarter:]

            one0 = conv(0)
            one1 = conv(1)
            two0 = first_act(0, one0)
            two1 = first_act(1, one1)
            three0 = second_act(0, two0)
            three1 = second_act(1, two1)
            combine(0, three0)
            sources()
            combine(1, three1)
            return carry

        return body

    pairs = side // wide
    build_pieces(0)
    lax.fori_loop(0, 1, forward(0), 0)

    neighbours = jnp.where(has_up, 1, 0) + jnp.where(has_down, 1, 0)
    pl.semaphore_wait(barrier, len(peers) + neighbours)
    exchange_start(0, halo_s, halo_r)
    span_out(0, back_ref)

    lax.fori_loop(1, pairs, forward(0), 0)

    def set_rim(values, row):
        for c in range(CIN):
            padf_ref[c, row : row + 1, :] = values[c : c + 1]

    exchange_wait(0, halo_s, halo_r, set_rim)
    build_pieces(1)
    span_solve(0, back_ref, sg_ref)
    lax.fori_loop(0, pairs, forward(1), 0)
    src_ref[...] = srcf_ref[...].astype(BF)
    span_out(1, src_ref)
    span_in(0, sg_ref)

    cacc_ref[...] = jnp.zeros_like(cacc_ref)
    macc_ref[...] = jnp.zeros_like(macc_ref)
    facc_ref[...] = jnp.zeros_like(facc_ref)

    def add_products(g, q, mixing, taps):
        macc_ref[q] += mixing
        cacc_ref[g, q * WIDTH : (q + 1) * WIDTH, :] += taps

    def backward(i, carry):
        cols = pl.ds(pl.multiple_of(i * wide, wide), wide)
        flux_cots = TIME_STEP * sg_ref[:, cols].astype(F32)
        products = []
        for g in range(2):
            for q in range(2):
                of = slice(q * WIDTH, (q + 1) * WIDTH)
                rows = jnp.concatenate(
                    [
                        jnp.broadcast_to(flux_cots[n : n + 1], (HID, wide)).astype(BF)
                        for n in [row_of(g, 4 * q + r) for r in range(4)]
                    ],
                    axis=0,
                )
                pre_first = v_ref[g, of, cols] * rows
                v_ref[g, of, cols] = pre_first
                mixing = nt(a1_ref[g, of, cols], u_ref[g, of, cols] * rows)
                taps = nt(pre_first, x_ref[g, :, cols])
                products.append((g, q, mixing, taps))
                if len(products) > 1:
                    add_products(*products[-2])
            cots = group_rows(flux_cots, g).astype(BF)
            facc_ref[...] += nt(cots, sa_ref[g, :, cols])
        add_products(*products[-1])
        return carry

    lax.fori_loop(0, side // wide, backward, 0)

    rolled = {}
    for g in range(2):
        for r in range(HALF):
            n = shift_of(g, r)
            term = cacc_ref[g, r * HID : (r + 1) * HID]
            rolled[n] = term if n not in rolled else rolled[n] + term
    taps = jnp.zeros((HID, WIDTH), F32)
    spare = jnp.zeros((HID, WIDTH - PIECES * 16), F32)
    for n, term in rolled.items():
        whole = jnp.concatenate([term, spare], axis=1)
        taps = taps + (whole if n == 0 else pltpu.roll(whole, WIDTH - n, axis=1))
    k_at = iota((HID, WIDTH), 0)
    col = iota((HID, WIDTH), 1)
    piece = col // 16
    tap_row = col % 16
    wanted = (tap_row * 3 + piece % 3) * CIN + piece // 3
    pick = onehot((k_at == wanted) & (tap_row < 3) & (piece < PIECES))
    low = jnp.zeros((HID, WIDTH), BF)
    right = jnp.zeros((HID, 2 * HID), F32)
    for t in split3(taps):
        right = right + nt(pick, jnp.concatenate([low, t], axis=0))
    tall = HALF * HID
    fold = onehot(mod(iota((tall, 2 * HID), 0), HID) + HID == iota((tall, 2 * HID), 1))
    mine = div(iota((HALF, tall), 1), HID) == iota((HALF, tall), 0)
    flux_rows = jnp.zeros((HALF, 2 * HID), F32)
    for f in split3(jnp.where(mine, facc_ref[...], 0.0)):
        flux_rows = flux_rows + nn(f, fold)
    flux_row = jnp.sum(flux_rows, axis=0, keepdims=True)
    right = right + jnp.where(iota((HID, 2 * HID), 0) == 9 * CIN, flux_row, 0.0)
    g_ref[...] = right
    blocks = []
    for r in range(4):
        of, at_span = slice(r * HID, (r + 1) * HID), slice((r // 2) * SPAN, (r // 2 + 1) * SPAN)
        blocks.append(macc_ref[0, of, at_span] + macc_ref[1, of, at_span])
    mixing = blocks[0] + blocks[2] + pltpu.roll(blocks[1] + blocks[3], HID, axis=1)
    g_ref[:, 0:HID] = mixing[:, 0:HID]

    own_block = pl.ds(pl.multiple_of(j_at * 8, 8), 8)
    p1_ref[j_at] = g_ref[own_block, :]
    stage1 = []
    for s in range(1, 8):
        other = mod(j_at + s, 8)
        stage1.append(
            remote(
                g_ref.at[pl.ds(pl.multiple_of(other * 8, 8), 8)],
                p1_ref.at[j_at],
                ar_ssem.at[0],
                ar_rsem.at[0],
                corner_peer(s),
            )
        )
    for copy in stage1:
        copy.start()

    span_solve(1, src_ref, across_ref)

    def features_back(i, carry):
        cols = pl.ds(pl.multiple_of(i * wide, wide), wide)
        for h in range(2):
            tt_ref[h, :, cols] = nn(wct_ref[h], v_ref[h, :, cols])
        return carry

    lax.fori_loop(0, side // wide, features_back, 0)

    def finish(stage, slots, send_peer):
        remote(
            slots.at[pl.ds(0, 7)],
            slots.at[pl.ds(0, 7)],
            ar_ssem.at[stage],
            ar_rsem.at[stage],
            send_peer(1),
        ).wait()

    def begin(stage, slots, at_index, source, send_peer):
        for s in range(1, 8):
            remote(
                source,
                slots.at[at_index],
                ar_ssem.at[stage],
                ar_rsem.at[stage],
                send_peer(s),
            ).start()

    def summed(slots):
        total = slots[0]
        for n in range(1, 8):
            total = total + slots[n]
        return total

    finish(0, p1_ref, corner_peer)
    q1_ref[...] = summed(p1_ref)
    p2_ref[z_at] = q1_ref[...]
    begin(1, p2_ref, z_at, q1_ref, z_peer)

    lane = iota((16, side), 1)
    for c in range(2):
        parts = []
        for h in range(2):
            s = c * 48
            left = jnp.where(lane == side - 1, 0.0, pltpu.roll(tt_ref[h, s : s + 16, :], side - 1, axis=1))
            right = jnp.where(lane == 0, 0.0, pltpu.roll(tt_ref[h, s + 32 : s + 48, :], 1, axis=1))
            parts.append(left + tt_ref[h, s + 16 : s + 32, :] + right)
        tot_ref[c, 0:8, :] = parts[1][0:8]
        tot_ref[c, 8:12, :] = jnp.zeros((4, side), F32)
        tot_ref[c, 12:20, :] = parts[1][8:16]
        tot_ref[c, 4:20, :] += parts[0]
        rim_s[0, c : c + 1, :] = parts[1][0:1]
        rim_s[1, c : c + 1, :] = parts[1][13:14]
    exchange_start(1, rim_s, rim_r)

    span_in(1, across_ref)
    pieces = [across_ref[:, k * SPAN : (k + 1) * SPAN] for k in range(nspan)]
    lines = jnp.concatenate(pieces, axis=0)
    f_hi = invs_ref[1, 0].reshape(NCLS * SPAN, SPAN)
    f_lo = invs_ref[1, 1].reshape(NCLS * SPAN, SPAN)
    products = nt(lines, f_hi) + nt(lines, f_lo)

    def store_final(k, value):
        final_ref[0, :, k * SPAN : (k + 1) * SPAN] = value

    span_select(products, scls_ref, store_final)
    final_out = pltpu.make_async_copy(final_ref, final_hbm, out_sem.at[0])
    final_out.start()

    finish(1, p2_ref, z_peer)
    q2_ref[...] = summed(p2_ref)
    p3_ref[y_at] = q2_ref[...]
    begin(2, p3_ref, y_at, q2_ref, y_peer)

    def add_rim(values, row):
        for c in range(2):
            at_row = 1 if row == 0 else ROWS
            tot_ref[c, at_row : at_row + 1, :] += values[c : c + 1]

    exchange_wait(1, rim_s, rim_r, add_rim)
    cot0 = tot_ref[0, 1 : ROWS + 1, :].astype(BF).astype(F32)
    cot1 = tot_ref[1, 1 : ROWS + 1, :].astype(BF).astype(F32)
    grad_ref[0] = sg_ref[...].astype(F32) + cot0 + 2.0 * film_ref[0] * cot1
    grad_out = pltpu.make_async_copy(grad_ref, grad_hbm, out_sem.at[1])
    grad_out.start()

    finish(2, p3_ref, y_peer)
    q3_ref[...] = summed(p3_ref)
    p4_ref[j_at] = q3_ref[...]
    begin(3, p4_ref, j_at, q3_ref, corner_peer)
    finish(3, p4_ref, corner_peer)
    scale = 1.0 / math.sqrt(DYHI * DCORE * side * side)
    gsum_ref[...] = p4_ref[...].reshape(HID, 2 * HID) * scale
    gsum_out = pltpu.make_async_copy(gsum_ref, gsum_hbm, out_sem.at[2])
    gsum_out.start()
    final_out.wait()
    grad_out.wait()
    gsum_out.wait()


def hand_out(final_in, grad_in, gsum_in, final_ref, grad_ref, convg_ref, mixg_ref, fluxg_ref):
    final_ref[...] = final_in[...]
    grad_ref[...] = grad_in[...]
    result = gsum_in[...]
    mixg_ref[...] = result[:, :HID]
    other = pltpu.roll(result, HID, axis=1)[:, :HID]
    for a in range(3):
        for b in range(3):
            k = (a * 3 + b) * CIN
            convg_ref[a, b] = other[k : k + CIN]
    fluxg_ref[...] = other[9 * CIN : 9 * CIN + 1]


def on_device(film, evap, mask, fcls, scls, inv, convw, mixw, fluxw, cot):
    side = film.shape[2]
    rows = film.shape[1]
    vmem = pl.BlockSpec(memory_space=pltpu.VMEM)
    hbm = pl.BlockSpec(memory_space=pltpu.HBM)
    free = pl.BlockSpec(memory_space=pl.ANY)
    args = (
        film,
        evap,
        mask,
        jnp.swapaxes(fcls, 1, 2),
        scls,
        inv,
        convw,
        mixw,
        fluxw.reshape(1, HID),
        cot,
    )
    args = tuple(pltpu.with_memory_space_constraint(a, pltpu.HBM) for a in args)
    chunk = side // GROUP
    tall = HALF * HID
    slab = jax.ShapeDtypeStruct(film.shape, F32)
    block = jax.ShapeDtypeStruct((HID, 2 * HID), F32)
    final, grad, gsum = pl.pallas_call(
        kernel,
        out_shape=(slab, slab, block),
        in_specs=[hbm] * 10,
        out_specs=(free,) * 3,
        scratch_shapes=[pltpu.VMEM(a.shape, a.dtype) for a in args]
        + [
            pltpu.VMEM(film.shape, F32),
            pltpu.VMEM(film.shape, F32),
            pltpu.VMEM((HID, 2 * HID), F32),
            pltpu.VMEM((2, 2, NCLS, SPAN, SPAN), BF),
            pltpu.VMEM((2, SPAN, chunk), BF),
            pltpu.VMEM((2, SPAN, chunk), BF),
            pltpu.VMEM((2, CIN, side), BF),
            pltpu.VMEM((2, CIN, side), BF),
            pltpu.VMEM((CIN, 24, side), F32),
            pltpu.VMEM((2, PIECES * 16, side), BF),
            pltpu.VMEM((2, tall, WIDTH), BF),
            pltpu.VMEM((2, 96, tall), BF),
            pltpu.VMEM((WIDTH, WIDTH), BF),
            pltpu.VMEM((WIDTH, WIDTH), BF),
            pltpu.VMEM((16, tall), BF),
            pltpu.VMEM((WIDTH, 2 * WIDTH), F32),
            pltpu.VMEM((2, tall, side), BF),
            pltpu.VMEM((tall, 2 * WIDTH), F32),
            pltpu.VMEM((2, tall, side), BF),
            pltpu.VMEM((2, tall, side), BF),
            pltpu.VMEM((2, tall, side), BF),
            pltpu.VMEM((rows, side), F32),
            pltpu.VMEM((rows, side), BF),
            pltpu.VMEM((rows, side), BF),
            pltpu.VMEM((rows, side), BF),
            pltpu.VMEM((rows, side), BF),
            pltpu.VMEM((2, tall, PIECES * 16), F32),
            pltpu.VMEM((2, WIDTH, WIDTH), F32),
            pltpu.VMEM((HALF, tall), F32),
            pltpu.VMEM((2, 96, side), F32),
            pltpu.VMEM((2, 24, side), F32),
            pltpu.VMEM((2, 2, side), F32),
            pltpu.VMEM((2, 2, side), F32),
            pltpu.VMEM((SPAN, SPAN), F32),
            pltpu.VMEM((HID, 2 * HID), F32),
            pltpu.VMEM((8, 8, 2 * HID), F32),
            pltpu.VMEM((8, 2 * HID), F32),
            pltpu.VMEM((8, 8, 2 * HID), F32),
            pltpu.VMEM((8, 2 * HID), F32),
            pltpu.VMEM((8, 8, 2 * HID), F32),
            pltpu.VMEM((8, 2 * HID), F32),
            pltpu.VMEM((8, 8, 2 * HID), F32),
            pltpu.SemaphoreType.DMA((10,)),
            pltpu.SemaphoreType.DMA((3,)),
            pltpu.SemaphoreType.DMA((4,)),
            pltpu.SemaphoreType.DMA((4,)),
            pltpu.SemaphoreType.DMA((2, 2)),
            pltpu.SemaphoreType.DMA((2, 2)),
            pltpu.SemaphoreType.DMA((4,)),
            pltpu.SemaphoreType.DMA((4,)),
        ],
        compiler_params=pltpu.CompilerParams(
            collective_id=0, has_side_effects=True, vmem_limit_bytes=48 * 1024 * 1024
        ),
    )(*args)
    outs = pl.pallas_call(
        hand_out,
        out_shape=(
            slab,
            slab,
            jax.ShapeDtypeStruct(convw.shape, F32),
            jax.ShapeDtypeStruct(mixw.shape, F32),
            jax.ShapeDtypeStruct((1, HID), F32),
        ),
        in_specs=[vmem] * 3,
        out_specs=(vmem,) * 5,
        compiler_params=pltpu.CompilerParams(vmem_limit_bytes=4 * 1024 * 1024),
    )(final, grad, gsum)
    return outs[0], outs[1], outs[2], outs[3], outs[4].reshape(HID)


def solution(mesh):
    sizes = dict(mesh.shape)
    assert sizes == {"rep": DYHI * DCORE, "sp": DYLO * DZ * DX}
    return jax.shard_map(
        on_device,
        mesh=mesh,
        in_specs=(
            P("rep", "sp", None),
            P("rep", "sp", None),
            P("rep", "sp", None),
            P("rep", None, None),
            P("rep", "sp", None),
            P(),
            P(),
            P(),
            P(),
            P("rep", "sp", None),
        ),
        out_specs=(P("rep", "sp", None), P("rep", "sp", None), P(), P(), P()),
        check_vma=False,
    )
```

```python
import math

import jax
import jax.numpy as jnp
from jax import lax
from jax.experimental import pallas as pl
from jax.experimental.pallas import tpu as pltpu
from jax.sharding import PartitionSpec as P

BF = jnp.bfloat16
F32 = jnp.float32
MESH = pl.DeviceIdType.MESH
SPAN = 128
ROWS = 16
HID = 64
CIN = 4
PIECES = 12
WIDTH = 256
NCLS = 4
GROUP = SPAN // ROWS
DX, DZ, DYLO, DYHI, DCORE = 4, 8, 4, 2, 2
TIME_STEP = 0.5


def nt(a, b):
    return lax.dot_general(a, b, (((1,), (1,)), ((), ())), preferred_element_type=F32)


def nn(a, b):
    return lax.dot_general(a, b, (((1,), (0,)), ((), ())), preferred_element_type=F32)


def split2(v):
    hi = v.astype(BF)
    return hi, (v - hi.astype(F32)).astype(BF)


def split3(v):
    hi = v.astype(BF)
    rest = v - hi.astype(F32)
    mid = rest.astype(BF)
    return hi, mid, (rest - mid.astype(F32)).astype(BF)


def mod(a, n):
    return lax.rem(a, jnp.int32(n))


def div(a, n):
    return lax.div(a, jnp.int32(n))


EDGE = 2
ORDER = list(range(EDGE, ROWS - EDGE)) + [0, 1, ROWS - 2, ROWS - 1]
SHIFTS = list(range(ROWS - 2 * EDGE)) + [0, 1, 8, 9]
CHUNKS = ((0, 1, 2), (3,))
COUNTS = (ROWS - 2 * EDGE, 2 * EDGE)


def group_of(m):
    return 0 if m in CHUNKS[0] else 1


def chunk_rows(m):
    return slice(m * WIDTH, (m + 1) * WIDTH)


def group_part(g):
    return slice(CHUNKS[g][0] * WIDTH, (CHUNKS[g][-1] + 1) * WIDTH)


def group_rows(values, group):
    if group == 0:
        return values[EDGE : ROWS - EDGE]
    return jnp.concatenate([values[:EDGE], values[ROWS - EDGE :]], axis=0)


def iota(shape, dim):
    return lax.broadcasted_iota(jnp.int32, shape, dim)


def onehot(cond):
    return jnp.where(cond, 1.0, 0.0).astype(BF)


def span_select(products, cls_ref, store):
    for k in range(products.shape[0] // ROWS):
        column = cls_ref[0, :, k : k + 1]
        result = products[k * ROWS : (k + 1) * ROWS, 0:SPAN]
        for group in range(1, NCLS):
            part = products[k * ROWS : (k + 1) * ROWS, group * SPAN : (group + 1) * SPAN]
            result = jnp.where(column == group, part, result)
        store(k, result)


def kernel(
    film_hbm,
    evap_hbm,
    mask_hbm,
    fcls_hbm,
    scls_hbm,
    inv_hbm,
    convw_hbm,
    mixw_hbm,
    fluxw_hbm,
    cot_hbm,
    final_hbm,
    grad_hbm,
    gsum_hbm,
    film_ref,
    evap_ref,
    mask_ref,
    fcls_ref,
    scls_ref,
    inv_ref,
    convw_ref,
    mixw_ref,
    fluxw_ref,
    cot_ref,
    final_ref,
    grad_ref,
    gsum_ref,
    invs_ref,
    recv_ref,
    mid_ref,
    halo_s,
    halo_r,
    padf_ref,
    x_ref,
    wb_ref,
    wct_ref,
    bdf_ref,
    bdb_ref,
    fwb_ref,
    fwc_ref,
    a1_ref,
    d1_ref,
    sa_ref,
    u_ref,
    v_ref,
    srcf_ref,
    src_ref,
    back_ref,
    sg_ref,
    across_ref,
    cacc_ref,
    macc_ref,
    facc_ref,
    tt_ref,
    tot_ref,
    rim_s,
    rim_r,
    w36_ref,
    g_ref,
    p1_ref,
    q1_ref,
    p2_ref,
    q2_ref,
    p3_ref,
    q3_ref,
    p4_ref,
    in_sem,
    out_sem,
    ag_ssem,
    ag_rsem,
    nb_ssem,
    nb_rsem,
    ar_ssem,
    ar_rsem,
    far_sem,
):
    inputs = [
        pltpu.make_async_copy(hbm, ref, in_sem.at[n])
        for n, (hbm, ref) in enumerate(
            (
                (convw_hbm, convw_ref),
                (mixw_hbm, mixw_ref),
                (fluxw_hbm, fluxw_ref),
                (cot_hbm, cot_ref),
                (inv_hbm, inv_ref),
                (scls_hbm, scls_ref),
                (film_hbm, film_ref),
                (evap_hbm, evap_ref),
                (mask_hbm, mask_ref),
                (fcls_hbm, fcls_ref),
            )
        )
    ]
    for copy in inputs[:6]:
        copy.start()
    side = film_ref.shape[2]
    sp = lax.axis_index("sp")
    rep = lax.axis_index("rep")
    nsp = DYLO * DZ * DX
    x_at = mod(sp, DX)
    z_at = mod(div(sp, DX), DZ)
    ylo_at = div(sp, DX * DZ)
    yhi_at = div(rep, DCORE)
    core_at = mod(rep, DCORE)
    y_at = yhi_at * DYLO + ylo_at
    member = mod(sp, GROUP)
    first = sp - member

    def at(r, s):
        return {"rep": r, "sp": s}

    def group_peer(s):
        return at(rep, first + mod(member + s, GROUP))

    j_at = core_at * DX + x_at

    def corner_peer(s):
        other = mod(j_at + s, DCORE * DX)
        return at(yhi_at * DCORE + div(other, DX), sp - x_at + mod(other, DX))

    def z_peer(s):
        return at(rep, sp + (mod(z_at + s, DZ) - z_at) * DX)

    def y_peer(s):
        other = mod(y_at + s, DYHI * DYLO)
        return at(
            div(other, DYLO) * DCORE + core_at,
            sp + (mod(other, DYLO) - ylo_at) * DX * DZ,
        )

    barrier = pltpu.get_barrier_semaphore()
    def signal(peer):
        pl.semaphore_signal(barrier, inc=1, device_id=peer, device_id_type=MESH)

    peers = [group_peer(s) for s in range(1, GROUP)]
    peers += [corner_peer(s) for s in range(1, 8)]
    beside = [z_peer(1), z_peer(7), y_peer(1), y_peer(7)]
    peers += beside
    has_up = sp > 0
    has_down = sp < nsp - 1
    for peer in peers:
        signal(peer)

    @pl.when(has_up)
    def _():
        signal(at(rep, sp - 1))

    @pl.when(has_down)
    def _():
        signal(at(rep, sp + 1))

    for copy in inputs[6:]:
        copy.start()

    def remote(src, dst, ssem, rsem, peer):
        return pltpu.make_async_remote_copy(
            src_ref=src,
            dst_ref=dst,
            send_sem=ssem,
            recv_sem=rsem,
            device_id=peer,
            device_id_type=MESH,
        )

    for copy in inputs[:3]:
        copy.wait()

    w36_ref[...] = jnp.zeros_like(w36_ref)
    for a in range(3):
        for b in range(3):
            k = (a * 3 + b) * CIN
            w36_ref[k : k + CIN, 0:HID] = convw_ref[a, b].astype(F32)
    w_t = w36_ref[...].T[:HID].astype(BF)
    k_at = iota((SPAN, WIDTH), 0)
    col = iota((SPAN, WIDTH), 1)
    piece = col // 16
    tap_row = col % 16
    wanted = (tap_row * 3 + piece % 3) * CIN + piece // 3
    pick = (k_at == wanted) & (tap_row < 3) & (piece < PIECES)
    band0 = nn(w_t, onehot(pick))
    rolls = [band0 if n == 0 else pltpu.roll(band0, n, axis=1) for n in range(max(SHIFTS) + 1)]
    for m in range(4):
        band = jnp.concatenate([rolls[n] for n in SHIFTS[4 * m : 4 * m + 4]], axis=0)
        wb_ref[chunk_rows(m), :] = band.astype(BF)
        wct_ref[:, chunk_rows(m)] = band[:, :SPAN].T[:96].astype(BF)
    mix = mixw_ref[...]
    tile4 = onehot(iota((HID, WIDTH), 1) % HID == iota((HID, WIDTH), 0))
    wide = nn(mix, tile4)
    tall = jnp.concatenate([wide] * 4, axis=0)
    same = iota((WIDTH, WIDTH), 0) // HID == iota((WIDTH, WIDTH), 1) // HID
    diag = jnp.where(same, tall, 0.0)
    bdb_ref[...] = diag.astype(BF)
    bdf_ref[...] = diag.T.astype(BF)
    fw = fluxw_ref[...]
    tile8 = onehot(mod(iota((HID, 3 * WIDTH), 1), HID) == iota((HID, 3 * WIDTH), 0))
    fw_wide = nn(jnp.broadcast_to(fw, (16, HID)), tile8)
    own = div(iota((16, 3 * WIDTH), 1), HID) == iota((16, 3 * WIDTH), 0)
    fwb_ref[...] = jnp.where(own, fw_wide, 0.0).astype(BF)
    eye = iota((HID, HID), 0) == iota((HID, HID), 1)
    fw_col = jnp.sum(
        jnp.where(eye, jnp.broadcast_to(fw.astype(F32), (HID, HID)), 0.0), axis=1, keepdims=True
    )
    fwc_ref[...] = jnp.concatenate([jnp.broadcast_to(fw_col, (HID, 2 * WIDTH))] * 4, axis=0)

    for copy in inputs[3:6]:
        copy.wait()
    inv_hi, inv_lo = split2(inv_ref[...].reshape(NCLS * SPAN, SPAN))
    for c in range(NCLS):
        of = slice(c * SPAN, (c + 1) * SPAN)
        t_hi, t_lo = split2(inv_ref[c].T)
        invs_ref[0, 0, c] = t_hi
        invs_ref[0, 1, c] = t_lo
        invs_ref[1, 0, c] = inv_hi[of]
        invs_ref[1, 1, c] = inv_lo[of]

    nspan = side // SPAN
    lines = jnp.concatenate(
        [cot_ref[0, :, k * SPAN : (k + 1) * SPAN] for k in range(nspan)], axis=0
    )
    l_hi, l_lo = split2(lines)
    right_hi = jnp.concatenate([inv_hi[c * SPAN : (c + 1) * SPAN] for c in range(NCLS)], axis=1)
    right_lo = jnp.concatenate([inv_lo[c * SPAN : (c + 1) * SPAN] for c in range(NCLS)], axis=1)
    products = nn(l_hi, right_hi) + nn(l_lo, right_hi) + nn(l_hi, right_lo)

    def store_back(k, value):
        back_ref[:, k * SPAN : (k + 1) * SPAN] = value.astype(BF)

    span_select(products, scls_ref, store_back)
    own_rows = pl.ds(pl.multiple_of(member * ROWS, ROWS), ROWS)
    chunk = side // GROUP

    def columns_of(n):
        return pl.ds(pl.multiple_of(n * chunk, chunk), chunk)

    def rows_of(n):
        return pl.ds(pl.multiple_of(n * ROWS, ROWS), ROWS)

    def span_out(which, field):
        recv_ref[which, own_rows, :] = field[:, columns_of(member)]
        for s in range(1, GROUP):
            remote(
                field.at[:, columns_of(mod(member + s, GROUP))],
                recv_ref.at[which, own_rows],
                ag_ssem.at[2 * which],
                ag_rsem.at[2 * which],
                group_peer(s),
            ).start()

    def span_solve(which, field, result):
        others = GROUP - 1
        remote(
            field.at[:, pl.ds(0, others * chunk)],
            recv_ref.at[which, pl.ds(0, others * ROWS)],
            ag_ssem.at[2 * which],
            ag_rsem.at[2 * which],
            group_peer(1),
        ).wait()
        values = recv_ref[which]
        line_cls = fcls_ref[0, :, columns_of(member)]
        own_span = iota(line_cls.shape, 0) == div(sp, GROUP)
        classes = jnp.sum(jnp.where(own_span, line_cls, 0), axis=0, keepdims=True)
        solved = None
        for c in range(NCLS):
            product = nn(invs_ref[which, 0, c], values) + nn(invs_ref[which, 1, c], values)
            solved = product if c == 0 else jnp.where(classes == c, product, solved)
        mid_ref[which] = solved.astype(BF)
        result[:, columns_of(member)] = mid_ref[which, own_rows, :]
        for s in range(1, GROUP):
            remote(
                mid_ref.at[which, rows_of(mod(member + s, GROUP))],
                result.at[:, columns_of(member)],
                ag_ssem.at[2 * which + 1],
                ag_rsem.at[2 * which + 1],
                group_peer(s),
            ).start()

    def span_in(which, result):
        others = GROUP - 1
        remote(
            mid_ref.at[which, pl.ds(0, others * ROWS)],
            result.at[:, pl.ds(0, others * chunk)],
            ag_ssem.at[2 * which + 1],
            ag_rsem.at[2 * which + 1],
            group_peer(1),
        ).wait()

    for copy in inputs[6:]:
        copy.wait()

    film = film_ref[0]
    evap = evap_ref[0]
    maskf = mask_ref[0].astype(F32)
    features = [f.astype(BF).astype(F32) for f in (film, film * film, maskf, evap)]
    for c, feature in enumerate(features):
        padf_ref[c, 0:1, :] = jnp.zeros((1, side), F32)
        padf_ref[c, 1 : ROWS + 1, :] = feature
        padf_ref[c, ROWS + 1 :, :] = jnp.zeros((7, side), F32)
    halo_s[0] = jnp.concatenate([f[0:1] for f in features], axis=0).astype(BF)
    halo_s[1] = jnp.concatenate([f[ROWS - 1 :] for f in features], axis=0).astype(BF)

    def to_neighbours(n, sent, landed):
        upward = remote(
            sent.at[0], landed.at[1], nb_ssem.at[n, 0], nb_rsem.at[n, 0], at(rep, sp - 1)
        )
        downward = remote(
            sent.at[1], landed.at[0], nb_ssem.at[n, 1], nb_rsem.at[n, 1], at(rep, sp + 1)
        )
        return upward, downward

    def exchange_start(n, sent, landed):
        upward, downward = to_neighbours(n, sent, landed)

        @pl.when(has_up)
        def _():
            upward.start()

        @pl.when(has_down)
        def _():
            downward.start()

    def exchange_wait(n, sent, landed, use):
        upward, downward = to_neighbours(n, sent, landed)

        @pl.when(has_up)
        def _():
            upward.wait_send()
            downward.wait_recv()
            use(landed[0].astype(F32), 0)

        @pl.when(has_down)
        def _():
            downward.wait_send()
            upward.wait_recv()
            use(landed[1].astype(F32), ROWS + 1)

    wide = 2 * WIDTH
    lane = iota((24, side), 1)

    def build_pieces(g):
        for c in range(CIN):
            middle = padf_ref[c]
            left = jnp.where(lane == 0, 0.0, pltpu.roll(middle, 1, axis=1))
            right = jnp.where(lane == side - 1, 0.0, pltpu.roll(middle, side - 1, axis=1))
            for b, values in enumerate((left, middle, right)):
                s = (c * 3 + b) * 16
                if g == 0:
                    piece = values[EDGE : EDGE + 16]
                else:
                    piece = jnp.concatenate([values[0:8], values[14:22]], axis=0)
                x_ref[g, s : s + 16, :] = piece.astype(BF)

    def forward(g, blocks):
        units = [(m, n) for n in range(blocks) for m in CHUNKS[g]]

        def body(i, carry):
            factors = {}

            def cols_at(n):
                return pl.ds(pl.multiple_of((i * blocks + n) * wide, wide), wide)

            def conv(m, n):
                return nn(wb_ref[chunk_rows(m), : PIECES * 16], x_ref[g, :, cols_at(n)])

            def first_act(m, n, total):
                t1 = jnp.tanh(total)
                a1 = t1.astype(BF)
                a1_ref[chunk_rows(m), cols_at(n)] = a1
                d1_ref[units.index((m, n))] = 1.0 - t1 * t1
                return nn(bdf_ref[...], a1)

            def second_act(m, n, total):
                t2 = jnp.tanh(total)
                active = t2.astype(BF)
                sa_ref[chunk_rows(m), cols_at(n)] = active
                u = (fwc_ref[...] * (1.0 - t2 * t2)).astype(BF)
                u_ref[chunk_rows(m), cols_at(n)] = u
                factors[m, n] = active
                return nn(bdb_ref[...], u)

            def combine(m, n, total):
                v = d1_ref[units.index((m, n))] * total
                v_ref[chunk_rows(m), cols_at(n)] = v.astype(BF)

            def sources(n):
                cols = cols_at(n)
                sa = jnp.concatenate([factors[m, n] for m in CHUNKS[g]], axis=0)
                flux = nn(fwb_ref[:, : sa.shape[0]], sa)[: COUNTS[g]]
                drain = mask_ref[0, :, cols].astype(F32) * evap_ref[0, :, cols]
                rest = film_ref[0, :, cols] - TIME_STEP * drain
                source = group_rows(rest, g) + TIME_STEP * flux
                if g == 0:
                    srcf_ref[EDGE : ROWS - EDGE, cols] = source
                else:
                    srcf_ref[0:EDGE, cols] = source[:EDGE]
                    srcf_ref[ROWS - EDGE :, cols] = source[EDGE:]

            one = [conv(*unit) for unit in units[:2]]
            two, three = [], []
            for k, unit in enumerate(units):
                two.append(first_act(*unit, one[k]))
                if k + 2 < len(units):
                    one.append(conv(*units[k + 2]))
                if k >= 1:
                    three.append(second_act(*units[k - 1], two[k - 1]))
                if k >= 2:
                    combine(*units[k - 2], three[k - 2])
            three.append(second_act(*units[-1], two[-1]))
            for k in range(max(0, len(units) - 2), len(units) - 1):
                combine(*units[k], three[k])
            for n in range(blocks):
                sources(n)
            combine(*units[-1], three[-1])
            return carry

        return body

    pairs = side // wide
    build_pieces(0)
    lax.fori_loop(0, 1, forward(0, 1), 0)

    neighbours = jnp.where(has_up, 1, 0) + jnp.where(has_down, 1, 0)
    pl.semaphore_wait(barrier, len(peers) + neighbours)
    exchange_start(0, halo_s, halo_r)

    def tell(n):
        for peer in beside:
            pl.semaphore_signal(far_sem.at[n], inc=1, device_id=peer, device_id_type=MESH)

    def hear(n):
        pl.semaphore_wait(far_sem.at[n], len(beside))

    tell(0)
    span_out(0, back_ref)

    lax.fori_loop(1, pairs, forward(0, 1), 0)

    span_solve(0, back_ref, sg_ref)

    hear(0)
    tell(1)

    def set_rim(values, row):
        for c in range(CIN):
            padf_ref[c, row : row + 1, :] = values[c : c + 1]

    exchange_wait(0, halo_s, halo_r, set_rim)
    build_pieces(1)
    lax.fori_loop(0, pairs // 2, forward(1, 2), 0)
    hear(1)
    tell(2)
    src_ref[...] = srcf_ref[...].astype(BF)
    span_out(1, src_ref)
    span_in(0, sg_ref)

    cacc_ref[...] = jnp.zeros_like(cacc_ref)
    macc_ref[...] = jnp.zeros_like(macc_ref)
    facc_ref[...] = jnp.zeros_like(facc_ref)

    def add_products(m, mixing, taps):
        macc_ref[m % 2] += mixing
        cacc_ref[chunk_rows(m), :] += taps

    def backward(i, carry):
        cols = pl.ds(pl.multiple_of(i * wide, wide), wide)
        flux_cots = TIME_STEP * sg_ref[:, cols].astype(F32)
        products = []
        for m in range(4):
            of = chunk_rows(m)
            rows = jnp.concatenate(
                [
                    jnp.broadcast_to(flux_cots[n : n + 1], (HID, wide)).astype(BF)
                    for n in ORDER[4 * m : 4 * m + 4]
                ],
                axis=0,
            )
            pre_first = v_ref[of, cols] * rows
            v_ref[of, cols] = pre_first
            mixing = nt(a1_ref[of, cols], u_ref[of, cols] * rows)
            taps = nt(pre_first, x_ref[group_of(m), :, cols])
            products.append((m, mixing, taps))
            if m > 0:
                add_products(*products[m - 1])
            if m == 1:
                cots = jnp.concatenate([group_rows(flux_cots, g) for g in range(2)], axis=0)
                facc_ref[...] += nt(cots.astype(BF), sa_ref[:, cols])
        add_products(*products[-1])
        return carry

    lax.fori_loop(0, side // wide, backward, 0)

    rolled = {}
    for r, n in enumerate(SHIFTS):
        term = cacc_ref[r * HID : (r + 1) * HID]
        rolled[n] = term if n not in rolled else rolled[n] + term
    taps = jnp.zeros((HID, WIDTH), F32)
    spare = jnp.zeros((HID, WIDTH - PIECES * 16), F32)
    for n, term in rolled.items():
        whole = jnp.concatenate([term, spare], axis=1)
        taps = taps + (whole if n == 0 else pltpu.roll(whole, WIDTH - n, axis=1))
    k_at = iota((HID, WIDTH), 0)
    col = iota((HID, WIDTH), 1)
    piece = col // 16
    tap_row = col % 16
    wanted = (tap_row * 3 + piece % 3) * CIN + piece // 3
    pick = onehot((k_at == wanted) & (tap_row < 3) & (piece < PIECES))
    low = jnp.zeros((HID, WIDTH), BF)
    right = jnp.zeros((HID, 2 * HID), F32)
    for t in split3(taps):
        right = right + nt(pick, jnp.concatenate([low, t], axis=0))
    tall = ROWS * HID
    fold = onehot(mod(iota((tall, 2 * HID), 0), HID) + HID == iota((tall, 2 * HID), 1))
    mine = div(iota((ROWS, tall), 1), HID) == iota((ROWS, tall), 0)
    flux_rows = jnp.zeros((ROWS, 2 * HID), F32)
    for f in split3(jnp.where(mine, facc_ref[...], 0.0)):
        flux_rows = flux_rows + nn(f, fold)
    flux_row = jnp.sum(flux_rows, axis=0, keepdims=True)
    right = right + jnp.where(iota((HID, 2 * HID), 0) == 9 * CIN, flux_row, 0.0)
    g_ref[...] = right
    blocks = []
    for r in range(4):
        of, at_span = slice(r * HID, (r + 1) * HID), slice((r // 2) * SPAN, (r // 2 + 1) * SPAN)
        blocks.append(macc_ref[0, of, at_span] + macc_ref[1, of, at_span])
    mixing = blocks[0] + blocks[2] + pltpu.roll(blocks[1] + blocks[3], HID, axis=1)
    g_ref[:, 0:HID] = mixing[:, 0:HID]

    own_block = pl.ds(pl.multiple_of(j_at * 8, 8), 8)
    p1_ref[j_at] = g_ref[own_block, :]
    stage1 = []
    for s in range(1, 8):
        other = mod(j_at + s, 8)
        stage1.append(
            remote(
                g_ref.at[pl.ds(pl.multiple_of(other * 8, 8), 8)],
                p1_ref.at[j_at],
                ar_ssem.at[0],
                ar_rsem.at[0],
                corner_peer(s),
            )
        )
    for copy in stage1:
        copy.start()

    span_solve(1, src_ref, across_ref)

    def features_back(i, carry):
        cols = pl.ds(pl.multiple_of(i * wide, wide), wide)
        for h in range(2):
            tt_ref[h, :, cols] = nn(wct_ref[:, group_part(h)], v_ref[group_part(h), cols])
        return carry

    lax.fori_loop(0, side // wide, features_back, 0)

    def finish(stage, slots, send_peer):
        remote(
            slots.at[pl.ds(0, 7)],
            slots.at[pl.ds(0, 7)],
            ar_ssem.at[stage],
            ar_rsem.at[stage],
            send_peer(1),
        ).wait()

    def begin(stage, slots, at_index, source, send_peer):
        for s in range(1, 8):
            remote(
                source,
                slots.at[at_index],
                ar_ssem.at[stage],
                ar_rsem.at[stage],
                send_peer(s),
            ).start()

    def summed(slots):
        total = slots[0]
        for n in range(1, 8):
            total = total + slots[n]
        return total

    hear(2)
    finish(0, p1_ref, corner_peer)
    q1_ref[...] = summed(p1_ref)
    p2_ref[z_at] = q1_ref[...]
    begin(1, p2_ref, z_at, q1_ref, z_peer)

    lane = iota((16, side), 1)
    for c in range(2):
        parts = []
        for h in range(2):
            s = c * 48
            left = jnp.where(lane == side - 1, 0.0, pltpu.roll(tt_ref[h, s : s + 16, :], side - 1, axis=1))
            right = jnp.where(lane == 0, 0.0, pltpu.roll(tt_ref[h, s + 32 : s + 48, :], 1, axis=1))
            parts.append(left + tt_ref[h, s + 16 : s + 32, :] + right)
        tot_ref[c, 0:8, :] = parts[1][0:8]
        tot_ref[c, 8:14, :] = jnp.zeros((6, side), F32)
        tot_ref[c, 14:22, :] = parts[1][8:16]
        tot_ref[c, 2:18, :] += parts[0]
        rim_s[0, c : c + 1, :] = parts[1][0:1]
        rim_s[1, c : c + 1, :] = parts[1][11:12]

    exchange_start(1, rim_s, rim_r)

    span_in(1, across_ref)
    pieces = [across_ref[:, k * SPAN : (k + 1) * SPAN] for k in range(nspan)]
    lines = jnp.concatenate(pieces, axis=0)
    f_hi = invs_ref[1, 0].reshape(NCLS * SPAN, SPAN)
    f_lo = invs_ref[1, 1].reshape(NCLS * SPAN, SPAN)
    products = nt(lines, f_hi) + nt(lines, f_lo)

    def store_final(k, value):
        final_ref[0, :, k * SPAN : (k + 1) * SPAN] = value

    span_select(products, scls_ref, store_final)
    final_out = pltpu.make_async_copy(final_ref, final_hbm, out_sem.at[0])
    final_out.start()

    finish(1, p2_ref, z_peer)
    q2_ref[...] = summed(p2_ref)
    p3_ref[y_at] = q2_ref[...]
    begin(2, p3_ref, y_at, q2_ref, y_peer)

    def add_rim(values, row):
        for c in range(2):
            at_row = 1 if row == 0 else ROWS
            tot_ref[c, at_row : at_row + 1, :] += values[c : c + 1]

    exchange_wait(1, rim_s, rim_r, add_rim)
    cot0 = tot_ref[0, 1 : ROWS + 1, :].astype(BF).astype(F32)
    cot1 = tot_ref[1, 1 : ROWS + 1, :].astype(BF).astype(F32)
    grad_ref[0] = sg_ref[...].astype(F32) + cot0 + 2.0 * film_ref[0] * cot1
    grad_out = pltpu.make_async_copy(grad_ref, grad_hbm, out_sem.at[1])
    grad_out.start()

    finish(2, p3_ref, y_peer)
    q3_ref[...] = summed(p3_ref)
    p4_ref[j_at] = q3_ref[...]
    begin(3, p4_ref, j_at, q3_ref, corner_peer)
    finish(3, p4_ref, corner_peer)
    scale = 1.0 / math.sqrt(DYHI * DCORE * side * side)
    gsum_ref[...] = p4_ref[...].reshape(HID, 2 * HID) * scale
    gsum_out = pltpu.make_async_copy(gsum_ref, gsum_hbm, out_sem.at[2])
    gsum_out.start()
    final_out.wait()
    grad_out.wait()
    gsum_out.wait()


def hand_out(final_in, grad_in, gsum_in, final_ref, grad_ref, convg_ref, mixg_ref, fluxg_ref):
    final_ref[...] = final_in[...]
    grad_ref[...] = grad_in[...]
    result = gsum_in[...]
    mixg_ref[...] = result[:, :HID]
    other = pltpu.roll(result, HID, axis=1)[:, :HID]
    for a in range(3):
        for b in range(3):
            k = (a * 3 + b) * CIN
            convg_ref[a, b] = other[k : k + CIN]
    fluxg_ref[...] = other[9 * CIN : 9 * CIN + 1]


def on_device(film, evap, mask, fcls, scls, inv, convw, mixw, fluxw, cot):
    side = film.shape[2]
    rows = film.shape[1]
    vmem = pl.BlockSpec(memory_space=pltpu.VMEM)
    hbm = pl.BlockSpec(memory_space=pltpu.HBM)
    free = pl.BlockSpec(memory_space=pl.ANY)
    args = (
        film,
        evap,
        mask,
        jnp.swapaxes(fcls, 1, 2),
        scls,
        inv,
        convw,
        mixw,
        fluxw.reshape(1, HID),
        cot,
    )
    args = tuple(pltpu.with_memory_space_constraint(a, pltpu.HBM) for a in args)
    chunk = side // GROUP
    tall = ROWS * HID
    slab = jax.ShapeDtypeStruct(film.shape, F32)
    block = jax.ShapeDtypeStruct((HID, 2 * HID), F32)
    final, grad, gsum = pl.pallas_call(
        kernel,
        out_shape=(slab, slab, block),
        in_specs=[hbm] * 10,
        out_specs=(free,) * 3,
        scratch_shapes=[pltpu.VMEM(a.shape, a.dtype) for a in args]
        + [
            pltpu.VMEM(film.shape, F32),
            pltpu.VMEM(film.shape, F32),
            pltpu.VMEM((HID, 2 * HID), F32),
            pltpu.VMEM((2, 2, NCLS, SPAN, SPAN), BF),
            pltpu.VMEM((2, SPAN, chunk), BF),
            pltpu.VMEM((2, SPAN, chunk), BF),
            pltpu.VMEM((2, CIN, side), BF),
            pltpu.VMEM((2, CIN, side), BF),
            pltpu.VMEM((CIN, 24, side), F32),
            pltpu.VMEM((2, PIECES * 16, side), BF),
            pltpu.VMEM((tall, WIDTH), BF),
            pltpu.VMEM((96, tall), BF),
            pltpu.VMEM((WIDTH, WIDTH), BF),
            pltpu.VMEM((WIDTH, WIDTH), BF),
            pltpu.VMEM((16, 3 * WIDTH), BF),
            pltpu.VMEM((WIDTH, 2 * WIDTH), F32),
            pltpu.VMEM((tall, side), BF),
            pltpu.VMEM((3, WIDTH, 2 * WIDTH), F32),
            pltpu.VMEM((tall, side), BF),
            pltpu.VMEM((tall, side), BF),
            pltpu.VMEM((tall, side), BF),
            pltpu.VMEM((rows, side), F32),
            pltpu.VMEM((rows, side), BF),
            pltpu.VMEM((rows, side), BF),
            pltpu.VMEM((rows, side), BF),
            pltpu.VMEM((rows, side), BF),
            pltpu.VMEM((tall, PIECES * 16), F32),
            pltpu.VMEM((2, WIDTH, WIDTH), F32),
            pltpu.VMEM((ROWS, tall), F32),
            pltpu.VMEM((2, 96, side), F32),
            pltpu.VMEM((2, 24, side), F32),
            pltpu.VMEM((2, 2, side), F32),
            pltpu.VMEM((2, 2, side), F32),
            pltpu.VMEM((SPAN, SPAN), F32),
            pltpu.VMEM((HID, 2 * HID), F32),
            pltpu.VMEM((8, 8, 2 * HID), F32),
            pltpu.VMEM((8, 2 * HID), F32),
            pltpu.VMEM((8, 8, 2 * HID), F32),
            pltpu.VMEM((8, 2 * HID), F32),
            pltpu.VMEM((8, 8, 2 * HID), F32),
            pltpu.VMEM((8, 2 * HID), F32),
            pltpu.VMEM((8, 8, 2 * HID), F32),
            pltpu.SemaphoreType.DMA((10,)),
            pltpu.SemaphoreType.DMA((3,)),
            pltpu.SemaphoreType.DMA((4,)),
            pltpu.SemaphoreType.DMA((4,)),
            pltpu.SemaphoreType.DMA((2, 2)),
            pltpu.SemaphoreType.DMA((2, 2)),
            pltpu.SemaphoreType.DMA((4,)),
            pltpu.SemaphoreType.DMA((4,)),
            pltpu.SemaphoreType.REGULAR((3,)),
        ],
        compiler_params=pltpu.CompilerParams(
            collective_id=0, has_side_effects=True, vmem_limit_bytes=48 * 1024 * 1024
        ),
    )(*args)
    outs = pl.pallas_call(
        hand_out,
        out_shape=(
            slab,
            slab,
            jax.ShapeDtypeStruct(convw.shape, F32),
            jax.ShapeDtypeStruct(mixw.shape, F32),
            jax.ShapeDtypeStruct((1, HID), F32),
        ),
        in_specs=[vmem] * 3,
        out_specs=(vmem,) * 5,
        compiler_params=pltpu.CompilerParams(vmem_limit_bytes=4 * 1024 * 1024),
    )(final, grad, gsum)
    return outs[0], outs[1], outs[2], outs[3], outs[4].reshape(HID)


def solution(mesh):
    sizes = dict(mesh.shape)
    assert sizes == {"rep": DYHI * DCORE, "sp": DYLO * DZ * DX}
    return jax.shard_map(
        on_device,
        mesh=mesh,
        in_specs=(
            P("rep", "sp", None),
            P("rep", "sp", None),
            P("rep", "sp", None),
            P("rep", None, None),
            P("rep", "sp", None),
            P(),
            P(),
            P(),
            P(),
            P("rep", "sp", None),
        ),
        out_specs=(P("rep", "sp", None), P("rep", "sp", None), P(), P(), P()),
        check_vma=False,
    )
```

```python
import math

import jax
import jax.numpy as jnp
from jax import lax
from jax.experimental import pallas as pl
from jax.experimental.pallas import tpu as pltpu
from jax.sharding import PartitionSpec as P

BF = jnp.bfloat16
F32 = jnp.float32
MESH = pl.DeviceIdType.MESH
SPAN = 128
ROWS = 16
HID = 64
CIN = 4
PIECES = 12
WIDTH = 256
NCLS = 4
GROUP = SPAN // ROWS
DX, DZ, DYLO, DYHI, DCORE = 4, 8, 4, 2, 2
TIME_STEP = 0.5
FAR_FIRST = (4, 3, 5, 2, 6, 1, 7)
FAR_FIRST_CORNER = (6, 2, 1, 3, 5, 7, 4)


def nt(a, b):
    return lax.dot_general(a, b, (((1,), (1,)), ((), ())), preferred_element_type=F32)


def nn(a, b):
    return lax.dot_general(a, b, (((1,), (0,)), ((), ())), preferred_element_type=F32)


def split2(v):
    hi = v.astype(BF)
    return hi, (v - hi.astype(F32)).astype(BF)


def split3(v):
    hi = v.astype(BF)
    rest = v - hi.astype(F32)
    mid = rest.astype(BF)
    return hi, mid, (rest - mid.astype(F32)).astype(BF)


def mod(a, n):
    return lax.rem(a, jnp.int32(n))


def div(a, n):
    return lax.div(a, jnp.int32(n))


EDGE = 2
ORDER = list(range(EDGE, ROWS - EDGE)) + [0, 1, ROWS - 2, ROWS - 1]
SHIFTS = list(range(ROWS - 2 * EDGE)) + [0, 1, 8, 9]
CHUNKS = ((0, 1, 2), (3,))
COUNTS = (ROWS - 2 * EDGE, 2 * EDGE)


def group_of(m):
    return 0 if m in CHUNKS[0] else 1


def chunk_rows(m):
    return slice(m * WIDTH, (m + 1) * WIDTH)


def group_part(g):
    return slice(CHUNKS[g][0] * WIDTH, (CHUNKS[g][-1] + 1) * WIDTH)


def group_rows(values, group):
    if group == 0:
        return values[EDGE : ROWS - EDGE]
    return jnp.concatenate([values[:EDGE], values[ROWS - EDGE :]], axis=0)


def iota(shape, dim):
    return lax.broadcasted_iota(jnp.int32, shape, dim)


def onehot(cond):
    return jnp.where(cond, 1.0, 0.0).astype(BF)


def span_select(products, cls_ref, store):
    for k in range(products.shape[0] // ROWS):
        column = cls_ref[0, :, k : k + 1]
        result = products[k * ROWS : (k + 1) * ROWS, 0:SPAN]
        for group in range(1, NCLS):
            part = products[k * ROWS : (k + 1) * ROWS, group * SPAN : (group + 1) * SPAN]
            result = jnp.where(column == group, part, result)
        store(k, result)


def kernel(
    film_hbm,
    evap_hbm,
    mask_hbm,
    fcls_hbm,
    scls_hbm,
    inv_hbm,
    convw_hbm,
    mixw_hbm,
    fluxw_hbm,
    cot_hbm,
    final_hbm,
    grad_hbm,
    gsum_hbm,
    film_ref,
    evap_ref,
    mask_ref,
    fcls_ref,
    scls_ref,
    inv_ref,
    convw_ref,
    mixw_ref,
    fluxw_ref,
    cot_ref,
    final_ref,
    grad_ref,
    gsum_ref,
    invs_ref,
    recv_ref,
    mid_ref,
    halo_s,
    halo_r,
    padf_ref,
    x_ref,
    wb_ref,
    wct_ref,
    bdf_ref,
    bdb_ref,
    fwb_ref,
    fwc_ref,
    a1_ref,
    d1_ref,
    sa_ref,
    u_ref,
    v_ref,
    srcf_ref,
    src_ref,
    back_ref,
    sg_ref,
    across_ref,
    cacc_ref,
    macc_ref,
    facc_ref,
    tt_ref,
    tot_ref,
    rim_s,
    rim_r,
    w36_ref,
    g_ref,
    p1_ref,
    q1_ref,
    p2_ref,
    q2_ref,
    p3_ref,
    q3_ref,
    p4_ref,
    in_sem,
    out_sem,
    ag_ssem,
    ag_rsem,
    nb_ssem,
    nb_rsem,
    ar_ssem,
    ar_rsem,
    far_sem,
):
    sp = lax.axis_index("sp")
    rep = lax.axis_index("rep")
    nsp = DYLO * DZ * DX
    has_up = sp > 0
    has_down = sp < nsp - 1
    barrier = pltpu.get_barrier_semaphore()

    def at(r, s):
        return {"rep": r, "sp": s}

    def signal(peer):
        pl.semaphore_signal(barrier, inc=1, device_id=peer, device_id_type=MESH)

    @pl.when(has_up)
    def _():
        signal(at(rep, sp - 1))

    @pl.when(has_down)
    def _():
        signal(at(rep, sp + 1))

    inputs = [
        pltpu.make_async_copy(hbm, ref, in_sem.at[n])
        for n, (hbm, ref) in enumerate(
            (
                (convw_hbm, convw_ref),
                (mixw_hbm, mixw_ref),
                (fluxw_hbm, fluxw_ref),
                (cot_hbm, cot_ref),
                (inv_hbm, inv_ref),
                (scls_hbm, scls_ref),
                (film_hbm, film_ref),
                (evap_hbm, evap_ref),
                (mask_hbm, mask_ref),
                (fcls_hbm, fcls_ref),
            )
        )
    ]
    for copy in inputs[:6]:
        copy.start()
    side = film_ref.shape[2]
    x_at = mod(sp, DX)
    z_at = mod(div(sp, DX), DZ)
    ylo_at = div(sp, DX * DZ)
    yhi_at = div(rep, DCORE)
    core_at = mod(rep, DCORE)
    y_at = yhi_at * DYLO + ylo_at
    member = mod(sp, GROUP)
    first = sp - member

    def group_peer(s):
        return at(rep, first + mod(member + s, GROUP))

    j_at = core_at * DX + x_at

    def corner_peer(s):
        other = mod(j_at + s, DCORE * DX)
        return at(yhi_at * DCORE + div(other, DX), sp - x_at + mod(other, DX))

    def z_peer(s):
        return at(rep, sp + (mod(z_at + s, DZ) - z_at) * DX)

    def y_peer(s):
        other = mod(y_at + s, DYHI * DYLO)
        return at(
            div(other, DYLO) * DCORE + core_at,
            sp + (mod(other, DYLO) - ylo_at) * DX * DZ,
        )

    peers = [group_peer(s) for s in range(1, GROUP)]
    peers += [corner_peer(s) for s in range(1, 8)]
    beside = [z_peer(1), z_peer(7), y_peer(1), y_peer(7)]
    peers += beside
    for peer in peers:
        signal(peer)
    for copy in inputs[6:]:
        copy.start()

    def remote(src, dst, ssem, rsem, peer):
        return pltpu.make_async_remote_copy(
            src_ref=src,
            dst_ref=dst,
            send_sem=ssem,
            recv_sem=rsem,
            device_id=peer,
            device_id_type=MESH,
        )

    for copy in inputs[:3]:
        copy.wait()

    w36_ref[...] = jnp.zeros_like(w36_ref)
    for a in range(3):
        for b in range(3):
            k = (a * 3 + b) * CIN
            w36_ref[k : k + CIN, 0:HID] = convw_ref[a, b].astype(F32)
    w_t = w36_ref[...].T[:HID].astype(BF)
    k_at = iota((SPAN, WIDTH), 0)
    col = iota((SPAN, WIDTH), 1)
    piece = col // 16
    tap_row = col % 16
    wanted = (tap_row * 3 + piece % 3) * CIN + piece // 3
    pick = (k_at == wanted) & (tap_row < 3) & (piece < PIECES)
    band0 = nn(w_t, onehot(pick))
    rolls = [band0 if n == 0 else pltpu.roll(band0, n, axis=1) for n in range(max(SHIFTS) + 1)]
    for m in range(4):
        band = jnp.concatenate([rolls[n] for n in SHIFTS[4 * m : 4 * m + 4]], axis=0)
        wb_ref[chunk_rows(m), :] = band.astype(BF)
        wct_ref[:, chunk_rows(m)] = band[:, :SPAN].T[:96].astype(BF)
    mix = mixw_ref[...]
    tile4 = onehot(iota((HID, WIDTH), 1) % HID == iota((HID, WIDTH), 0))
    wide = nn(mix, tile4)
    tall = jnp.concatenate([wide] * 4, axis=0)
    same = iota((WIDTH, WIDTH), 0) // HID == iota((WIDTH, WIDTH), 1) // HID
    diag = jnp.where(same, tall, 0.0)
    bdb_ref[...] = diag.astype(BF)
    bdf_ref[...] = diag.T.astype(BF)
    fw = fluxw_ref[...]
    tile8 = onehot(mod(iota((HID, 3 * WIDTH), 1), HID) == iota((HID, 3 * WIDTH), 0))
    fw_wide = nn(jnp.broadcast_to(fw, (16, HID)), tile8)
    own = div(iota((16, 3 * WIDTH), 1), HID) == iota((16, 3 * WIDTH), 0)
    fwb_ref[...] = jnp.where(own, fw_wide, 0.0).astype(BF)
    eye = iota((HID, HID), 0) == iota((HID, HID), 1)
    fw_col = jnp.sum(
        jnp.where(eye, jnp.broadcast_to(fw.astype(F32), (HID, HID)), 0.0), axis=1, keepdims=True
    )
    fwc_ref[...] = jnp.concatenate([jnp.broadcast_to(fw_col, (HID, 2 * WIDTH))] * 4, axis=0)

    for copy in inputs[3:6]:
        copy.wait()
    inv_hi, inv_lo = split2(inv_ref[...].reshape(NCLS * SPAN, SPAN))
    for c in range(NCLS):
        of = slice(c * SPAN, (c + 1) * SPAN)
        t_hi, t_lo = split2(inv_ref[c].T)
        invs_ref[0, 0, c] = t_hi
        invs_ref[0, 1, c] = t_lo
        invs_ref[1, 0, c] = inv_hi[of]
        invs_ref[1, 1, c] = inv_lo[of]

    nspan = side // SPAN
    lines = jnp.concatenate(
        [cot_ref[0, :, k * SPAN : (k + 1) * SPAN] for k in range(nspan)], axis=0
    )
    l_hi, l_lo = split2(lines)
    right_hi = jnp.concatenate([inv_hi[c * SPAN : (c + 1) * SPAN] for c in range(NCLS)], axis=1)
    right_lo = jnp.concatenate([inv_lo[c * SPAN : (c + 1) * SPAN] for c in range(NCLS)], axis=1)
    products = nn(l_hi, right_hi) + nn(l_lo, right_hi) + nn(l_hi, right_lo)

    def store_back(k, value):
        back_ref[:, k * SPAN : (k + 1) * SPAN] = value.astype(BF)

    span_select(products, scls_ref, store_back)
    own_rows = pl.ds(pl.multiple_of(member * ROWS, ROWS), ROWS)
    chunk = side // GROUP

    def columns_of(n):
        return pl.ds(pl.multiple_of(n * chunk, chunk), chunk)

    def rows_of(n):
        return pl.ds(pl.multiple_of(n * ROWS, ROWS), ROWS)

    def span_out(which, field):
        recv_ref[which, own_rows, :] = field[:, columns_of(member)]
        for s in FAR_FIRST_CORNER:
            remote(
                field.at[:, columns_of(mod(member + s, GROUP))],
                recv_ref.at[which, own_rows],
                ag_ssem.at[2 * which],
                ag_rsem.at[2 * which],
                group_peer(s),
            ).start()

    def span_solve(which, field, result):
        others = GROUP - 1
        remote(
            field.at[:, pl.ds(0, others * chunk)],
            recv_ref.at[which, pl.ds(0, others * ROWS)],
            ag_ssem.at[2 * which],
            ag_rsem.at[2 * which],
            group_peer(1),
        ).wait()
        values = recv_ref[which]
        line_cls = fcls_ref[0, :, columns_of(member)]
        own_span = iota(line_cls.shape, 0) == div(sp, GROUP)
        classes = jnp.sum(jnp.where(own_span, line_cls, 0), axis=0, keepdims=True)
        solved = None
        for c in range(NCLS):
            product = nn(invs_ref[which, 0, c], values) + nn(invs_ref[which, 1, c], values)
            solved = product if c == 0 else jnp.where(classes == c, product, solved)
        mid_ref[which] = solved.astype(BF)
        result[:, columns_of(member)] = mid_ref[which, own_rows, :]
        for s in FAR_FIRST_CORNER:
            remote(
                mid_ref.at[which, rows_of(mod(member + s, GROUP))],
                result.at[:, columns_of(member)],
                ag_ssem.at[2 * which + 1],
                ag_rsem.at[2 * which + 1],
                group_peer(s),
            ).start()

    def span_in(which, result):
        others = GROUP - 1
        remote(
            mid_ref.at[which, pl.ds(0, others * ROWS)],
            result.at[:, pl.ds(0, others * chunk)],
            ag_ssem.at[2 * which + 1],
            ag_rsem.at[2 * which + 1],
            group_peer(1),
        ).wait()

    for copy in inputs[6:]:
        copy.wait()

    film = film_ref[0]
    evap = evap_ref[0]
    maskf = mask_ref[0].astype(F32)
    features = [f.astype(BF).astype(F32) for f in (film, film * film, maskf, evap)]
    for c, feature in enumerate(features):
        padf_ref[c, 0:1, :] = jnp.zeros((1, side), F32)
        padf_ref[c, 1 : ROWS + 1, :] = feature
        padf_ref[c, ROWS + 1 :, :] = jnp.zeros((7, side), F32)
    halo_s[0] = jnp.concatenate([f[0:1] for f in features], axis=0).astype(BF)
    halo_s[1] = jnp.concatenate([f[ROWS - 1 :] for f in features], axis=0).astype(BF)

    def to_neighbours(n, sent, landed):
        upward = remote(
            sent.at[0], landed.at[1], nb_ssem.at[n, 0], nb_rsem.at[n, 0], at(rep, sp - 1)
        )
        downward = remote(
            sent.at[1], landed.at[0], nb_ssem.at[n, 1], nb_rsem.at[n, 1], at(rep, sp + 1)
        )
        return upward, downward

    def exchange_start(n, sent, landed):
        upward, downward = to_neighbours(n, sent, landed)

        @pl.when(has_up)
        def _():
            upward.start()

        @pl.when(has_down)
        def _():
            downward.start()

    def exchange_wait(n, sent, landed, use):
        upward, downward = to_neighbours(n, sent, landed)

        @pl.when(has_up)
        def _():
            upward.wait_send()
            downward.wait_recv()
            use(landed[0].astype(F32), 0)

        @pl.when(has_down)
        def _():
            downward.wait_send()
            upward.wait_recv()
            use(landed[1].astype(F32), ROWS + 1)

    wide = 2 * WIDTH
    lane = iota((24, side), 1)

    def build_pieces(g):
        for c in range(CIN):
            middle = padf_ref[c]
            left = jnp.where(lane == 0, 0.0, pltpu.roll(middle, 1, axis=1))
            right = jnp.where(lane == side - 1, 0.0, pltpu.roll(middle, side - 1, axis=1))
            for b, values in enumerate((left, middle, right)):
                s = (c * 3 + b) * 16
                if g == 0:
                    piece = values[EDGE : EDGE + 16]
                else:
                    piece = jnp.concatenate([values[0:8], values[14:22]], axis=0)
                x_ref[g, s : s + 16, :] = piece.astype(BF)

    def forward(g, blocks):
        units = [(m, n) for n in range(blocks) for m in CHUNKS[g]]

        def body(i, carry):
            factors = {}

            def cols_at(n):
                return pl.ds(pl.multiple_of((i * blocks + n) * wide, wide), wide)

            def conv(m, n):
                return nn(wb_ref[chunk_rows(m), : PIECES * 16], x_ref[g, :, cols_at(n)])

            def first_act(m, n, total):
                t1 = jnp.tanh(total)
                a1 = t1.astype(BF)
                a1_ref[chunk_rows(m), cols_at(n)] = a1
                d1_ref[units.index((m, n))] = 1.0 - t1 * t1
                return nn(bdf_ref[...], a1)

            def second_act(m, n, total):
                t2 = jnp.tanh(total)
                active = t2.astype(BF)
                sa_ref[chunk_rows(m), cols_at(n)] = active
                u = (fwc_ref[...] * (1.0 - t2 * t2)).astype(BF)
                u_ref[chunk_rows(m), cols_at(n)] = u
                factors[m, n] = active
                return nn(bdb_ref[...], u)

            def combine(m, n, total):
                v = d1_ref[units.index((m, n))] * total
                v_ref[chunk_rows(m), cols_at(n)] = v.astype(BF)

            def sources(n):
                cols = cols_at(n)
                sa = jnp.concatenate([factors[m, n] for m in CHUNKS[g]], axis=0)
                flux = nn(fwb_ref[:, : sa.shape[0]], sa)[: COUNTS[g]]
                drain = mask_ref[0, :, cols].astype(F32) * evap_ref[0, :, cols]
                rest = film_ref[0, :, cols] - TIME_STEP * drain
                source = group_rows(rest, g) + TIME_STEP * flux
                if g == 0:
                    srcf_ref[EDGE : ROWS - EDGE, cols] = source
                else:
                    srcf_ref[0:EDGE, cols] = source[:EDGE]
                    srcf_ref[ROWS - EDGE :, cols] = source[EDGE:]

            one = [conv(*unit) for unit in units[:2]]
            two, three = [], []
            for k, unit in enumerate(units):
                two.append(first_act(*unit, one[k]))
                if k + 2 < len(units):
                    one.append(conv(*units[k + 2]))
                if k >= 1:
                    three.append(second_act(*units[k - 1], two[k - 1]))
                if k >= 2:
                    combine(*units[k - 2], three[k - 2])
            three.append(second_act(*units[-1], two[-1]))
            for k in range(max(0, len(units) - 2), len(units) - 1):
                combine(*units[k], three[k])
            for n in range(blocks):
                sources(n)
            combine(*units[-1], three[-1])
            return carry

        return body

    pairs = side // wide
    build_pieces(0)

    neighbours = jnp.where(has_up, 1, 0) + jnp.where(has_down, 1, 0)
    pl.semaphore_wait(barrier, len(peers) + neighbours)
    span_out(0, back_ref)
    exchange_start(0, halo_s, halo_r)

    def tell(n):
        for peer in beside:
            pl.semaphore_signal(far_sem.at[n], inc=1, device_id=peer, device_id_type=MESH)

    def hear(n):
        pl.semaphore_wait(far_sem.at[n], len(beside))

    tell(0)

    lax.fori_loop(0, pairs - 1, forward(0, 1), 0)
    span_solve(0, back_ref, sg_ref)
    lax.fori_loop(pairs - 1, pairs, forward(0, 1), 0)

    hear(0)
    tell(1)

    def set_rim(values, row):
        for c in range(CIN):
            padf_ref[c, row : row + 1, :] = values[c : c + 1]

    exchange_wait(0, halo_s, halo_r, set_rim)
    build_pieces(1)
    lax.fori_loop(0, pairs // 2, forward(1, 2), 0)
    hear(1)
    tell(2)
    src_ref[...] = srcf_ref[...].astype(BF)
    span_out(1, src_ref)
    span_in(0, sg_ref)

    cacc_ref[...] = jnp.zeros_like(cacc_ref)
    macc_ref[...] = jnp.zeros_like(macc_ref)
    facc_ref[...] = jnp.zeros_like(facc_ref)

    def add_products(m, mixing, taps):
        macc_ref[m % 2] += mixing
        cacc_ref[chunk_rows(m), :] += taps

    def backward(i, carry):
        cols = pl.ds(pl.multiple_of(i * wide, wide), wide)
        flux_cots = TIME_STEP * sg_ref[:, cols].astype(F32)
        products = []
        for m in range(4):
            of = chunk_rows(m)
            rows = jnp.concatenate(
                [
                    jnp.broadcast_to(flux_cots[n : n + 1], (HID, wide)).astype(BF)
                    for n in ORDER[4 * m : 4 * m + 4]
                ],
                axis=0,
            )
            pre_first = v_ref[of, cols] * rows
            v_ref[of, cols] = pre_first
            mixing = nt(a1_ref[of, cols], u_ref[of, cols] * rows)
            taps = nt(pre_first, x_ref[group_of(m), :, cols])
            products.append((m, mixing, taps))
            if m > 0:
                add_products(*products[m - 1])
            active = (sa_ref[of, cols] * rows).astype(F32)
            part = active[:HID]
            for r in range(1, 4):
                part = part + active[r * HID : (r + 1) * HID]
            facc_ref[...] += part
        add_products(*products[-1])
        return carry

    lax.fori_loop(0, side // wide, backward, 0)

    rolled = {}
    for r, n in enumerate(SHIFTS):
        term = cacc_ref[r * HID : (r + 1) * HID]
        rolled[n] = term if n not in rolled else rolled[n] + term
    taps = jnp.zeros((HID, WIDTH), F32)
    spare = jnp.zeros((HID, WIDTH - PIECES * 16), F32)
    for n, term in rolled.items():
        whole = jnp.concatenate([term, spare], axis=1)
        taps = taps + (whole if n == 0 else pltpu.roll(whole, WIDTH - n, axis=1))
    k_at = iota((HID, WIDTH), 0)
    col = iota((HID, WIDTH), 1)
    piece = col // 16
    tap_row = col % 16
    wanted = (tap_row * 3 + piece % 3) * CIN + piece // 3
    pick = onehot((k_at == wanted) & (tap_row < 3) & (piece < PIECES))
    low = jnp.zeros((HID, WIDTH), BF)
    right = jnp.zeros((HID, 2 * HID), F32)
    for t in split3(taps):
        right = right + nt(pick, jnp.concatenate([low, t], axis=0))
    flux_all = facc_ref[...]
    flux_lanes = flux_all[:, :SPAN]
    for n in range(1, 4):
        flux_lanes = flux_lanes + flux_all[:, n * SPAN : (n + 1) * SPAN]
    flux_row = jnp.zeros((1, 2 * HID), F32)
    ones = jnp.ones((8, SPAN), BF)
    spare_rows = jnp.zeros((HID, SPAN), BF)
    for f in split3(flux_lanes):
        flux_row = flux_row + nt(ones, jnp.concatenate([spare_rows, f], axis=0))[:1]
    right = right + jnp.where(iota((HID, 2 * HID), 0) == 9 * CIN, flux_row, 0.0)
    g_ref[...] = right
    blocks = []
    for r in range(4):
        of, at_span = slice(r * HID, (r + 1) * HID), slice((r // 2) * SPAN, (r // 2 + 1) * SPAN)
        blocks.append(macc_ref[0, of, at_span] + macc_ref[1, of, at_span])
    mixing = blocks[0] + blocks[2] + pltpu.roll(blocks[1] + blocks[3], HID, axis=1)
    g_ref[:, 0:HID] = mixing[:, 0:HID]

    own_block = pl.ds(pl.multiple_of(j_at * 8, 8), 8)
    p1_ref[j_at] = g_ref[own_block, :]
    stage1 = []
    for s in FAR_FIRST_CORNER:
        other = mod(j_at + s, 8)
        stage1.append(
            remote(
                g_ref.at[pl.ds(pl.multiple_of(other * 8, 8), 8)],
                p1_ref.at[j_at],
                ar_ssem.at[0],
                ar_rsem.at[0],
                corner_peer(s),
            )
        )
    for copy in stage1:
        copy.start()

    span_solve(1, src_ref, across_ref)

    def features_back(i, carry):
        cols = pl.ds(pl.multiple_of(i * wide, wide), wide)
        for h in range(2):
            tt_ref[h, :, cols] = nn(wct_ref[:, group_part(h)], v_ref[group_part(h), cols])
        return carry

    lax.fori_loop(0, side // wide, features_back, 0)

    def finish(stage, slots, send_peer):
        remote(
            slots.at[pl.ds(0, 7)],
            slots.at[pl.ds(0, 7)],
            ar_ssem.at[stage],
            ar_rsem.at[stage],
            send_peer(1),
        ).wait()

    def begin(stage, slots, at_index, source, send_peer):
        for s in FAR_FIRST_CORNER if stage == 3 else FAR_FIRST:
            remote(
                source,
                slots.at[at_index],
                ar_ssem.at[stage],
                ar_rsem.at[stage],
                send_peer(s),
            ).start()

    def summed(slots):
        total = slots[0]
        for n in range(1, 8):
            total = total + slots[n]
        return total

    hear(2)
    finish(0, p1_ref, corner_peer)
    q1_ref[...] = summed(p1_ref)
    p2_ref[z_at] = q1_ref[...]
    begin(1, p2_ref, z_at, q1_ref, z_peer)

    lane = iota((16, side), 1)
    for c in range(2):
        parts = []
        for h in range(2):
            s = c * 48
            left = jnp.where(lane == side - 1, 0.0, pltpu.roll(tt_ref[h, s : s + 16, :], side - 1, axis=1))
            right = jnp.where(lane == 0, 0.0, pltpu.roll(tt_ref[h, s + 32 : s + 48, :], 1, axis=1))
            parts.append(left + tt_ref[h, s + 16 : s + 32, :] + right)
        tot_ref[c, 0:8, :] = parts[1][0:8]
        tot_ref[c, 8:14, :] = jnp.zeros((6, side), F32)
        tot_ref[c, 14:22, :] = parts[1][8:16]
        tot_ref[c, 2:18, :] += parts[0]
        rim_s[0, c : c + 1, :] = parts[1][0:1]
        rim_s[1, c : c + 1, :] = parts[1][11:12]

    exchange_start(1, rim_s, rim_r)

    span_in(1, across_ref)
    pieces = [across_ref[:, k * SPAN : (k + 1) * SPAN] for k in range(nspan)]
    lines = jnp.concatenate(pieces, axis=0)
    f_hi = invs_ref[1, 0].reshape(NCLS * SPAN, SPAN)
    f_lo = invs_ref[1, 1].reshape(NCLS * SPAN, SPAN)
    products = nt(lines, f_hi) + nt(lines, f_lo)

    def store_final(k, value):
        final_ref[0, :, k * SPAN : (k + 1) * SPAN] = value

    span_select(products, scls_ref, store_final)
    final_out = pltpu.make_async_copy(final_ref, final_hbm, out_sem.at[0])
    final_out.start()

    finish(1, p2_ref, z_peer)
    q2_ref[...] = summed(p2_ref)
    p3_ref[y_at] = q2_ref[...]
    begin(2, p3_ref, y_at, q2_ref, y_peer)

    def add_rim(values, row):
        for c in range(2):
            at_row = 1 if row == 0 else ROWS
            tot_ref[c, at_row : at_row + 1, :] += values[c : c + 1]

    exchange_wait(1, rim_s, rim_r, add_rim)
    cot0 = tot_ref[0, 1 : ROWS + 1, :].astype(BF).astype(F32)
    cot1 = tot_ref[1, 1 : ROWS + 1, :].astype(BF).astype(F32)
    grad_ref[0] = sg_ref[...].astype(F32) + cot0 + 2.0 * film_ref[0] * cot1
    grad_out = pltpu.make_async_copy(grad_ref, grad_hbm, out_sem.at[1])
    grad_out.start()

    finish(2, p3_ref, y_peer)
    q3_ref[...] = summed(p3_ref)
    p4_ref[j_at] = q3_ref[...]
    begin(3, p4_ref, j_at, q3_ref, corner_peer)
    finish(3, p4_ref, corner_peer)
    scale = 1.0 / math.sqrt(DYHI * DCORE * side * side)
    gsum_ref[...] = p4_ref[...].reshape(HID, 2 * HID) * scale
    gsum_out = pltpu.make_async_copy(gsum_ref, gsum_hbm, out_sem.at[2])
    gsum_out.start()
    final_out.wait()
    grad_out.wait()
    gsum_out.wait()


def hand_out(final_in, grad_in, gsum_in, final_ref, grad_ref, convg_ref, mixg_ref, fluxg_ref):
    final_ref[...] = final_in[...]
    grad_ref[...] = grad_in[...]
    result = gsum_in[...]
    mixg_ref[...] = result[:, :HID]
    other = pltpu.roll(result, HID, axis=1)[:, :HID]
    for a in range(3):
        for b in range(3):
            k = (a * 3 + b) * CIN
            convg_ref[a, b] = other[k : k + CIN]
    fluxg_ref[...] = other[9 * CIN : 9 * CIN + 1]


def on_device(film, evap, mask, fcls, scls, inv, convw, mixw, fluxw, cot):
    side = film.shape[2]
    rows = film.shape[1]
    vmem = pl.BlockSpec(memory_space=pltpu.VMEM)
    hbm = pl.BlockSpec(memory_space=pltpu.HBM)
    free = pl.BlockSpec(memory_space=pl.ANY)
    args = (
        film,
        evap,
        mask,
        jnp.swapaxes(fcls, 1, 2),
        scls,
        inv,
        convw,
        mixw,
        fluxw.reshape(1, HID),
        cot,
    )
    args = tuple(pltpu.with_memory_space_constraint(a, pltpu.HBM) for a in args)
    chunk = side // GROUP
    tall = ROWS * HID
    slab = jax.ShapeDtypeStruct(film.shape, F32)
    block = jax.ShapeDtypeStruct((HID, 2 * HID), F32)
    final, grad, gsum = pl.pallas_call(
        kernel,
        out_shape=(slab, slab, block),
        in_specs=[hbm] * 10,
        out_specs=(free,) * 3,
        scratch_shapes=[pltpu.VMEM(a.shape, a.dtype) for a in args]
        + [
            pltpu.VMEM(film.shape, F32),
            pltpu.VMEM(film.shape, F32),
            pltpu.VMEM((HID, 2 * HID), F32),
            pltpu.VMEM((2, 2, NCLS, SPAN, SPAN), BF),
            pltpu.VMEM((2, SPAN, chunk), BF),
            pltpu.VMEM((2, SPAN, chunk), BF),
            pltpu.VMEM((2, CIN, side), BF),
            pltpu.VMEM((2, CIN, side), BF),
            pltpu.VMEM((CIN, 24, side), F32),
            pltpu.VMEM((2, PIECES * 16, side), BF),
            pltpu.VMEM((tall, WIDTH), BF),
            pltpu.VMEM((96, tall), BF),
            pltpu.VMEM((WIDTH, WIDTH), BF),
            pltpu.VMEM((WIDTH, WIDTH), BF),
            pltpu.VMEM((16, 3 * WIDTH), BF),
            pltpu.VMEM((WIDTH, 2 * WIDTH), F32),
            pltpu.VMEM((tall, side), BF),
            pltpu.VMEM((3, WIDTH, 2 * WIDTH), F32),
            pltpu.VMEM((tall, side), BF),
            pltpu.VMEM((tall, side), BF),
            pltpu.VMEM((tall, side), BF),
            pltpu.VMEM((rows, side), F32),
            pltpu.VMEM((rows, side), BF),
            pltpu.VMEM((rows, side), BF),
            pltpu.VMEM((rows, side), BF),
            pltpu.VMEM((rows, side), BF),
            pltpu.VMEM((tall, PIECES * 16), F32),
            pltpu.VMEM((2, WIDTH, WIDTH), F32),
            pltpu.VMEM((HID, 2 * WIDTH), F32),
            pltpu.VMEM((2, 96, side), F32),
            pltpu.VMEM((2, 24, side), F32),
            pltpu.VMEM((2, 2, side), F32),
            pltpu.VMEM((2, 2, side), F32),
            pltpu.VMEM((SPAN, SPAN), F32),
            pltpu.VMEM((HID, 2 * HID), F32),
            pltpu.VMEM((8, 8, 2 * HID), F32),
            pltpu.VMEM((8, 2 * HID), F32),
            pltpu.VMEM((8, 8, 2 * HID), F32),
            pltpu.VMEM((8, 2 * HID), F32),
            pltpu.VMEM((8, 8, 2 * HID), F32),
            pltpu.VMEM((8, 2 * HID), F32),
            pltpu.VMEM((8, 8, 2 * HID), F32),
            pltpu.SemaphoreType.DMA((10,)),
            pltpu.SemaphoreType.DMA((3,)),
            pltpu.SemaphoreType.DMA((4,)),
            pltpu.SemaphoreType.DMA((4,)),
            pltpu.SemaphoreType.DMA((2, 2)),
            pltpu.SemaphoreType.DMA((2, 2)),
            pltpu.SemaphoreType.DMA((4,)),
            pltpu.SemaphoreType.DMA((4,)),
            pltpu.SemaphoreType.REGULAR((3,)),
        ],
        compiler_params=pltpu.CompilerParams(
            collective_id=0, has_side_effects=True, vmem_limit_bytes=48 * 1024 * 1024
        ),
    )(*args)
    outs = pl.pallas_call(
        hand_out,
        out_shape=(
            slab,
            slab,
            jax.ShapeDtypeStruct(convw.shape, F32),
            jax.ShapeDtypeStruct(mixw.shape, F32),
            jax.ShapeDtypeStruct((1, HID), F32),
        ),
        in_specs=[vmem] * 3,
        out_specs=(vmem,) * 5,
        compiler_params=pltpu.CompilerParams(vmem_limit_bytes=4 * 1024 * 1024),
    )(final, grad, gsum)
    return outs[0], outs[1], outs[2], outs[3], outs[4].reshape(HID)


def solution(mesh):
    sizes = dict(mesh.shape)
    assert sizes == {"rep": DYHI * DCORE, "sp": DYLO * DZ * DX}
    return jax.shard_map(
        on_device,
        mesh=mesh,
        in_specs=(
            P("rep", "sp", None),
            P("rep", "sp", None),
            P("rep", "sp", None),
            P("rep", None, None),
            P("rep", "sp", None),
            P(),
            P(),
            P(),
            P(),
            P("rep", "sp", None),
        ),
        out_specs=(P("rep", "sp", None), P("rep", "sp", None), P(), P(), P()),
        check_vma=False,
    )
```

```python
import math

import jax
import jax.numpy as jnp
from jax import lax
from jax.experimental import pallas as pl
from jax.experimental.pallas import tpu as pltpu
from jax.sharding import PartitionSpec as P

BF = jnp.bfloat16
F32 = jnp.float32
MESH = pl.DeviceIdType.MESH
SPAN = 128
ROWS = 16
HID = 64
CIN = 4
PIECES = 12
WIDTH = 256
NCLS = 4
GROUP = SPAN // ROWS
DX, DZ, DYLO, DYHI, DCORE = 4, 8, 4, 2, 2
TIME_STEP = 0.5
FAR_FIRST = (4, 3, 5, 2, 6, 1, 7)
FAR_FIRST_CORNER = (6, 2, 1, 3, 5, 7, 4)


def nt(a, b):
    return lax.dot_general(a, b, (((1,), (1,)), ((), ())), preferred_element_type=F32)


def nn(a, b):
    return lax.dot_general(a, b, (((1,), (0,)), ((), ())), preferred_element_type=F32)


def split2(v):
    hi = v.astype(BF)
    return hi, (v - hi.astype(F32)).astype(BF)


def split3(v):
    hi = v.astype(BF)
    rest = v - hi.astype(F32)
    mid = rest.astype(BF)
    return hi, mid, (rest - mid.astype(F32)).astype(BF)


def mod(a, n):
    return lax.rem(a, jnp.int32(n))


def div(a, n):
    return lax.div(a, jnp.int32(n))


EDGE = 2
ORDER = list(range(EDGE, ROWS - EDGE)) + [0, 1, ROWS - 2, ROWS - 1]
SHIFTS = list(range(ROWS - 2 * EDGE)) + [0, 1, 8, 9]
CHUNKS = ((0, 1, 2), (3,))
COUNTS = (ROWS - 2 * EDGE, 2 * EDGE)


def group_of(m):
    return 0 if m in CHUNKS[0] else 1


def chunk_rows(m):
    return slice(m * WIDTH, (m + 1) * WIDTH)


def group_part(g):
    return slice(CHUNKS[g][0] * WIDTH, (CHUNKS[g][-1] + 1) * WIDTH)


def group_rows(values, group):
    if group == 0:
        return values[EDGE : ROWS - EDGE]
    return jnp.concatenate([values[:EDGE], values[ROWS - EDGE :]], axis=0)


def iota(shape, dim):
    return lax.broadcasted_iota(jnp.int32, shape, dim)


def onehot(cond):
    return jnp.where(cond, 1.0, 0.0).astype(BF)


def span_select(products, cls_ref, store):
    for k in range(products.shape[0] // ROWS):
        column = cls_ref[0, :, k : k + 1]
        result = products[k * ROWS : (k + 1) * ROWS, 0:SPAN]
        for group in range(1, NCLS):
            part = products[k * ROWS : (k + 1) * ROWS, group * SPAN : (group + 1) * SPAN]
            result = jnp.where(column == group, part, result)
        store(k, result)


def kernel(
    film_hbm,
    evap_hbm,
    mask_hbm,
    fcls_hbm,
    scls_hbm,
    inv_hbm,
    convw_hbm,
    mixw_hbm,
    fluxw_hbm,
    cot_hbm,
    final_hbm,
    grad_hbm,
    gsum_hbm,
    film_ref,
    evap_ref,
    mask_ref,
    fcls_ref,
    scls_ref,
    inv_ref,
    convw_ref,
    mixw_ref,
    fluxw_ref,
    cot_ref,
    final_ref,
    grad_ref,
    gsum_ref,
    invs_ref,
    recv_ref,
    mid_ref,
    halo_s,
    halo_r,
    padf_ref,
    x_ref,
    wb_ref,
    wct_ref,
    bdf_ref,
    bdb_ref,
    fwb_ref,
    fwc_ref,
    a1_ref,
    d1_ref,
    sa_ref,
    u_ref,
    v_ref,
    srcf_ref,
    src_ref,
    back_ref,
    sg_ref,
    across_ref,
    cacc_ref,
    macc_ref,
    facc_ref,
    tt_ref,
    tot_ref,
    rim_s,
    rim_r,
    w36_ref,
    g_ref,
    p1_ref,
    q1_ref,
    p2_ref,
    q2_ref,
    p3_ref,
    q3_ref,
    p4_ref,
    in_sem,
    out_sem,
    ag_ssem,
    ag_rsem,
    nb_ssem,
    nb_rsem,
    ar_ssem,
    ar_rsem,
    far_sem,
):
    sp = lax.axis_index("sp")
    rep = lax.axis_index("rep")
    nsp = DYLO * DZ * DX
    has_up = sp > 0
    has_down = sp < nsp - 1
    barrier = pltpu.get_barrier_semaphore()

    def at(r, s):
        return {"rep": r, "sp": s}

    def signal(peer):
        pl.semaphore_signal(barrier, inc=1, device_id=peer, device_id_type=MESH)

    @pl.when(has_up)
    def _():
        signal(at(rep, sp - 1))

    @pl.when(has_down)
    def _():
        signal(at(rep, sp + 1))

    inputs = [
        pltpu.make_async_copy(hbm, ref, in_sem.at[n])
        for n, (hbm, ref) in enumerate(
            (
                (convw_hbm, convw_ref),
                (mixw_hbm, mixw_ref),
                (fluxw_hbm, fluxw_ref),
                (cot_hbm, cot_ref),
                (inv_hbm, inv_ref),
                (scls_hbm, scls_ref),
                (film_hbm, film_ref),
                (evap_hbm, evap_ref),
                (mask_hbm, mask_ref),
                (fcls_hbm, fcls_ref),
            )
        )
    ]
    for copy in inputs[:6]:
        copy.start()
    side = film_ref.shape[2]
    x_at = mod(sp, DX)
    z_at = mod(div(sp, DX), DZ)
    ylo_at = div(sp, DX * DZ)
    yhi_at = div(rep, DCORE)
    core_at = mod(rep, DCORE)
    y_at = yhi_at * DYLO + ylo_at
    member = mod(sp, GROUP)
    first = sp - member

    def group_peer(s):
        return at(rep, first + mod(member + s, GROUP))

    j_at = core_at * DX + x_at

    def corner_peer(s):
        other = mod(j_at + s, DCORE * DX)
        return at(yhi_at * DCORE + div(other, DX), sp - x_at + mod(other, DX))

    def z_peer(s):
        return at(rep, sp + (mod(z_at + s, DZ) - z_at) * DX)

    def y_peer(s):
        other = mod(y_at + s, DYHI * DYLO)
        return at(
            div(other, DYLO) * DCORE + core_at,
            sp + (mod(other, DYLO) - ylo_at) * DX * DZ,
        )

    peers = [group_peer(s) for s in range(1, GROUP)]
    peers += [corner_peer(s) for s in range(1, 8)]
    beside = [z_peer(1), z_peer(7), y_peer(1), y_peer(7)]
    peers += beside
    for peer in peers:
        signal(peer)
    for copy in inputs[6:]:
        copy.start()

    def remote(src, dst, ssem, rsem, peer):
        return pltpu.make_async_remote_copy(
            src_ref=src,
            dst_ref=dst,
            send_sem=ssem,
            recv_sem=rsem,
            device_id=peer,
            device_id_type=MESH,
        )

    for copy in inputs[:3]:
        copy.wait()

    w36_ref[...] = jnp.zeros_like(w36_ref)
    for a in range(3):
        for b in range(3):
            k = (a * 3 + b) * CIN
            w36_ref[k : k + CIN, 0:HID] = convw_ref[a, b].astype(F32)
    w_t = w36_ref[...].T[:HID].astype(BF)
    k_at = iota((SPAN, WIDTH), 0)
    col = iota((SPAN, WIDTH), 1)
    piece = col // 16
    tap_row = col % 16
    wanted = (tap_row * 3 + piece % 3) * CIN + piece // 3
    pick = (k_at == wanted) & (tap_row < 3) & (piece < PIECES)
    band0 = nn(w_t, onehot(pick))
    rolls = [band0 if n == 0 else pltpu.roll(band0, n, axis=1) for n in range(max(SHIFTS) + 1)]
    for m in range(4):
        band = jnp.concatenate([rolls[n] for n in SHIFTS[4 * m : 4 * m + 4]], axis=0)
        wb_ref[chunk_rows(m), :] = band.astype(BF)
        wct_ref[:, chunk_rows(m)] = band[:, :SPAN].T[:96].astype(BF)
    mix = mixw_ref[...]
    tile4 = onehot(iota((HID, WIDTH), 1) % HID == iota((HID, WIDTH), 0))
    wide = nn(mix, tile4)
    tall = jnp.concatenate([wide] * 4, axis=0)
    same = iota((WIDTH, WIDTH), 0) // HID == iota((WIDTH, WIDTH), 1) // HID
    diag = jnp.where(same, tall, 0.0)
    bdb_ref[...] = diag.astype(BF)
    bdf_ref[...] = diag.T.astype(BF)
    fw = fluxw_ref[...]
    tile8 = onehot(mod(iota((HID, 3 * WIDTH), 1), HID) == iota((HID, 3 * WIDTH), 0))
    fw_wide = nn(jnp.broadcast_to(fw, (16, HID)), tile8)
    own = div(iota((16, 3 * WIDTH), 1), HID) == iota((16, 3 * WIDTH), 0)
    fwb_ref[...] = jnp.where(own, fw_wide, 0.0).astype(BF)
    eye = iota((HID, HID), 0) == iota((HID, HID), 1)
    fw_col = jnp.sum(
        jnp.where(eye, jnp.broadcast_to(fw.astype(F32), (HID, HID)), 0.0), axis=1, keepdims=True
    )
    fwc_ref[...] = jnp.concatenate([jnp.broadcast_to(fw_col, (HID, 2 * WIDTH))] * 4, axis=0)

    for copy in inputs[3:6]:
        copy.wait()
    inv_hi, inv_lo = split2(inv_ref[...].reshape(NCLS * SPAN, SPAN))
    for c in range(NCLS):
        of = slice(c * SPAN, (c + 1) * SPAN)
        t_hi, t_lo = split2(inv_ref[c].T)
        invs_ref[0, 0, c] = t_hi
        invs_ref[0, 1, c] = t_lo
        invs_ref[1, 0, c] = inv_hi[of]
        invs_ref[1, 1, c] = inv_lo[of]

    nspan = side // SPAN
    lines = jnp.concatenate(
        [cot_ref[0, :, k * SPAN : (k + 1) * SPAN] for k in range(nspan)], axis=0
    )
    l_hi, l_lo = split2(lines)
    right_hi = jnp.concatenate([inv_hi[c * SPAN : (c + 1) * SPAN] for c in range(NCLS)], axis=1)
    right_lo = jnp.concatenate([inv_lo[c * SPAN : (c + 1) * SPAN] for c in range(NCLS)], axis=1)
    products = nn(l_hi, right_hi) + nn(l_lo, right_hi) + nn(l_hi, right_lo)

    def store_back(k, value):
        back_ref[:, k * SPAN : (k + 1) * SPAN] = value.astype(BF)

    span_select(products, scls_ref, store_back)
    own_rows = pl.ds(pl.multiple_of(member * ROWS, ROWS), ROWS)
    chunk = side // GROUP

    def columns_of(n):
        return pl.ds(pl.multiple_of(n * chunk, chunk), chunk)

    def rows_of(n):
        return pl.ds(pl.multiple_of(n * ROWS, ROWS), ROWS)

    def span_out(which, field):
        recv_ref[which, own_rows, :] = field[:, columns_of(member)]
        for s in FAR_FIRST_CORNER:
            remote(
                field.at[:, columns_of(mod(member + s, GROUP))],
                recv_ref.at[which, own_rows],
                ag_ssem.at[2 * which],
                ag_rsem.at[2 * which],
                group_peer(s),
            ).start()

    def span_solve(which, field, result):
        others = GROUP - 1
        remote(
            field.at[:, pl.ds(0, others * chunk)],
            recv_ref.at[which, pl.ds(0, others * ROWS)],
            ag_ssem.at[2 * which],
            ag_rsem.at[2 * which],
            group_peer(1),
        ).wait()
        values = recv_ref[which]
        line_cls = fcls_ref[0, :, columns_of(member)]
        own_span = iota(line_cls.shape, 0) == div(sp, GROUP)
        classes = jnp.sum(jnp.where(own_span, line_cls, 0), axis=0, keepdims=True)
        solved = None
        for c in range(NCLS):
            product = nn(invs_ref[which, 0, c], values) + nn(invs_ref[which, 1, c], values)
            solved = product if c == 0 else jnp.where(classes == c, product, solved)
        mid_ref[which] = solved.astype(BF)
        result[:, columns_of(member)] = mid_ref[which, own_rows, :]
        for s in FAR_FIRST_CORNER:
            remote(
                mid_ref.at[which, rows_of(mod(member + s, GROUP))],
                result.at[:, columns_of(member)],
                ag_ssem.at[2 * which + 1],
                ag_rsem.at[2 * which + 1],
                group_peer(s),
            ).start()

    def span_in(which, result):
        others = GROUP - 1
        remote(
            mid_ref.at[which, pl.ds(0, others * ROWS)],
            result.at[:, pl.ds(0, others * chunk)],
            ag_ssem.at[2 * which + 1],
            ag_rsem.at[2 * which + 1],
            group_peer(1),
        ).wait()

    for copy in inputs[6:]:
        copy.wait()

    film = film_ref[0]
    evap = evap_ref[0]
    maskf = mask_ref[0].astype(F32)
    features = [f.astype(BF).astype(F32) for f in (film, film * film, maskf, evap)]
    for c, feature in enumerate(features):
        padf_ref[c, 0:1, :] = jnp.zeros((1, side), F32)
        padf_ref[c, 1 : ROWS + 1, :] = feature
        padf_ref[c, ROWS + 1 :, :] = jnp.zeros((7, side), F32)
    halo_s[0] = jnp.concatenate([f[0:1] for f in features], axis=0).astype(BF)
    halo_s[1] = jnp.concatenate([f[ROWS - 1 :] for f in features], axis=0).astype(BF)

    def to_neighbours(n, sent, landed):
        upward = remote(
            sent.at[0], landed.at[1], nb_ssem.at[n, 0], nb_rsem.at[n, 0], at(rep, sp - 1)
        )
        downward = remote(
            sent.at[1], landed.at[0], nb_ssem.at[n, 1], nb_rsem.at[n, 1], at(rep, sp + 1)
        )
        return upward, downward

    def exchange_start(n, sent, landed):
        upward, downward = to_neighbours(n, sent, landed)

        @pl.when(has_up)
        def _():
            upward.start()

        @pl.when(has_down)
        def _():
            downward.start()

    def exchange_wait(n, sent, landed, use):
        upward, downward = to_neighbours(n, sent, landed)

        @pl.when(has_up)
        def _():
            upward.wait_send()
            downward.wait_recv()
            use(landed[0].astype(F32), 0)

        @pl.when(has_down)
        def _():
            downward.wait_send()
            upward.wait_recv()
            use(landed[1].astype(F32), ROWS + 1)

    wide = 2 * WIDTH
    lane = iota((24, side), 1)

    def build_pieces(g):
        for c in range(CIN):
            middle = padf_ref[c]
            left = jnp.where(lane == 0, 0.0, pltpu.roll(middle, 1, axis=1))
            right = jnp.where(lane == side - 1, 0.0, pltpu.roll(middle, side - 1, axis=1))
            for b, values in enumerate((left, middle, right)):
                s = (c * 3 + b) * 16
                if g == 0:
                    piece = values[EDGE : EDGE + 16]
                else:
                    piece = jnp.concatenate([values[0:8], values[14:22]], axis=0)
                x_ref[g, s : s + 16, :] = piece.astype(BF)

    def forward(g, blocks):
        units = [(m, n) for n in range(blocks) for m in CHUNKS[g]]

        def body(i, carry):
            factors = {}

            def cols_at(n):
                return pl.ds(pl.multiple_of((i * blocks + n) * wide, wide), wide)

            def conv(m, n):
                return nn(wb_ref[chunk_rows(m), : PIECES * 16], x_ref[g, :, cols_at(n)])

            def first_act(m, n, total):
                t1 = jnp.tanh(total)
                a1 = t1.astype(BF)
                a1_ref[chunk_rows(m), cols_at(n)] = a1
                d1_ref[units.index((m, n))] = 1.0 - t1 * t1
                return nn(bdf_ref[...], a1)

            def second_act(m, n, total):
                t2 = jnp.tanh(total)
                active = t2.astype(BF)
                sa_ref[chunk_rows(m), cols_at(n)] = active
                u = (fwc_ref[...] * (1.0 - t2 * t2)).astype(BF)
                u_ref[chunk_rows(m), cols_at(n)] = u
                factors[m, n] = active
                return nn(bdb_ref[...], u)

            def combine(m, n, total):
                v = d1_ref[units.index((m, n))] * total
                v_ref[chunk_rows(m), cols_at(n)] = v.astype(BF)

            def sources(n):
                cols = cols_at(n)
                sa = jnp.concatenate([factors[m, n] for m in CHUNKS[g]], axis=0)
                flux = nn(fwb_ref[:, : sa.shape[0]], sa)[: COUNTS[g]]
                drain = mask_ref[0, :, cols].astype(F32) * evap_ref[0, :, cols]
                rest = film_ref[0, :, cols] - TIME_STEP * drain
                source = group_rows(rest, g) + TIME_STEP * flux
                if g == 0:
                    srcf_ref[EDGE : ROWS - EDGE, cols] = source
                else:
                    srcf_ref[0:EDGE, cols] = source[:EDGE]
                    srcf_ref[ROWS - EDGE :, cols] = source[EDGE:]

            one = [conv(*unit) for unit in units[:2]]
            two, three = [], []
            for k, unit in enumerate(units):
                two.append(first_act(*unit, one[k]))
                if k + 2 < len(units):
                    one.append(conv(*units[k + 2]))
                if k >= 1:
                    three.append(second_act(*units[k - 1], two[k - 1]))
                if k >= 2:
                    combine(*units[k - 2], three[k - 2])
            three.append(second_act(*units[-1], two[-1]))
            for k in range(max(0, len(units) - 2), len(units) - 1):
                combine(*units[k], three[k])
            for n in range(blocks):
                sources(n)
            combine(*units[-1], three[-1])
            return carry

        return body

    pairs = side // wide
    build_pieces(0)

    neighbours = jnp.where(has_up, 1, 0) + jnp.where(has_down, 1, 0)
    pl.semaphore_wait(barrier, len(peers) + neighbours)
    span_out(0, back_ref)
    exchange_start(0, halo_s, halo_r)

    def tell(n):
        for peer in beside:
            pl.semaphore_signal(far_sem.at[n], inc=1, device_id=peer, device_id_type=MESH)

    def hear(n):
        pl.semaphore_wait(far_sem.at[n], len(beside))

    tell(0)

    lax.fori_loop(0, pairs - 1, forward(0, 1), 0)
    cacc_ref[...] = jnp.zeros_like(cacc_ref)
    macc_ref[...] = jnp.zeros_like(macc_ref)
    facc_ref[...] = jnp.zeros_like(facc_ref)
    span_solve(0, back_ref, sg_ref)
    lax.fori_loop(pairs - 1, pairs, forward(0, 1), 0)

    hear(0)
    tell(1)

    def set_rim(values, row):
        for c in range(CIN):
            padf_ref[c, row : row + 1, :] = values[c : c + 1]

    exchange_wait(0, halo_s, halo_r, set_rim)
    build_pieces(1)
    lax.fori_loop(0, pairs // 2, forward(1, 2), 0)
    hear(1)
    tell(2)
    src_ref[...] = srcf_ref[...].astype(BF)
    span_out(1, src_ref)
    span_in(0, sg_ref)

    def add_products(m, mixing, taps):
        macc_ref[m % 2] += mixing
        cacc_ref[chunk_rows(m), : PIECES * 16] += taps

    broad = 2 * wide

    def backward(i, carry):
        cols = pl.ds(pl.multiple_of(i * broad, broad), broad)
        flux_cots = TIME_STEP * sg_ref[:, cols].astype(F32)
        products = []
        for m in range(4):
            of = chunk_rows(m)
            rows = jnp.concatenate(
                [
                    jnp.broadcast_to(flux_cots[n : n + 1], (HID, broad)).astype(BF)
                    for n in ORDER[4 * m : 4 * m + 4]
                ],
                axis=0,
            )
            pre_first = v_ref[of, cols] * rows
            v_ref[of, cols] = pre_first
            mixing = nt(a1_ref[of, cols], u_ref[of, cols] * rows)
            taps = nt(pre_first, x_ref[group_of(m), :, cols])
            products.append((m, mixing, taps))
            if m > 0:
                add_products(*products[m - 1])
            active = (sa_ref[of, cols] * rows).astype(F32)
            part = active[:HID]
            for r in range(1, 4):
                part = part + active[r * HID : (r + 1) * HID]
            facc_ref[...] += part
        add_products(*products[-1])
        return carry

    lax.fori_loop(0, side // broad, backward, 0)

    rolled = {}
    for r, n in enumerate(SHIFTS):
        term = cacc_ref[r * HID : (r + 1) * HID]
        rolled[n] = term if n not in rolled else rolled[n] + term
    taps = jnp.zeros((HID, WIDTH), F32)
    for n, term in rolled.items():
        taps = taps + (term if n == 0 else pltpu.roll(term, WIDTH - n, axis=1))
    k_at = iota((HID, WIDTH), 0)
    col = iota((HID, WIDTH), 1)
    piece = col // 16
    tap_row = col % 16
    wanted = (tap_row * 3 + piece % 3) * CIN + piece // 3
    pick = onehot((k_at == wanted) & (tap_row < 3) & (piece < PIECES))
    low = jnp.zeros((HID, WIDTH), BF)
    right = jnp.zeros((HID, 2 * HID), F32)
    for t in split2(taps):
        right = right + nt(pick, jnp.concatenate([low, t], axis=0))
    flux_all = facc_ref[...]
    flux_lanes = flux_all[:, :SPAN]
    for n in range(1, 8):
        flux_lanes = flux_lanes + flux_all[:, n * SPAN : (n + 1) * SPAN]
    flux_row = jnp.zeros((1, 2 * HID), F32)
    ones = jnp.ones((8, SPAN), BF)
    spare_rows = jnp.zeros((HID, SPAN), BF)
    for f in split2(flux_lanes):
        flux_row = flux_row + nt(ones, jnp.concatenate([spare_rows, f], axis=0))[:1]
    right = right + jnp.where(iota((HID, 2 * HID), 0) == 9 * CIN, flux_row, 0.0)
    g_ref[...] = right
    blocks = []
    for r in range(4):
        of, at_span = slice(r * HID, (r + 1) * HID), slice((r // 2) * SPAN, (r // 2 + 1) * SPAN)
        blocks.append(macc_ref[0, of, at_span] + macc_ref[1, of, at_span])
    mixing = blocks[0] + blocks[2] + pltpu.roll(blocks[1] + blocks[3], HID, axis=1)
    g_ref[:, 0:HID] = mixing[:, 0:HID]

    own_block = pl.ds(pl.multiple_of(j_at * 8, 8), 8)
    p1_ref[j_at] = g_ref[own_block, :]
    stage1 = []
    for s in FAR_FIRST_CORNER:
        other = mod(j_at + s, 8)
        stage1.append(
            remote(
                g_ref.at[pl.ds(pl.multiple_of(other * 8, 8), 8)],
                p1_ref.at[j_at],
                ar_ssem.at[0],
                ar_rsem.at[0],
                corner_peer(s),
            )
        )
    for copy in stage1:
        copy.start()

    span_solve(1, src_ref, across_ref)

    def features_back(i, carry):
        cols = pl.ds(pl.multiple_of(i * wide, wide), wide)
        for h in range(2):
            tt_ref[h, :, cols] = nn(wct_ref[:, group_part(h)], v_ref[group_part(h), cols])
        return carry

    lax.fori_loop(0, side // wide, features_back, 0)

    def finish(stage, slots, send_peer):
        remote(
            slots.at[pl.ds(0, 7)],
            slots.at[pl.ds(0, 7)],
            ar_ssem.at[stage],
            ar_rsem.at[stage],
            send_peer(1),
        ).wait()

    def begin(stage, slots, at_index, source, send_peer):
        for s in FAR_FIRST_CORNER if stage == 3 else FAR_FIRST:
            remote(
                source,
                slots.at[at_index],
                ar_ssem.at[stage],
                ar_rsem.at[stage],
                send_peer(s),
            ).start()

    def summed(slots):
        total = slots[0]
        for n in range(1, 8):
            total = total + slots[n]
        return total

    hear(2)
    finish(0, p1_ref, corner_peer)
    q1_ref[...] = summed(p1_ref)
    p2_ref[z_at] = q1_ref[...]
    begin(1, p2_ref, z_at, q1_ref, z_peer)

    lane = iota((16, side), 1)
    for c in range(2):
        parts = []
        for h in range(2):
            s = c * 48
            left = jnp.where(lane == side - 1, 0.0, pltpu.roll(tt_ref[h, s : s + 16, :], side - 1, axis=1))
            right = jnp.where(lane == 0, 0.0, pltpu.roll(tt_ref[h, s + 32 : s + 48, :], 1, axis=1))
            parts.append(left + tt_ref[h, s + 16 : s + 32, :] + right)
        tot_ref[c, 0:8, :] = parts[1][0:8]
        tot_ref[c, 8:14, :] = jnp.zeros((6, side), F32)
        tot_ref[c, 14:22, :] = parts[1][8:16]
        tot_ref[c, 2:18, :] += parts[0]
        rim_s[0, c : c + 1, :] = parts[1][0:1]
        rim_s[1, c : c + 1, :] = parts[1][11:12]

    exchange_start(1, rim_s, rim_r)

    span_in(1, across_ref)
    pieces = [across_ref[:, k * SPAN : (k + 1) * SPAN] for k in range(nspan)]
    lines = jnp.concatenate(pieces, axis=0)
    f_hi = invs_ref[1, 0].reshape(NCLS * SPAN, SPAN)
    f_lo = invs_ref[1, 1].reshape(NCLS * SPAN, SPAN)
    products = nt(lines, f_hi) + nt(lines, f_lo)

    def store_final(k, value):
        final_ref[0, :, k * SPAN : (k + 1) * SPAN] = value

    span_select(products, scls_ref, store_final)
    final_out = pltpu.make_async_copy(final_ref, final_hbm, out_sem.at[0])
    final_out.start()

    finish(1, p2_ref, z_peer)
    q2_ref[...] = summed(p2_ref)
    p3_ref[y_at] = q2_ref[...]
    begin(2, p3_ref, y_at, q2_ref, y_peer)

    def add_rim(values, row):
        for c in range(2):
            at_row = 1 if row == 0 else ROWS
            tot_ref[c, at_row : at_row + 1, :] += values[c : c + 1]

    exchange_wait(1, rim_s, rim_r, add_rim)
    cot0 = tot_ref[0, 1 : ROWS + 1, :].astype(BF).astype(F32)
    cot1 = tot_ref[1, 1 : ROWS + 1, :].astype(BF).astype(F32)
    grad_ref[0] = sg_ref[...].astype(F32) + cot0 + 2.0 * film_ref[0] * cot1
    grad_out = pltpu.make_async_copy(grad_ref, grad_hbm, out_sem.at[1])
    grad_out.start()

    finish(2, p3_ref, y_peer)
    q3_ref[...] = summed(p3_ref)
    p4_ref[j_at] = q3_ref[...]
    begin(3, p4_ref, j_at, q3_ref, corner_peer)
    finish(3, p4_ref, corner_peer)
    scale = 1.0 / math.sqrt(DYHI * DCORE * side * side)
    gsum_ref[...] = p4_ref[...].reshape(HID, 2 * HID) * scale
    gsum_out = pltpu.make_async_copy(gsum_ref, gsum_hbm, out_sem.at[2])
    gsum_out.start()
    final_out.wait()
    grad_out.wait()
    gsum_out.wait()


def hand_out(final_in, grad_in, gsum_in, final_ref, grad_ref, convg_ref, mixg_ref, fluxg_ref):
    final_ref[...] = final_in[...]
    grad_ref[...] = grad_in[...]
    result = gsum_in[...]
    mixg_ref[...] = result[:, :HID]
    other = pltpu.roll(result, HID, axis=1)[:, :HID]
    for a in range(3):
        for b in range(3):
            k = (a * 3 + b) * CIN
            convg_ref[a, b] = other[k : k + CIN]
    fluxg_ref[...] = other[9 * CIN : 9 * CIN + 1]


def on_device(film, evap, mask, fcls, scls, inv, convw, mixw, fluxw, cot):
    side = film.shape[2]
    rows = film.shape[1]
    vmem = pl.BlockSpec(memory_space=pltpu.VMEM)
    hbm = pl.BlockSpec(memory_space=pltpu.HBM)
    free = pl.BlockSpec(memory_space=pl.ANY)
    args = (
        film,
        evap,
        mask,
        jnp.swapaxes(fcls, 1, 2),
        scls,
        inv,
        convw,
        mixw,
        fluxw.reshape(1, HID),
        cot,
    )
    args = tuple(pltpu.with_memory_space_constraint(a, pltpu.HBM) for a in args)
    chunk = side // GROUP
    tall = ROWS * HID
    slab = jax.ShapeDtypeStruct(film.shape, F32)
    block = jax.ShapeDtypeStruct((HID, 2 * HID), F32)
    final, grad, gsum = pl.pallas_call(
        kernel,
        out_shape=(slab, slab, block),
        in_specs=[hbm] * 10,
        out_specs=(free,) * 3,
        scratch_shapes=[pltpu.VMEM(a.shape, a.dtype) for a in args]
        + [
            pltpu.VMEM(film.shape, F32),
            pltpu.VMEM(film.shape, F32),
            pltpu.VMEM((HID, 2 * HID), F32),
            pltpu.VMEM((2, 2, NCLS, SPAN, SPAN), BF),
            pltpu.VMEM((2, SPAN, chunk), BF),
            pltpu.VMEM((2, SPAN, chunk), BF),
            pltpu.VMEM((2, CIN, side), BF),
            pltpu.VMEM((2, CIN, side), BF),
            pltpu.VMEM((CIN, 24, side), F32),
            pltpu.VMEM((2, PIECES * 16, side), BF),
            pltpu.VMEM((tall, WIDTH), BF),
            pltpu.VMEM((96, tall), BF),
            pltpu.VMEM((WIDTH, WIDTH), BF),
            pltpu.VMEM((WIDTH, WIDTH), BF),
            pltpu.VMEM((16, 3 * WIDTH), BF),
            pltpu.VMEM((WIDTH, 2 * WIDTH), F32),
            pltpu.VMEM((tall, side), BF),
            pltpu.VMEM((3, WIDTH, 2 * WIDTH), F32),
            pltpu.VMEM((tall, side), BF),
            pltpu.VMEM((tall, side), BF),
            pltpu.VMEM((tall, side), BF),
            pltpu.VMEM((rows, side), F32),
            pltpu.VMEM((rows, side), BF),
            pltpu.VMEM((rows, side), BF),
            pltpu.VMEM((rows, side), BF),
            pltpu.VMEM((rows, side), BF),
            pltpu.VMEM((tall, WIDTH), F32),
            pltpu.VMEM((2, WIDTH, WIDTH), F32),
            pltpu.VMEM((HID, 4 * WIDTH), F32),
            pltpu.VMEM((2, 96, side), F32),
            pltpu.VMEM((2, 24, side), F32),
            pltpu.VMEM((2, 2, side), F32),
            pltpu.VMEM((2, 2, side), F32),
            pltpu.VMEM((SPAN, SPAN), F32),
            pltpu.VMEM((HID, 2 * HID), F32),
            pltpu.VMEM((8, 8, 2 * HID), F32),
            pltpu.VMEM((8, 2 * HID), F32),
            pltpu.VMEM((8, 8, 2 * HID), F32),
            pltpu.VMEM((8, 2 * HID), F32),
            pltpu.VMEM((8, 8, 2 * HID), F32),
            pltpu.VMEM((8, 2 * HID), F32),
            pltpu.VMEM((8, 8, 2 * HID), F32),
            pltpu.SemaphoreType.DMA((10,)),
            pltpu.SemaphoreType.DMA((3,)),
            pltpu.SemaphoreType.DMA((4,)),
            pltpu.SemaphoreType.DMA((4,)),
            pltpu.SemaphoreType.DMA((2, 2)),
            pltpu.SemaphoreType.DMA((2, 2)),
            pltpu.SemaphoreType.DMA((4,)),
            pltpu.SemaphoreType.DMA((4,)),
            pltpu.SemaphoreType.REGULAR((3,)),
        ],
        compiler_params=pltpu.CompilerParams(
            collective_id=0, has_side_effects=True, vmem_limit_bytes=48 * 1024 * 1024
        ),
    )(*args)
    outs = pl.pallas_call(
        hand_out,
        out_shape=(
            slab,
            slab,
            jax.ShapeDtypeStruct(convw.shape, F32),
            jax.ShapeDtypeStruct(mixw.shape, F32),
            jax.ShapeDtypeStruct((1, HID), F32),
        ),
        in_specs=[vmem] * 3,
        out_specs=(vmem,) * 5,
        compiler_params=pltpu.CompilerParams(vmem_limit_bytes=4 * 1024 * 1024),
    )(final, grad, gsum)
    return outs[0], outs[1], outs[2], outs[3], outs[4].reshape(HID)


def solution(mesh):
    sizes = dict(mesh.shape)
    assert sizes == {"rep": DYHI * DCORE, "sp": DYLO * DZ * DX}
    return jax.shard_map(
        on_device,
        mesh=mesh,
        in_specs=(
            P("rep", "sp", None),
            P("rep", "sp", None),
            P("rep", "sp", None),
            P("rep", None, None),
            P("rep", "sp", None),
            P(),
            P(),
            P(),
            P(),
            P("rep", "sp", None),
        ),
        out_specs=(P("rep", "sp", None), P("rep", "sp", None), P(), P(), P()),
        check_vma=False,
    )
```

```python
import math

import jax
import jax.numpy as jnp
from jax import lax
from jax.experimental import pallas as pl
from jax.experimental.pallas import tpu as pltpu
from jax.sharding import PartitionSpec as P

BF = jnp.bfloat16
F32 = jnp.float32
MESH = pl.DeviceIdType.MESH
SPAN = 128
ROWS = 16
HID = 64
CIN = 4
PIECES = 12
WIDTH = 256
NCLS = 4
GROUP = SPAN // ROWS
DX, DZ, DYLO, DYHI, DCORE = 4, 8, 4, 2, 2
TIME_STEP = 0.5
FAR_FIRST = (4, 3, 5, 2, 6, 1, 7)
FAR_FIRST_CORNER = (6, 2, 1, 3, 5, 7, 4)


def nt(a, b):
    return lax.dot_general(a, b, (((1,), (1,)), ((), ())), preferred_element_type=F32)


def nn(a, b):
    return lax.dot_general(a, b, (((1,), (0,)), ((), ())), preferred_element_type=F32)


def split2(v):
    hi = v.astype(BF)
    return hi, (v - hi.astype(F32)).astype(BF)


def split3(v):
    hi = v.astype(BF)
    rest = v - hi.astype(F32)
    mid = rest.astype(BF)
    return hi, mid, (rest - mid.astype(F32)).astype(BF)


def mod(a, n):
    return lax.rem(a, jnp.int32(n))


def div(a, n):
    return lax.div(a, jnp.int32(n))


EDGE = 2
ORDER = list(range(EDGE, ROWS - EDGE)) + [0, 1, ROWS - 2, ROWS - 1]
SHIFTS = list(range(ROWS - 2 * EDGE)) + [0, 1, 8, 9]
CHUNKS = ((0, 1, 2), (3,))
COUNTS = (ROWS - 2 * EDGE, 2 * EDGE)


def group_of(m):
    return 0 if m in CHUNKS[0] else 1


def chunk_rows(m):
    return slice(m * WIDTH, (m + 1) * WIDTH)


def group_part(g):
    return slice(CHUNKS[g][0] * WIDTH, (CHUNKS[g][-1] + 1) * WIDTH)


def group_rows(values, group):
    if group == 0:
        return values[EDGE : ROWS - EDGE]
    return jnp.concatenate([values[:EDGE], values[ROWS - EDGE :]], axis=0)


def iota(shape, dim):
    return lax.broadcasted_iota(jnp.int32, shape, dim)


def onehot(cond):
    return jnp.where(cond, 1.0, 0.0).astype(BF)


def span_select(products, cls_ref, store):
    for k in range(products.shape[0] // ROWS):
        column = cls_ref[0, :, k : k + 1]
        result = products[k * ROWS : (k + 1) * ROWS, 0:SPAN]
        for group in range(1, NCLS):
            part = products[k * ROWS : (k + 1) * ROWS, group * SPAN : (group + 1) * SPAN]
            result = jnp.where(column == group, part, result)
        store(k, result)


def kernel(
    film_hbm,
    evap_hbm,
    mask_hbm,
    fcls_hbm,
    scls_hbm,
    inv_hbm,
    convw_hbm,
    mixw_hbm,
    fluxw_hbm,
    cot_hbm,
    final_hbm,
    grad_hbm,
    gsum_hbm,
    film_ref,
    evap_ref,
    mask_ref,
    fcls_ref,
    scls_ref,
    inv_ref,
    convw_ref,
    mixw_ref,
    fluxw_ref,
    cot_ref,
    final_ref,
    grad_ref,
    gsum_ref,
    invs_ref,
    recv_ref,
    mid_ref,
    halo_s,
    halo_r,
    padf_ref,
    x_ref,
    wb_ref,
    wct_ref,
    bdf_ref,
    bdb_ref,
    fwb_ref,
    fwc_ref,
    a1_ref,
    d1_ref,
    sa_ref,
    u_ref,
    v_ref,
    srcf_ref,
    src_ref,
    back_ref,
    sg_ref,
    across_ref,
    cacc_ref,
    macc_ref,
    facc_ref,
    tt_ref,
    tot_ref,
    rim_s,
    rim_r,
    w36_ref,
    g_ref,
    p1_ref,
    q1_ref,
    p2_ref,
    q2_ref,
    p3_ref,
    q3_ref,
    p4_ref,
    in_sem,
    out_sem,
    ag_ssem,
    ag_rsem,
    nb_ssem,
    nb_rsem,
    ar_ssem,
    ar_rsem,
    far_sem,
):
    sp = lax.axis_index("sp")
    rep = lax.axis_index("rep")
    nsp = DYLO * DZ * DX
    has_up = sp > 0
    has_down = sp < nsp - 1
    barrier = pltpu.get_barrier_semaphore()

    def at(r, s):
        return {"rep": r, "sp": s}

    def signal(peer):
        pl.semaphore_signal(barrier, inc=1, device_id=peer, device_id_type=MESH)

    @pl.when(has_up)
    def _():
        signal(at(rep, sp - 1))

    @pl.when(has_down)
    def _():
        signal(at(rep, sp + 1))

    inputs = [
        pltpu.make_async_copy(hbm, ref, in_sem.at[n])
        for n, (hbm, ref) in enumerate(
            (
                (convw_hbm, convw_ref),
                (mixw_hbm, mixw_ref),
                (fluxw_hbm, fluxw_ref),
                (cot_hbm, cot_ref),
                (inv_hbm, inv_ref),
                (scls_hbm, scls_ref),
                (film_hbm, film_ref),
                (evap_hbm, evap_ref),
                (mask_hbm, mask_ref),
                (fcls_hbm, fcls_ref),
            )
        )
    ]
    side = film_ref.shape[2]
    x_at = mod(sp, DX)
    z_at = mod(div(sp, DX), DZ)
    ylo_at = div(sp, DX * DZ)
    yhi_at = div(rep, DCORE)
    core_at = mod(rep, DCORE)
    y_at = yhi_at * DYLO + ylo_at
    member = mod(sp, GROUP)
    first = sp - member

    def group_peer(s):
        return at(rep, first + mod(member + s, GROUP))

    j_at = core_at * DX + x_at

    def corner_peer(s):
        other = mod(j_at + s, DCORE * DX)
        return at(yhi_at * DCORE + div(other, DX), sp - x_at + mod(other, DX))

    def z_peer(s):
        return at(rep, sp + (mod(z_at + s, DZ) - z_at) * DX)

    def y_peer(s):
        other = mod(y_at + s, DYHI * DYLO)
        return at(
            div(other, DYLO) * DCORE + core_at,
            sp + (mod(other, DYLO) - ylo_at) * DX * DZ,
        )

    peers = [group_peer(s) for s in range(1, GROUP)]
    peers += [corner_peer(s) for s in range(1, 8)]
    beside = [z_peer(1), z_peer(7), y_peer(1), y_peer(7)]
    peers += beside
    for peer in peers:
        signal(peer)
    for copy in inputs:
        copy.start()

    def remote(src, dst, ssem, rsem, peer):
        return pltpu.make_async_remote_copy(
            src_ref=src,
            dst_ref=dst,
            send_sem=ssem,
            recv_sem=rsem,
            device_id=peer,
            device_id_type=MESH,
        )

    for copy in inputs[:3]:
        copy.wait()

    w36_ref[...] = jnp.zeros_like(w36_ref)
    for a in range(3):
        for b in range(3):
            k = (a * 3 + b) * CIN
            w36_ref[k : k + CIN, 0:HID] = convw_ref[a, b].astype(F32)
    w_t = w36_ref[...].T[:HID].astype(BF)
    k_at = iota((SPAN, WIDTH), 0)
    col = iota((SPAN, WIDTH), 1)
    piece = col // 16
    tap_row = col % 16
    wanted = (tap_row * 3 + piece % 3) * CIN + piece // 3
    pick = (k_at == wanted) & (tap_row < 3) & (piece < PIECES)
    band0 = nn(w_t, onehot(pick))
    rolls = [band0 if n == 0 else pltpu.roll(band0, n, axis=1) for n in range(max(SHIFTS) + 1)]
    for m in range(4):
        band = jnp.concatenate([rolls[n] for n in SHIFTS[4 * m : 4 * m + 4]], axis=0)
        wb_ref[chunk_rows(m), :] = band.astype(BF)
        wct_ref[:, chunk_rows(m)] = band[:, :SPAN].T[:96].astype(BF)
    mix = mixw_ref[...]
    tile4 = onehot(iota((HID, WIDTH), 1) % HID == iota((HID, WIDTH), 0))
    wide = nn(mix, tile4)
    tall = jnp.concatenate([wide] * 4, axis=0)
    same = iota((WIDTH, WIDTH), 0) // HID == iota((WIDTH, WIDTH), 1) // HID
    diag = jnp.where(same, tall, 0.0)
    bdb_ref[...] = diag.astype(BF)
    bdf_ref[...] = diag.T.astype(BF)
    fw = fluxw_ref[...]
    tile8 = onehot(mod(iota((HID, 3 * WIDTH), 1), HID) == iota((HID, 3 * WIDTH), 0))
    fw_wide = nn(jnp.broadcast_to(fw, (16, HID)), tile8)
    own = div(iota((16, 3 * WIDTH), 1), HID) == iota((16, 3 * WIDTH), 0)
    fwb_ref[...] = jnp.where(own, fw_wide, 0.0).astype(BF)
    eye = iota((HID, HID), 0) == iota((HID, HID), 1)
    fw_col = jnp.sum(
        jnp.where(eye, jnp.broadcast_to(fw.astype(F32), (HID, HID)), 0.0), axis=1, keepdims=True
    )
    fwc_ref[...] = jnp.concatenate([jnp.broadcast_to(fw_col, (HID, 2 * WIDTH))] * 4, axis=0)

    for copy in inputs[3:6]:
        copy.wait()
    inv_hi, inv_lo = split2(inv_ref[...].reshape(NCLS * SPAN, SPAN))
    for c in range(NCLS):
        of = slice(c * SPAN, (c + 1) * SPAN)
        t_hi, t_lo = split2(inv_ref[c].T)
        invs_ref[0, 0, c] = t_hi
        invs_ref[0, 1, c] = t_lo
        invs_ref[1, 0, c] = inv_hi[of]
        invs_ref[1, 1, c] = inv_lo[of]

    nspan = side // SPAN
    lines = jnp.concatenate(
        [cot_ref[0, :, k * SPAN : (k + 1) * SPAN] for k in range(nspan)], axis=0
    )
    l_hi, l_lo = split2(lines)
    right_hi = jnp.concatenate([inv_hi[c * SPAN : (c + 1) * SPAN] for c in range(NCLS)], axis=1)
    right_lo = jnp.concatenate([inv_lo[c * SPAN : (c + 1) * SPAN] for c in range(NCLS)], axis=1)
    products = nn(l_hi, right_hi) + nn(l_lo, right_hi) + nn(l_hi, right_lo)

    def store_back(k, value):
        back_ref[:, k * SPAN : (k + 1) * SPAN] = value.astype(BF)

    span_select(products, scls_ref, store_back)
    own_rows = pl.ds(pl.multiple_of(member * ROWS, ROWS), ROWS)
    chunk = side // GROUP

    def columns_of(n):
        return pl.ds(pl.multiple_of(n * chunk, chunk), chunk)

    def rows_of(n):
        return pl.ds(pl.multiple_of(n * ROWS, ROWS), ROWS)

    def span_out(which, field):
        recv_ref[which, own_rows, :] = field[:, columns_of(member)]
        for s in FAR_FIRST_CORNER:
            remote(
                field.at[:, columns_of(mod(member + s, GROUP))],
                recv_ref.at[which, own_rows],
                ag_ssem.at[2 * which],
                ag_rsem.at[2 * which],
                group_peer(s),
            ).start()

    def span_solve(which, field, result):
        others = GROUP - 1
        remote(
            field.at[:, pl.ds(0, others * chunk)],
            recv_ref.at[which, pl.ds(0, others * ROWS)],
            ag_ssem.at[2 * which],
            ag_rsem.at[2 * which],
            group_peer(1),
        ).wait()
        values = recv_ref[which]
        line_cls = fcls_ref[0, :, columns_of(member)]
        own_span = iota(line_cls.shape, 0) == div(sp, GROUP)
        classes = jnp.sum(jnp.where(own_span, line_cls, 0), axis=0, keepdims=True)
        solved = None
        for c in range(NCLS):
            product = nn(invs_ref[which, 0, c], values) + nn(invs_ref[which, 1, c], values)
            solved = product if c == 0 else jnp.where(classes == c, product, solved)
        mid_ref[which] = solved.astype(BF)
        result[:, columns_of(member)] = mid_ref[which, own_rows, :]
        for s in FAR_FIRST_CORNER:
            remote(
                mid_ref.at[which, rows_of(mod(member + s, GROUP))],
                result.at[:, columns_of(member)],
                ag_ssem.at[2 * which + 1],
                ag_rsem.at[2 * which + 1],
                group_peer(s),
            ).start()

    def span_in(which, result):
        others = GROUP - 1
        remote(
            mid_ref.at[which, pl.ds(0, others * ROWS)],
            result.at[:, pl.ds(0, others * chunk)],
            ag_ssem.at[2 * which + 1],
            ag_rsem.at[2 * which + 1],
            group_peer(1),
        ).wait()

    for copy in inputs[6:]:
        copy.wait()

    film = film_ref[0]
    evap = evap_ref[0]
    maskf = mask_ref[0].astype(F32)
    features = [f.astype(BF).astype(F32) for f in (film, film * film, maskf, evap)]
    for c, feature in enumerate(features):
        padf_ref[c, 0:1, :] = jnp.zeros((1, side), F32)
        padf_ref[c, 1 : ROWS + 1, :] = feature
        padf_ref[c, ROWS + 1 :, :] = jnp.zeros((7, side), F32)
    halo_s[0] = jnp.concatenate([f[0:1] for f in features], axis=0).astype(BF)
    halo_s[1] = jnp.concatenate([f[ROWS - 1 :] for f in features], axis=0).astype(BF)

    def to_neighbours(n, sent, landed):
        upward = remote(
            sent.at[0], landed.at[1], nb_ssem.at[n, 0], nb_rsem.at[n, 0], at(rep, sp - 1)
        )
        downward = remote(
            sent.at[1], landed.at[0], nb_ssem.at[n, 1], nb_rsem.at[n, 1], at(rep, sp + 1)
        )
        return upward, downward

    def exchange_start(n, sent, landed):
        upward, downward = to_neighbours(n, sent, landed)

        @pl.when(has_up)
        def _():
            upward.start()

        @pl.when(has_down)
        def _():
            downward.start()

    def exchange_wait(n, sent, landed, use):
        upward, downward = to_neighbours(n, sent, landed)

        @pl.when(has_up)
        def _():
            upward.wait_send()
            downward.wait_recv()
            use(landed[0].astype(F32), 0)

        @pl.when(has_down)
        def _():
            downward.wait_send()
            upward.wait_recv()
            use(landed[1].astype(F32), ROWS + 1)

    wide = 2 * WIDTH
    lane = iota((24, side), 1)

    def build_pieces(g):
        for c in range(CIN):
            middle = padf_ref[c]
            left = jnp.where(lane == 0, 0.0, pltpu.roll(middle, 1, axis=1))
            right = jnp.where(lane == side - 1, 0.0, pltpu.roll(middle, side - 1, axis=1))
            for b, values in enumerate((left, middle, right)):
                s = (c * 3 + b) * 16
                if g == 0:
                    piece = values[EDGE : EDGE + 16]
                else:
                    piece = jnp.concatenate([values[0:8], values[14:22]], axis=0)
                x_ref[g, s : s + 16, :] = piece.astype(BF)

    def forward(g, blocks):
        units = [(m, n) for n in range(blocks) for m in CHUNKS[g]]

        def body(i, carry):
            factors = {}

            def cols_at(n):
                return pl.ds(pl.multiple_of((i * blocks + n) * wide, wide), wide)

            def conv(m, n):
                return nn(wb_ref[chunk_rows(m), : PIECES * 16], x_ref[g, :, cols_at(n)])

            def first_act(m, n, total):
                t1 = jnp.tanh(total)
                a1 = t1.astype(BF)
                a1_ref[chunk_rows(m), cols_at(n)] = a1
                d1_ref[units.index((m, n))] = 1.0 - t1 * t1
                return nn(bdf_ref[...], a1)

            def second_act(m, n, total):
                t2 = jnp.tanh(total)
                active = t2.astype(BF)
                sa_ref[chunk_rows(m), cols_at(n)] = active
                u = (fwc_ref[...] * (1.0 - t2 * t2)).astype(BF)
                u_ref[chunk_rows(m), cols_at(n)] = u
                factors[m, n] = active
                return nn(bdb_ref[...], u)

            def combine(m, n, total):
                v = d1_ref[units.index((m, n))] * total
                v_ref[chunk_rows(m), cols_at(n)] = v.astype(BF)

            def sources(n):
                cols = cols_at(n)
                sa = jnp.concatenate([factors[m, n] for m in CHUNKS[g]], axis=0)
                flux = nn(fwb_ref[:, : sa.shape[0]], sa)[: COUNTS[g]]
                drain = mask_ref[0, :, cols].astype(F32) * evap_ref[0, :, cols]
                rest = film_ref[0, :, cols] - TIME_STEP * drain
                source = group_rows(rest, g) + TIME_STEP * flux
                if g == 0:
                    srcf_ref[EDGE : ROWS - EDGE, cols] = source
                else:
                    srcf_ref[0:EDGE, cols] = source[:EDGE]
                    srcf_ref[ROWS - EDGE :, cols] = source[EDGE:]

            one = [conv(*unit) for unit in units[:2]]
            two, three = [], []
            for k, unit in enumerate(units):
                two.append(first_act(*unit, one[k]))
                if k + 2 < len(units):
                    one.append(conv(*units[k + 2]))
                if k >= 1:
                    three.append(second_act(*units[k - 1], two[k - 1]))
                if k >= 2:
                    combine(*units[k - 2], three[k - 2])
            three.append(second_act(*units[-1], two[-1]))
            for k in range(max(0, len(units) - 2), len(units) - 1):
                combine(*units[k], three[k])
            for n in range(blocks):
                sources(n)
            combine(*units[-1], three[-1])
            return carry

        return body

    pairs = side // wide
    build_pieces(0)

    neighbours = jnp.where(has_up, 1, 0) + jnp.where(has_down, 1, 0)
    pl.semaphore_wait(barrier, len(peers) + neighbours)
    span_out(0, back_ref)
    exchange_start(0, halo_s, halo_r)

    def tell(n):
        for peer in beside:
            pl.semaphore_signal(far_sem.at[n], inc=1, device_id=peer, device_id_type=MESH)

    def hear(n):
        pl.semaphore_wait(far_sem.at[n], len(beside))

    tell(0)

    lax.fori_loop(0, pairs - 1, forward(0, 1), 0)
    cacc_ref[...] = jnp.zeros_like(cacc_ref)
    macc_ref[...] = jnp.zeros_like(macc_ref)
    facc_ref[...] = jnp.zeros_like(facc_ref)
    span_solve(0, back_ref, sg_ref)
    lax.fori_loop(pairs - 1, pairs, forward(0, 1), 0)

    hear(0)
    tell(1)

    def set_rim(values, row):
        for c in range(CIN):
            padf_ref[c, row : row + 1, :] = values[c : c + 1]

    exchange_wait(0, halo_s, halo_r, set_rim)
    build_pieces(1)
    lax.fori_loop(0, pairs // 2, forward(1, 2), 0)
    hear(1)
    tell(2)
    src_ref[...] = srcf_ref[...].astype(BF)
    span_out(1, src_ref)
    span_in(0, sg_ref)

    def add_products(m, mixing, taps):
        macc_ref[m % 2] += mixing
        cacc_ref[chunk_rows(m), : PIECES * 16] += taps

    broad = 2 * wide

    def backward(i, carry):
        cols = pl.ds(pl.multiple_of(i * broad, broad), broad)
        flux_cots = TIME_STEP * sg_ref[:, cols].astype(F32)
        products = []
        for m in range(4):
            of = chunk_rows(m)
            rows = jnp.concatenate(
                [
                    jnp.broadcast_to(flux_cots[n : n + 1], (HID, broad)).astype(BF)
                    for n in ORDER[4 * m : 4 * m + 4]
                ],
                axis=0,
            )
            pre_first = v_ref[of, cols] * rows
            v_ref[of, cols] = pre_first
            mixing = nt(a1_ref[of, cols], u_ref[of, cols] * rows)
            taps = nt(pre_first, x_ref[group_of(m), :, cols])
            products.append((m, mixing, taps))
            if m > 0:
                add_products(*products[m - 1])
            active = (sa_ref[of, cols] * rows).astype(F32)
            part = active[:HID]
            for r in range(1, 4):
                part = part + active[r * HID : (r + 1) * HID]
            facc_ref[...] += part
        add_products(*products[-1])
        return carry

    lax.fori_loop(0, side // broad, backward, 0)

    rolled = {}
    for r, n in enumerate(SHIFTS):
        term = cacc_ref[r * HID : (r + 1) * HID]
        rolled[n] = term if n not in rolled else rolled[n] + term
    taps = jnp.zeros((HID, WIDTH), F32)
    for n, term in rolled.items():
        taps = taps + (term if n == 0 else pltpu.roll(term, WIDTH - n, axis=1))
    k_at = iota((HID, WIDTH), 0)
    col = iota((HID, WIDTH), 1)
    piece = col // 16
    tap_row = col % 16
    wanted = (tap_row * 3 + piece % 3) * CIN + piece // 3
    pick = onehot((k_at == wanted) & (tap_row < 3) & (piece < PIECES))
    low = jnp.zeros((HID, WIDTH), BF)
    right = jnp.zeros((HID, 2 * HID), F32)
    for t in split2(taps):
        right = right + nt(pick, jnp.concatenate([low, t], axis=0))
    flux_all = facc_ref[...]
    flux_lanes = flux_all[:, :SPAN]
    for n in range(1, 8):
        flux_lanes = flux_lanes + flux_all[:, n * SPAN : (n + 1) * SPAN]
    flux_row = jnp.zeros((1, 2 * HID), F32)
    ones = jnp.ones((8, SPAN), BF)
    spare_rows = jnp.zeros((HID, SPAN), BF)
    for f in split2(flux_lanes):
        flux_row = flux_row + nt(ones, jnp.concatenate([spare_rows, f], axis=0))[:1]
    right = right + jnp.where(iota((HID, 2 * HID), 0) == 9 * CIN, flux_row, 0.0)
    g_ref[...] = right
    blocks = []
    for r in range(4):
        of, at_span = slice(r * HID, (r + 1) * HID), slice((r // 2) * SPAN, (r // 2 + 1) * SPAN)
        blocks.append(macc_ref[0, of, at_span] + macc_ref[1, of, at_span])
    mixing = blocks[0] + blocks[2] + pltpu.roll(blocks[1] + blocks[3], HID, axis=1)
    g_ref[:, 0:HID] = mixing[:, 0:HID]

    own_block = pl.ds(pl.multiple_of(j_at * 8, 8), 8)
    stage1 = []
    for s in FAR_FIRST_CORNER:
        other = mod(j_at + s, 8)
        stage1.append(
            remote(
                g_ref.at[pl.ds(pl.multiple_of(other * 8, 8), 8)],
                p1_ref.at[j_at],
                ar_ssem.at[0],
                ar_rsem.at[0],
                corner_peer(s),
            )
        )
    for copy in stage1:
        copy.start()
    p1_ref[j_at] = g_ref[own_block, :]

    span_solve(1, src_ref, across_ref)

    def features_back(i, carry):
        cols = pl.ds(pl.multiple_of(i * wide, wide), wide)
        for h in range(2):
            tt_ref[h, :, cols] = nn(wct_ref[:, group_part(h)], v_ref[group_part(h), cols])
        return carry

    lax.fori_loop(0, side // wide, features_back, 0)

    def finish(stage, slots, send_peer):
        remote(
            slots.at[pl.ds(0, 7)],
            slots.at[pl.ds(0, 7)],
            ar_ssem.at[stage],
            ar_rsem.at[stage],
            send_peer(1),
        ).wait()

    def begin(stage, slots, at_index, source, send_peer):
        for s in FAR_FIRST_CORNER if stage == 3 else FAR_FIRST:
            remote(
                source,
                slots.at[at_index],
                ar_ssem.at[stage],
                ar_rsem.at[stage],
                send_peer(s),
            ).start()

    def summed(slots):
        total = slots[0]
        for n in range(1, 8):
            total = total + slots[n]
        return total

    hear(2)
    finish(0, p1_ref, corner_peer)
    q1_ref[...] = summed(p1_ref)
    begin(1, p2_ref, z_at, q1_ref, z_peer)
    p2_ref[z_at] = q1_ref[...]

    lane = iota((16, side), 1)
    for c in range(2):
        parts = []
        for h in range(2):
            s = c * 48
            left = jnp.where(lane == side - 1, 0.0, pltpu.roll(tt_ref[h, s : s + 16, :], side - 1, axis=1))
            right = jnp.where(lane == 0, 0.0, pltpu.roll(tt_ref[h, s + 32 : s + 48, :], 1, axis=1))
            parts.append(left + tt_ref[h, s + 16 : s + 32, :] + right)
        tot_ref[c, 0:8, :] = parts[1][0:8]
        tot_ref[c, 8:14, :] = jnp.zeros((6, side), F32)
        tot_ref[c, 14:22, :] = parts[1][8:16]
        tot_ref[c, 2:18, :] += parts[0]
        rim_s[0, c : c + 1, :] = parts[1][0:1]
        rim_s[1, c : c + 1, :] = parts[1][11:12]

    exchange_start(1, rim_s, rim_r)

    span_in(1, across_ref)
    pieces = [across_ref[:, k * SPAN : (k + 1) * SPAN] for k in range(nspan)]
    lines = jnp.concatenate(pieces, axis=0)
    f_hi = invs_ref[1, 0].reshape(NCLS * SPAN, SPAN)
    f_lo = invs_ref[1, 1].reshape(NCLS * SPAN, SPAN)
    products = nt(lines, f_hi) + nt(lines, f_lo)

    def store_final(k, value):
        final_ref[0, :, k * SPAN : (k + 1) * SPAN] = value

    span_select(products, scls_ref, store_final)
    final_out = pltpu.make_async_copy(final_ref, final_hbm, out_sem.at[0])
    final_out.start()

    finish(1, p2_ref, z_peer)
    q2_ref[...] = summed(p2_ref)
    begin(2, p3_ref, y_at, q2_ref, y_peer)
    p3_ref[y_at] = q2_ref[...]

    def add_rim(values, row):
        for c in range(2):
            at_row = 1 if row == 0 else ROWS
            tot_ref[c, at_row : at_row + 1, :] += values[c : c + 1]

    exchange_wait(1, rim_s, rim_r, add_rim)
    cot0 = tot_ref[0, 1 : ROWS + 1, :].astype(BF).astype(F32)
    cot1 = tot_ref[1, 1 : ROWS + 1, :].astype(BF).astype(F32)
    grad_ref[0] = sg_ref[...].astype(F32) + cot0 + 2.0 * film_ref[0] * cot1
    grad_out = pltpu.make_async_copy(grad_ref, grad_hbm, out_sem.at[1])
    grad_out.start()

    finish(2, p3_ref, y_peer)
    q3_ref[...] = summed(p3_ref)
    begin(3, p4_ref, j_at, q3_ref, corner_peer)
    p4_ref[j_at] = q3_ref[...]
    finish(3, p4_ref, corner_peer)
    scale = 1.0 / math.sqrt(DYHI * DCORE * side * side)
    gsum_ref[...] = p4_ref[...].reshape(HID, 2 * HID) * scale
    gsum_out = pltpu.make_async_copy(gsum_ref, gsum_hbm, out_sem.at[2])
    gsum_out.start()
    final_out.wait()
    grad_out.wait()
    gsum_out.wait()


def hand_out(final_in, grad_in, gsum_in, final_ref, grad_ref, convg_ref, mixg_ref, fluxg_ref):
    final_ref[...] = final_in[...]
    grad_ref[...] = grad_in[...]
    result = gsum_in[...]
    mixg_ref[...] = result[:, :HID]
    other = pltpu.roll(result, HID, axis=1)[:, :HID]
    for a in range(3):
        for b in range(3):
            k = (a * 3 + b) * CIN
            convg_ref[a, b] = other[k : k + CIN]
    fluxg_ref[...] = other[9 * CIN : 9 * CIN + 1]


def on_device(film, evap, mask, fcls, scls, inv, convw, mixw, fluxw, cot):
    side = film.shape[2]
    rows = film.shape[1]
    vmem = pl.BlockSpec(memory_space=pltpu.VMEM)
    hbm = pl.BlockSpec(memory_space=pltpu.HBM)
    free = pl.BlockSpec(memory_space=pl.ANY)
    args = (
        film,
        evap,
        mask,
        jnp.swapaxes(fcls, 1, 2),
        scls,
        inv,
        convw,
        mixw,
        fluxw.reshape(1, HID),
        cot,
    )
    args = tuple(pltpu.with_memory_space_constraint(a, pltpu.HBM) for a in args)
    chunk = side // GROUP
    tall = ROWS * HID
    slab = jax.ShapeDtypeStruct(film.shape, F32)
    block = jax.ShapeDtypeStruct((HID, 2 * HID), F32)
    final, grad, gsum = pl.pallas_call(
        kernel,
        out_shape=(slab, slab, block),
        in_specs=[hbm] * 10,
        out_specs=(free,) * 3,
        scratch_shapes=[pltpu.VMEM(a.shape, a.dtype) for a in args]
        + [
            pltpu.VMEM(film.shape, F32),
            pltpu.VMEM(film.shape, F32),
            pltpu.VMEM((HID, 2 * HID), F32),
            pltpu.VMEM((2, 2, NCLS, SPAN, SPAN), BF),
            pltpu.VMEM((2, SPAN, chunk), BF),
            pltpu.VMEM((2, SPAN, chunk), BF),
            pltpu.VMEM((2, CIN, side), BF),
            pltpu.VMEM((2, CIN, side), BF),
            pltpu.VMEM((CIN, 24, side), F32),
            pltpu.VMEM((2, PIECES * 16, side), BF),
            pltpu.VMEM((tall, WIDTH), BF),
            pltpu.VMEM((96, tall), BF),
            pltpu.VMEM((WIDTH, WIDTH), BF),
            pltpu.VMEM((WIDTH, WIDTH), BF),
            pltpu.VMEM((16, 3 * WIDTH), BF),
            pltpu.VMEM((WIDTH, 2 * WIDTH), F32),
            pltpu.VMEM((tall, side), BF),
            pltpu.VMEM((3, WIDTH, 2 * WIDTH), F32),
            pltpu.VMEM((tall, side), BF),
            pltpu.VMEM((tall, side), BF),
            pltpu.VMEM((tall, side), BF),
            pltpu.VMEM((rows, side), F32),
            pltpu.VMEM((rows, side), BF),
            pltpu.VMEM((rows, side), BF),
            pltpu.VMEM((rows, side), BF),
            pltpu.VMEM((rows, side), BF),
            pltpu.VMEM((tall, WIDTH), F32),
            pltpu.VMEM((2, WIDTH, WIDTH), F32),
            pltpu.VMEM((HID, 4 * WIDTH), F32),
            pltpu.VMEM((2, 96, side), F32),
            pltpu.VMEM((2, 24, side), F32),
            pltpu.VMEM((2, 2, side), F32),
            pltpu.VMEM((2, 2, side), F32),
            pltpu.VMEM((SPAN, SPAN), F32),
            pltpu.VMEM((HID, 2 * HID), F32),
            pltpu.VMEM((8, 8, 2 * HID), F32),
            pltpu.VMEM((8, 2 * HID), F32),
            pltpu.VMEM((8, 8, 2 * HID), F32),
            pltpu.VMEM((8, 2 * HID), F32),
            pltpu.VMEM((8, 8, 2 * HID), F32),
            pltpu.VMEM((8, 2 * HID), F32),
            pltpu.VMEM((8, 8, 2 * HID), F32),
            pltpu.SemaphoreType.DMA((10,)),
            pltpu.SemaphoreType.DMA((3,)),
            pltpu.SemaphoreType.DMA((4,)),
            pltpu.SemaphoreType.DMA((4,)),
            pltpu.SemaphoreType.DMA((2, 2)),
            pltpu.SemaphoreType.DMA((2, 2)),
            pltpu.SemaphoreType.DMA((4,)),
            pltpu.SemaphoreType.DMA((4,)),
            pltpu.SemaphoreType.REGULAR((3,)),
        ],
        compiler_params=pltpu.CompilerParams(
            collective_id=0, has_side_effects=True, vmem_limit_bytes=48 * 1024 * 1024
        ),
    )(*args)
    outs = pl.pallas_call(
        hand_out,
        out_shape=(
            slab,
            slab,
            jax.ShapeDtypeStruct(convw.shape, F32),
            jax.ShapeDtypeStruct(mixw.shape, F32),
            jax.ShapeDtypeStruct((1, HID), F32),
        ),
        in_specs=[vmem] * 3,
        out_specs=(vmem,) * 5,
        compiler_params=pltpu.CompilerParams(vmem_limit_bytes=4 * 1024 * 1024),
    )(final, grad, gsum)
    return outs[0], outs[1], outs[2], outs[3], outs[4].reshape(HID)


def solution(mesh):
    sizes = dict(mesh.shape)
    assert sizes == {"rep": DYHI * DCORE, "sp": DYLO * DZ * DX}
    return jax.shard_map(
        on_device,
        mesh=mesh,
        in_specs=(
            P("rep", "sp", None),
            P("rep", "sp", None),
            P("rep", "sp", None),
            P("rep", None, None),
            P("rep", "sp", None),
            P(),
            P(),
            P(),
            P(),
            P("rep", "sp", None),
        ),
        out_specs=(P("rep", "sp", None), P("rep", "sp", None), P(), P(), P()),
        check_vma=False,
    )
```
